256 devices in a mesh: section: 2 (over core), tile: 128 (over y, x, z).
Axes of the slice: x: 4, y: 4, z: 8, core: 2. Of those that a mesh axis runs over, the one named last changes fastest.
Arguments:
- aerial_patch_grid: bfloat16 [384, 384, 768], P('tile'), may hold values from -6 to 6
- patch_conv_weight: bfloat16 [3, 4, 4, 96], replicated, may hold values from -0.875 to 0.875
- patch_bias: float32 [96], replicated, may hold values from -3 to 3
- merging_conv_weight: bfloat16 [2, 2, 96, 192], replicated, may hold values from -0.3125 to 0.3125
- merge_bias: float32 [192], replicated, may hold values from -3 to 3
- down_weight: bfloat16 [3, 3, 192, 384], replicated, may hold values from -0.15625 to 0.15625
- down_bias: float32 [384], replicated, may hold values from -3 to 3
- norm_gain: float32 [384], replicated, may hold values from 0.1 to 1.9
- spectral_filter: bfloat16 [384, 2, 384, 384], P('tile'), may hold values from -6 to 6
Outputs:
- block_output: bfloat16 [384, 384, 384], P('section', 'tile')
The draws below stay inside these ranges and needn't reach their ends.
All inputs are finite; a program needn't handle non-finite values.
Results may differ from the reference program's by a relative error of at most 0.015.
Values may be sent and summed in bfloat16 or wider, within the bound.
A program may use at most 64 MiB of HBM per device.

```python
import math
import jax
import jax.numpy as jnp
from jax import lax

BANDS = 3
C1 = 96
C2 = 192
C = 384
FH = 384
FW = 384
IH = 6144
IW = 6144


def steps_of(stream_key, extent, split, least, high):
    loudness = 1.0
    for position, parts in split:
        steps = jax.random.uniform(jax.random.fold_in(jax.random.fold_in(stream_key, 6), position), (parts,), jnp.float32, least / len(split), high / len(split))
        loudness = loudness * jnp.repeat(jnp.exp(steps), extent[position] // parts).reshape((-1,) + (1,) * (len(extent) - 1 - position))
    return loudness


def noise(stream_key, dims, spread, reach, shards=(), kind=jnp.bfloat16):
    values = jax.random.normal(stream_key, dims, jnp.float32) * spread
    if len(shards) > 0:
        values = steps_of(stream_key, dims, shards, -0.22, 0.18) * values
    return jnp.clip(values, min=-reach, max=reach).astype(kind)


def setup_inputs(seed: int = 0) -> dict:
    arg_keys = jax.random.split(jax.random.key(seed), 10)
    aerial_patch_grid = noise(arg_keys[0], (FH, FW, 256 * BANDS), 1.0, 6.0, ((0, 128),))
    patch_conv_weight = noise(arg_keys[1], (BANDS, 4, 4, C1), (BANDS * 16) ** -0.5, 0.875)
    patch_bias = noise(arg_keys[2], (C1,), 0.5, 3.0, (), jnp.float32)
    merging_conv_weight = noise(arg_keys[3], (2, 2, C1, C2), (4 * C1) ** -0.5, 0.3125)
    merge_bias = noise(arg_keys[4], (C2,), 0.5, 3.0, (), jnp.float32)
    down_weight = noise(arg_keys[5], (3, 3, C2, C), (9 * C2) ** -0.5, 0.15625)
    down_bias = noise(arg_keys[6], (C,), 0.5, 3.0, (), jnp.float32)
    norm_gain = jnp.clip(1.0 + 0.18 * jax.random.normal(arg_keys[7], (C,), jnp.float32), 0.1, 1.9)
    spectral_filter = noise(arg_keys[8], (C, 2, FH, FW), 1.0, 6.0, ((0, 128),))
    return dict(aerial_patch_grid=aerial_patch_grid, patch_conv_weight=patch_conv_weight, patch_bias=patch_bias, merging_conv_weight=merging_conv_weight, merge_bias=merge_bias, down_weight=down_weight, down_bias=down_bias, norm_gain=norm_gain, spectral_filter=spectral_filter)


EPSILON = 1e-05

def fourier_tables(length):
    indices = jnp.arange(length, dtype=jnp.int32)
    product = indices[:, None] * indices[None, :] % length
    angles = product.astype(jnp.float32) * (2.0 * math.pi / length)
    return (jnp.cos(angles).astype(jnp.bfloat16), jnp.sin(angles).astype(jnp.bfloat16))

def stem_block(padded_image, block_index, block_rows, patch_conv_weight, patch_bias, merging_conv_weight, merge_bias, down_weight, down_bias):
    band_count = padded_image.shape[0]
    image_rows = 16 * block_rows + 16
    row_begin = (block_index * (16 * block_rows)).astype(jnp.int32)
    piece = lax.dynamic_slice_in_dim(padded_image, row_begin, image_rows, 1).astype(jnp.float32)
    image_cols = piece.shape[2]
    blocks = piece.reshape(band_count, image_rows // 4, 4, image_cols // 4, 4)
    initial_layer = jnp.einsum('brawq,baqc->rwc', blocks, patch_conv_weight.astype(jnp.float32))
    initial_layer = jax.nn.gelu(initial_layer + patch_bias, approximate=True).astype(jnp.bfloat16)
    one_rows, one_cols, one_width = initial_layer.shape
    pairs = initial_layer.astype(jnp.float32).reshape(one_rows // 2, 2, one_cols // 2, 2, one_width)
    layer_two = jnp.einsum('rawqk,aqkc->rwc', pairs, merging_conv_weight.astype(jnp.float32))
    layer_two = jax.nn.gelu(layer_two + merge_bias, approximate=True).astype(jnp.bfloat16)
    global_rows = block_index * (2 * block_rows) - 2 + jnp.arange(2 * block_rows + 2, dtype=jnp.int32)
    layer_two = jnp.where((global_rows >= 0)[:, None, None], layer_two, jnp.zeros_like(layer_two))
    padded = jnp.pad(layer_two, ((0, 0), (1, 0), (0, 0)))
    out_cols = layer_two.shape[1] // 2
    summed = jnp.zeros((down_weight.shape[3], block_rows, out_cols), jnp.float32)
    for row_tap in range(3):
        for col_tap in range(3):
            window = padded[1 + row_tap:1 + row_tap + 2 * block_rows:2, col_tap:col_tap + 2 * out_cols:2, :]
            summed = summed + jnp.einsum('rwk,kc->crw', window.astype(jnp.float32), down_weight[row_tap, col_tap].astype(jnp.float32))
    return (summed + down_bias[:, None, None]).astype(jnp.bfloat16)

def layer_norm(features, norm_gain):
    values = features.astype(jnp.float32)
    mean_value = lax.optimization_barrier(jnp.mean(values, axis=0, keepdims=True))
    centered = values - mean_value
    variance = lax.optimization_barrier(jnp.mean(centered * centered, axis=0, keepdims=True))
    return (norm_gain[:, None, None] * centered * lax.rsqrt(variance + EPSILON)).astype(jnp.bfloat16)

def filter_channel(field, kernel, forward_table, forward_h, inverse_h, inverse_table, norm_scale):
    row_spectrum = jnp.einsum('hx,xqw->hqw', field.astype(jnp.float32), forward_table.astype(jnp.float32)).astype(jnp.bfloat16)
    spectrum = jnp.einsum('puqh,hqw->puw', forward_h.astype(jnp.float32), row_spectrum.astype(jnp.float32)).astype(jnp.bfloat16)
    spec_real = spectrum[0].astype(jnp.float32)
    spec_imag = spectrum[1].astype(jnp.float32)
    filter_real = kernel[0].astype(jnp.float32)
    filter_imag = kernel[1].astype(jnp.float32)
    weighted = jnp.stack([filter_real * spec_real - filter_imag * spec_imag, filter_real * spec_imag + filter_imag * spec_real], axis=0).astype(jnp.bfloat16)
    back_rows = jnp.einsum('qhpu,puw->hqw', inverse_h.astype(jnp.float32), weighted.astype(jnp.float32)).astype(jnp.bfloat16)
    result = jnp.einsum('hqw,qwv->hv', back_rows.astype(jnp.float32), inverse_table.astype(jnp.float32))
    return (result * norm_scale).astype(jnp.bfloat16)

def reference(aerial_patch_grid, patch_conv_weight, patch_bias, merging_conv_weight, merge_bias, down_weight, down_bias, norm_gain, spectral_filter):
    block_rows = math.gcd(FH, 8)
    block_count = FH // block_rows
    image = aerial_patch_grid.reshape(FH, FW, BANDS, 16, 16)
    image = jnp.transpose(image, (2, 0, 3, 1, 4)).reshape(BANDS, IH, IW)
    padded_image = jnp.pad(image, ((0, 0), (16, 0), (0, 0)))

    def one_block(block_index):
        return stem_block(padded_image, block_index, block_rows, patch_conv_weight, patch_bias, merging_conv_weight, merge_bias, down_weight, down_bias)
    pieces = lax.map(one_block, jnp.arange(block_count, dtype=jnp.int32))
    features = jnp.transpose(pieces, (1, 0, 2, 3)).reshape(C, FH, FW)
    normed = layer_norm(features, norm_gain)
    cos_h, sin_h = fourier_tables(FH)
    cos_w, sin_w = fourier_tables(FW)
    forward_table = jnp.stack([cos_w, -sin_w], axis=1)
    forward_h = jnp.stack([jnp.stack([cos_h, sin_h], axis=1), jnp.stack([-sin_h, cos_h], axis=1)], axis=0)
    inverse_h = jnp.stack([jnp.stack([cos_h, -sin_h], axis=1), jnp.stack([sin_h, cos_h], axis=1)], axis=0)
    inverse_table = jnp.stack([cos_w, -sin_w], axis=0)
    norm_scale = 1.0 / (FH * FW)

    def one_channel(operands):
        return filter_channel(operands[0], operands[1], forward_table, forward_h, inverse_h, inverse_table, norm_scale)
    filtered = lax.map(one_channel, (normed, spectral_filter))
    return (features.astype(jnp.float32) + filtered.astype(jnp.float32)).astype(jnp.bfloat16)
```

```python
import math

import jax
import jax.numpy as jnp
from jax import lax
from jax.sharding import PartitionSpec as P

EPSILON = 1e-05


def from_behind(block, axis, distance):
    devices = range(lax.axis_size(axis))
    route = [(i - distance, i) for i in devices if i - distance in devices]
    return lax.ppermute(block, axis, route)


def fourier_tables(length):
    indices = jnp.arange(length, dtype=jnp.int32)
    product = indices[:, None] * indices[None, :] % length
    angles = product.astype(jnp.float32) * (2.0 * math.pi / length)
    return (jnp.cos(angles).astype(jnp.bfloat16), jnp.sin(angles).astype(jnp.bfloat16))


def one_hot_rows(indices, width):
    return (indices[:, None] == jnp.arange(width, dtype=jnp.int32)[None, :]).astype(jnp.bfloat16)


def spread_kernel(weight_rows, row_pick, row_cell, col_cell, width, out_cols):
    picked = jnp.dot(
        one_hot_rows(row_pick, weight_rows.shape[0]), weight_rows,
        preferred_element_type=jnp.float32,
    ).astype(jnp.bfloat16)
    col = jnp.arange(out_cols, dtype=jnp.int32)
    repeat = one_hot_rows(col % width, width).T
    full = jnp.dot(picked, repeat, preferred_element_type=jnp.float32)
    mask = row_cell[:, None] == col_cell[None, :]
    return jnp.where(mask, full, 0.0).astype(jnp.bfloat16)


def patch_kernel_matrix(patch_conv_weight):
    band_count = patch_conv_weight.shape[0]
    width = patch_conv_weight.shape[3]
    row = jnp.arange(band_count * 256, dtype=jnp.int32)
    pick = (row // 256) * 16 + ((row // 16) % 4) * 4 + row % 4
    row_cell = ((row // 64) % 4) * 4 + (row // 4) % 4
    col = jnp.arange(16 * width, dtype=jnp.int32)
    col_cell = col // width
    weight_rows = patch_conv_weight.reshape(band_count * 16, width)
    return spread_kernel(weight_rows, pick, row_cell, col_cell, width, 16 * width)


def merging_kernel_matrix(merging_conv_weight):
    in_width = merging_conv_weight.shape[2]
    out_width = merging_conv_weight.shape[3]
    row = jnp.arange(16 * in_width, dtype=jnp.int32)
    pos = row // in_width
    pick = ((pos // 4) % 2 * 2 + pos % 2) * in_width + row % in_width
    row_cell = (pos // 8) * 2 + (pos // 2) % 2
    col = jnp.arange(4 * out_width, dtype=jnp.int32)
    col_cell = col // out_width
    weight_rows = merging_conv_weight.reshape(4 * in_width, out_width)
    return spread_kernel(weight_rows, pick, row_cell, col_cell, out_width, 4 * out_width)


def down_matrices(down_weight):
    nothing = jnp.zeros_like(down_weight[0, 0])
    in_width = down_weight.shape[2]
    out_width = down_weight.shape[3]

    def arrange(entries):
        return jnp.stack(
            [jnp.stack(entries[0], axis=0), jnp.stack(entries[1], axis=0)], axis=0
        ).reshape(4 * in_width, out_width)

    own_taps = arrange(
        [[down_weight[1, 1], down_weight[1, 2]], [down_weight[2, 1], down_weight[2, 2]]]
    )
    upper_taps = arrange([[nothing, nothing], [down_weight[0, 1], down_weight[0, 2]]])
    left_taps = arrange([[nothing, down_weight[1, 0]], [nothing, down_weight[2, 0]]])
    corner_taps = arrange([[nothing, nothing], [nothing, down_weight[0, 0]]])
    return (own_taps, upper_taps, left_taps, corner_taps)


def stem_layers(aerial_patch_grid, patch_conv_weight, patch_bias, merging_conv_weight, merge_bias):
    initial_layer = jnp.einsum(
        "zji,if->zjf",
        aerial_patch_grid,
        patch_kernel_matrix(patch_conv_weight),
        preferred_element_type=jnp.float32,
    )
    initial_layer = jax.nn.gelu(initial_layer + jnp.tile(patch_bias, 16), approximate=True).astype(
        jnp.bfloat16
    )
    layer_two = jnp.einsum(
        "zji,if->zjf",
        initial_layer,
        merging_kernel_matrix(merging_conv_weight),
        preferred_element_type=jnp.float32,
    )
    return jax.nn.gelu(layer_two + jnp.tile(merge_bias, 4), approximate=True).astype(jnp.bfloat16)


def rim_above(extended):
    return from_behind(extended[-1:], "tile", 1)


def down_conv(upper_rim, extended, down_weight, down_bias):
    stacked = jnp.concatenate([upper_rim, extended], axis=0)
    own_taps, upper_taps, left_taps, corner_taps = down_matrices(down_weight)
    summed = jnp.einsum(
        "rwk,kc->crw", stacked[1:, 1:], own_taps, preferred_element_type=jnp.float32
    )
    summed = summed + jnp.einsum(
        "rwk,kc->crw", stacked[:-1, 1:], upper_taps, preferred_element_type=jnp.float32
    )
    summed = summed + jnp.einsum(
        "rwk,kc->crw", stacked[1:, :-1], left_taps, preferred_element_type=jnp.float32
    )
    summed = summed + jnp.einsum(
        "rwk,kc->crw", stacked[:-1, :-1], corner_taps, preferred_element_type=jnp.float32
    )
    return (summed + down_bias[:, None, None]).astype(jnp.bfloat16)


def layer_norm(features, norm_gain):
    values = features.astype(jnp.float32)
    mean_value = jnp.mean(values, axis=0, keepdims=True)
    centered = values - mean_value
    variance = jnp.mean(centered * centered, axis=0, keepdims=True)
    return (norm_gain[:, None, None] * centered * lax.rsqrt(variance + EPSILON)).astype(
        jnp.bfloat16
    )


def filter_columns(row_spectrum, kernel, forward_h, inverse_h):
    spectrum = jnp.einsum(
        "puqh,chqw->cpuw", forward_h, row_spectrum, preferred_element_type=jnp.float32
    ).astype(jnp.bfloat16)
    spec_real = spectrum[:, 0].astype(jnp.float32)
    spec_imag = spectrum[:, 1].astype(jnp.float32)
    filter_real = kernel[:, 0].astype(jnp.float32)
    filter_imag = kernel[:, 1].astype(jnp.float32)
    weighted = jnp.stack(
        [
            filter_real * spec_real - filter_imag * spec_imag,
            filter_real * spec_imag + filter_imag * spec_real,
        ],
        axis=1,
    ).astype(jnp.bfloat16)
    return jnp.einsum(
        "qhpu,cpuw->chqw", inverse_h, weighted, preferred_element_type=jnp.float32
    ).astype(jnp.bfloat16)


def local(
    aerial_patch_grid,
    patch_conv_weight,
    patch_bias,
    merging_conv_weight,
    merge_bias,
    down_weight,
    down_bias,
    norm_gain,
    spectral_filter,
):
    section_index = lax.axis_index("section")
    field_cols = aerial_patch_grid.shape[1]
    channels = down_weight.shape[3]
    full_rows = spectral_filter.shape[2]
    half_channels = channels // 2
    cell_half = field_cols // 2
    image_part = lax.dynamic_slice_in_dim(
        aerial_patch_grid, section_index * cell_half, cell_half, 1
    )
    layer_two = stem_layers(
        image_part, patch_conv_weight, patch_bias, merging_conv_weight, merge_bias
    )
    left_column = from_behind(layer_two[:, -1:], "section", 1)
    extended = jnp.concatenate([left_column, layer_two], axis=1)
    upper_rim = rim_above(extended)
    feature_half = down_conv(upper_rim, extended, down_weight, down_bias)
    normed_half = layer_norm(feature_half, norm_gain)
    fields = lax.all_to_all(normed_half, "tile", split_axis=0, concat_axis=1, tiled=True)
    fields = lax.all_gather(fields, "section", axis=2, tiled=True)

    cos_h, sin_h = fourier_tables(full_rows)
    if full_rows == field_cols:
        cos_w, sin_w = cos_h, sin_h
    else:
        cos_w, sin_w = fourier_tables(field_cols)
    cos_part = lax.dynamic_slice_in_dim(cos_w, section_index * cell_half, cell_half, 1)
    sin_part = lax.dynamic_slice_in_dim(sin_w, section_index * cell_half, cell_half, 1)
    forward_table = jnp.stack([cos_part, -sin_part], axis=1)
    inverse_table = jnp.stack([cos_part, -sin_part], axis=0)
    forward_h = jnp.stack(
        [jnp.stack([cos_h, sin_h], axis=1), jnp.stack([-sin_h, cos_h], axis=1)], axis=0
    )
    inverse_h = jnp.stack(
        [jnp.stack([cos_h, -sin_h], axis=1), jnp.stack([sin_h, cos_h], axis=1)], axis=0
    )
    norm_scale = 1.0 / (full_rows * field_cols)
    kernel_part = lax.dynamic_slice_in_dim(
        spectral_filter, section_index * cell_half, cell_half, 3
    )
    frequency_rows = jnp.einsum(
        "chx,xqw->chqw", fields, forward_table, preferred_element_type=jnp.float32
    ).astype(jnp.bfloat16)
    back_rows = filter_columns(frequency_rows, kernel_part, forward_h, inverse_h)
    back_rows = lax.all_gather(back_rows, "section", axis=3, tiled=True)
    result = jnp.einsum(
        "chqw,qwv->chv", back_rows, inverse_table, preferred_element_type=jnp.float32
    )
    filtered_fields = (result * norm_scale).astype(jnp.bfloat16)
    rows_back = lax.all_to_all(filtered_fields, "tile", split_axis=1, concat_axis=0, tiled=True)
    summed = (feature_half.astype(jnp.float32) + rows_back.astype(jnp.float32)).astype(
        jnp.bfloat16
    )
    kept = lax.dynamic_slice_in_dim(summed, section_index * half_channels, half_channels, 0)
    sent = lax.dynamic_slice_in_dim(
        summed, (1 - section_index) * half_channels, half_channels, 0
    )
    received = lax.ppermute(sent, "section", [(0, 1), (1, 0)])
    return jnp.where(
        section_index == 0,
        jnp.concatenate([kept, received], axis=2),
        jnp.concatenate([received, kept], axis=2),
    )


def solution(mesh):
    return jax.shard_map(
        local,
        mesh=mesh,
        in_specs=(
            P("tile", None, None),
            P(),
            P(),
            P(),
            P(),
            P(),
            P(),
            P(),
            P("tile", None, None, None),
        ),
        out_specs=P("section", "tile", None),
        check_vma=False,
    )
```

```python
import math

import jax
import jax.numpy as jnp
from jax import lax
from jax.experimental import pallas as pl
from jax.experimental.pallas import tpu as pltpu
from jax.sharding import PartitionSpec as P

EPSILON = 1e-05
MESH_ID = pl.DeviceIdType.MESH


def exchange_kernel(x_ref, o_ref, send_sem, recv_sem, own_sem):
    count = x_ref.shape[0]
    me = lax.axis_index("tile")
    section = lax.axis_index("section")
    barrier = pltpu.get_barrier_semaphore()

    def greet(step, carry):
        peer = lax.rem(me + step, count)
        pl.semaphore_signal(barrier, 1, device_id=(section, peer), device_id_type=MESH_ID)
        return carry

    lax.fori_loop(1, count, greet, 0)
    pl.semaphore_wait(barrier, count - 1)
    own = pltpu.make_async_copy(x_ref.at[pl.ds(me, 1)], o_ref.at[pl.ds(me, 1)], own_sem)
    own.start()

    def send(step, carry):
        peer = lax.rem(me + step, count)
        pltpu.make_async_remote_copy(
            src_ref=x_ref.at[pl.ds(peer, 1)],
            dst_ref=o_ref.at[pl.ds(me, 1)],
            send_sem=send_sem,
            recv_sem=recv_sem,
            device_id=(section, peer),
            device_id_type=MESH_ID,
        ).start()
        return carry

    lax.fori_loop(1, count, send, 0)
    every = pltpu.make_async_remote_copy(
        src_ref=x_ref.at[pl.ds(0, count - 1)],
        dst_ref=o_ref.at[pl.ds(0, count - 1)],
        send_sem=send_sem,
        recv_sem=recv_sem,
        device_id=(section, lax.rem(me + 1, count)),
        device_id_type=MESH_ID,
    )
    every.wait_send()
    every.wait_recv()
    own.wait()


def exchange(chunks, collective_id):
    return pl.pallas_call(
        exchange_kernel,
        out_shape=jax.ShapeDtypeStruct(chunks.shape, chunks.dtype),
        in_specs=[pl.BlockSpec(memory_space=pl.ANY)],
        out_specs=pl.BlockSpec(memory_space=pl.ANY),
        scratch_shapes=[pltpu.SemaphoreType.DMA(())] * 3,
        compiler_params=pltpu.CompilerParams(collective_id=collective_id, has_side_effects=True),
    )(chunks)


def exchange_chunks(chunks, collective_id):
    count, length = chunks.shape
    padded = -(-length // 2048) * 2048
    slabs = jnp.pad(chunks, ((0, 0), (0, padded - length))).reshape(count, padded // 128, 128)
    return exchange(slabs, collective_id).reshape(count, padded)[:, :length]


def from_behind(block, axis, distance):
    devices = range(lax.axis_size(axis))
    route = [(i - distance, i) for i in devices if i - distance in devices]
    return lax.ppermute(block, axis, route)


def fourier_tables(length):
    indices = jnp.arange(length, dtype=jnp.int32)
    product = indices[:, None] * indices[None, :] % length
    angles = product.astype(jnp.float32) * (2.0 * math.pi / length)
    return (jnp.cos(angles).astype(jnp.bfloat16), jnp.sin(angles).astype(jnp.bfloat16))


def one_hot_rows(indices, width):
    return (indices[:, None] == jnp.arange(width, dtype=jnp.int32)[None, :]).astype(jnp.bfloat16)


def spread_kernel(weight_rows, row_pick, row_cell, col_cell, width, out_cols):
    picked = jnp.dot(
        one_hot_rows(row_pick, weight_rows.shape[0]), weight_rows,
        preferred_element_type=jnp.float32,
    ).astype(jnp.bfloat16)
    col = jnp.arange(out_cols, dtype=jnp.int32)
    repeat = one_hot_rows(col % width, width).T
    full = jnp.dot(picked, repeat, preferred_element_type=jnp.float32)
    mask = row_cell[:, None] == col_cell[None, :]
    return jnp.where(mask, full, 0.0).astype(jnp.bfloat16)


def patch_kernel_matrix(patch_conv_weight):
    band_count = patch_conv_weight.shape[0]
    width = patch_conv_weight.shape[3]
    row = jnp.arange(band_count * 256, dtype=jnp.int32)
    pick = (row // 256) * 16 + ((row // 16) % 4) * 4 + row % 4
    row_cell = ((row // 64) % 4) * 4 + (row // 4) % 4
    col = jnp.arange(16 * width, dtype=jnp.int32)
    col_cell = col // width
    weight_rows = patch_conv_weight.reshape(band_count * 16, width)
    return spread_kernel(weight_rows, pick, row_cell, col_cell, width, 16 * width)


def merging_kernel_matrix(merging_conv_weight):
    in_width = merging_conv_weight.shape[2]
    out_width = merging_conv_weight.shape[3]
    row = jnp.arange(16 * in_width, dtype=jnp.int32)
    pos = row // in_width
    pick = ((pos // 4) % 2 * 2 + pos % 2) * in_width + row % in_width
    row_cell = (pos // 8) * 2 + (pos // 2) % 2
    col = jnp.arange(4 * out_width, dtype=jnp.int32)
    col_cell = col // out_width
    weight_rows = merging_conv_weight.reshape(4 * in_width, out_width)
    return spread_kernel(weight_rows, pick, row_cell, col_cell, out_width, 4 * out_width)


def down_matrices(down_weight):
    nothing = jnp.zeros_like(down_weight[0, 0])
    in_width = down_weight.shape[2]
    out_width = down_weight.shape[3]

    def arrange(entries):
        return jnp.stack(
            [jnp.stack(entries[0], axis=0), jnp.stack(entries[1], axis=0)], axis=0
        ).reshape(4 * in_width, out_width)

    own_taps = arrange(
        [[down_weight[1, 1], down_weight[1, 2]], [down_weight[2, 1], down_weight[2, 2]]]
    )
    upper_taps = arrange([[nothing, nothing], [down_weight[0, 1], down_weight[0, 2]]])
    left_taps = arrange([[nothing, down_weight[1, 0]], [nothing, down_weight[2, 0]]])
    corner_taps = arrange([[nothing, nothing], [nothing, down_weight[0, 0]]])
    return (own_taps, upper_taps, left_taps, corner_taps)


def stem_layers(aerial_patch_grid, patch_conv_weight, patch_bias, merging_conv_weight, merge_bias):
    initial_layer = jnp.einsum(
        "zji,if->zjf",
        aerial_patch_grid,
        patch_kernel_matrix(patch_conv_weight),
        preferred_element_type=jnp.float32,
    )
    initial_layer = jax.nn.gelu(initial_layer + jnp.tile(patch_bias, 16), approximate=True).astype(
        jnp.bfloat16
    )
    layer_two = jnp.einsum(
        "zji,if->zjf",
        initial_layer,
        merging_kernel_matrix(merging_conv_weight),
        preferred_element_type=jnp.float32,
    )
    return jax.nn.gelu(layer_two + jnp.tile(merge_bias, 4), approximate=True).astype(jnp.bfloat16)


def rim_above(extended):
    return from_behind(extended[-1:], "tile", 1)


def down_conv(upper_rim, extended, down_weight, down_bias):
    stacked = jnp.concatenate([upper_rim, extended], axis=0)
    own_taps, upper_taps, left_taps, corner_taps = down_matrices(down_weight)
    summed = jnp.einsum(
        "rwk,kc->crw", stacked[1:, 1:], own_taps, preferred_element_type=jnp.float32
    )
    summed = summed + jnp.einsum(
        "rwk,kc->crw", stacked[:-1, 1:], upper_taps, preferred_element_type=jnp.float32
    )
    summed = summed + jnp.einsum(
        "rwk,kc->crw", stacked[1:, :-1], left_taps, preferred_element_type=jnp.float32
    )
    summed = summed + jnp.einsum(
        "rwk,kc->crw", stacked[:-1, :-1], corner_taps, preferred_element_type=jnp.float32
    )
    return (summed + down_bias[:, None, None]).astype(jnp.bfloat16)


def layer_norm(features, norm_gain):
    values = features.astype(jnp.float32)
    mean_value = jnp.mean(values, axis=0, keepdims=True)
    centered = values - mean_value
    variance = jnp.mean(centered * centered, axis=0, keepdims=True)
    return (norm_gain[:, None, None] * centered * lax.rsqrt(variance + EPSILON)).astype(
        jnp.bfloat16
    )


def filter_columns(row_spectrum, kernel, forward_h, inverse_h):
    spectrum = jnp.einsum(
        "puqh,chqw->cpuw", forward_h, row_spectrum, preferred_element_type=jnp.float32
    ).astype(jnp.bfloat16)
    spec_real = spectrum[:, 0].astype(jnp.float32)
    spec_imag = spectrum[:, 1].astype(jnp.float32)
    filter_real = kernel[:, 0].astype(jnp.float32)
    filter_imag = kernel[:, 1].astype(jnp.float32)
    weighted = jnp.stack(
        [
            filter_real * spec_real - filter_imag * spec_imag,
            filter_real * spec_imag + filter_imag * spec_real,
        ],
        axis=1,
    ).astype(jnp.bfloat16)
    return jnp.einsum(
        "qhpu,cpuw->chqw", inverse_h, weighted, preferred_element_type=jnp.float32
    ).astype(jnp.bfloat16)


def local(
    aerial_patch_grid,
    patch_conv_weight,
    patch_bias,
    merging_conv_weight,
    merge_bias,
    down_weight,
    down_bias,
    norm_gain,
    spectral_filter,
):
    section_index = lax.axis_index("section")
    field_cols = aerial_patch_grid.shape[1]
    channels = down_weight.shape[3]
    full_rows = spectral_filter.shape[2]
    half_channels = channels // 2
    cell_half = field_cols // 2
    image_part = lax.dynamic_slice_in_dim(
        aerial_patch_grid, section_index * cell_half, cell_half, 1
    )
    layer_two = stem_layers(
        image_part, patch_conv_weight, patch_bias, merging_conv_weight, merge_bias
    )
    left_column = from_behind(layer_two[:, -1:], "section", 1)
    extended = jnp.concatenate([left_column, layer_two], axis=1)
    upper_rim = rim_above(extended)
    feature_half = down_conv(upper_rim, extended, down_weight, down_bias)
    normed_half = layer_norm(feature_half, norm_gain)
    tiles = lax.axis_size("tile")
    group_width, tile_rows = channels // tiles, normed_half.shape[1]
    arrived = exchange_chunks(normed_half.reshape(tiles, -1), 0)
    fields = (
        arrived.reshape(tiles, group_width, tile_rows, cell_half)
        .transpose(1, 0, 2, 3)
        .reshape(group_width, tiles * tile_rows, cell_half)
    )
    fields = lax.all_gather(fields, "section", axis=2, tiled=True)

    cos_h, sin_h = fourier_tables(full_rows)
    if full_rows == field_cols:
        cos_w, sin_w = cos_h, sin_h
    else:
        cos_w, sin_w = fourier_tables(field_cols)
    cos_part = lax.dynamic_slice_in_dim(cos_w, section_index * cell_half, cell_half, 1)
    sin_part = lax.dynamic_slice_in_dim(sin_w, section_index * cell_half, cell_half, 1)
    forward_table = jnp.stack([cos_part, -sin_part], axis=1)
    inverse_table = jnp.stack([cos_part, -sin_part], axis=0)
    forward_h = jnp.stack(
        [jnp.stack([cos_h, sin_h], axis=1), jnp.stack([-sin_h, cos_h], axis=1)], axis=0
    )
    inverse_h = jnp.stack(
        [jnp.stack([cos_h, -sin_h], axis=1), jnp.stack([sin_h, cos_h], axis=1)], axis=0
    )
    norm_scale = 1.0 / (full_rows * field_cols)
    kernel_part = lax.dynamic_slice_in_dim(
        spectral_filter, section_index * cell_half, cell_half, 3
    )
    frequency_rows = jnp.einsum(
        "chx,xqw->chqw", fields, forward_table, preferred_element_type=jnp.float32
    ).astype(jnp.bfloat16)
    back_rows = filter_columns(frequency_rows, kernel_part, forward_h, inverse_h)
    back_rows = lax.all_gather(back_rows, "section", axis=3, tiled=True)
    result = jnp.einsum(
        "chqw,qwv->chv", back_rows, inverse_table, preferred_element_type=jnp.float32
    )
    filtered_fields = (result * norm_scale).astype(jnp.bfloat16)
    outgoing = (
        filtered_fields.reshape(group_width, tiles, tile_rows, cell_half)
        .transpose(1, 0, 2, 3)
        .reshape(tiles, -1)
    )
    rows_back = exchange_chunks(outgoing, 1).reshape(channels, tile_rows, cell_half)
    summed = (feature_half.astype(jnp.float32) + rows_back.astype(jnp.float32)).astype(
        jnp.bfloat16
    )
    kept = lax.dynamic_slice_in_dim(summed, section_index * half_channels, half_channels, 0)
    sent = lax.dynamic_slice_in_dim(
        summed, (1 - section_index) * half_channels, half_channels, 0
    )
    received = lax.ppermute(sent, "section", [(0, 1), (1, 0)])
    return jnp.where(
        section_index == 0,
        jnp.concatenate([kept, received], axis=2),
        jnp.concatenate([received, kept], axis=2),
    )


def solution(mesh):
    return jax.shard_map(
        local,
        mesh=mesh,
        in_specs=(
            P("tile", None, None),
            P(),
            P(),
            P(),
            P(),
            P(),
            P(),
            P(),
            P("tile", None, None, None),
        ),
        out_specs=P("section", "tile", None),
        check_vma=False,
    )
```

```python
import math

import jax
import jax.numpy as jnp
from jax import lax
from jax.experimental import pallas as pl
from jax.experimental.pallas import tpu as pltpu
from jax.sharding import PartitionSpec as P

EPSILON = 1e-05
MESH_ID = pl.DeviceIdType.MESH


def exchange_kernel(x_ref, o_ref, send_sem, recv_sem, own_sem):
    count = x_ref.shape[0]
    me = lax.axis_index("tile")
    section = lax.axis_index("section")
    barrier = pltpu.get_barrier_semaphore()

    def greet(step, carry):
        peer = lax.rem(me + step, count)
        pl.semaphore_signal(barrier, 1, device_id=(section, peer), device_id_type=MESH_ID)
        return carry

    lax.fori_loop(1, count, greet, 0)
    pl.semaphore_wait(barrier, count - 1)
    own = pltpu.make_async_copy(x_ref.at[pl.ds(me, 1)], o_ref.at[pl.ds(me, 1)], own_sem)
    own.start()

    def send(step, carry):
        peer = lax.rem(me + step, count)
        pltpu.make_async_remote_copy(
            src_ref=x_ref.at[pl.ds(peer, 1)],
            dst_ref=o_ref.at[pl.ds(me, 1)],
            send_sem=send_sem,
            recv_sem=recv_sem,
            device_id=(section, peer),
            device_id_type=MESH_ID,
        ).start()
        return carry

    lax.fori_loop(1, count, send, 0)
    every = pltpu.make_async_remote_copy(
        src_ref=x_ref.at[pl.ds(0, count - 1)],
        dst_ref=o_ref.at[pl.ds(0, count - 1)],
        send_sem=send_sem,
        recv_sem=recv_sem,
        device_id=(section, lax.rem(me + 1, count)),
        device_id_type=MESH_ID,
    )
    every.wait_send()
    every.wait_recv()
    own.wait()


def exchange(chunks, collective_id):
    return pl.pallas_call(
        exchange_kernel,
        out_shape=jax.ShapeDtypeStruct(chunks.shape, chunks.dtype),
        in_specs=[pl.BlockSpec(memory_space=pl.ANY)],
        out_specs=pl.BlockSpec(memory_space=pl.ANY),
        scratch_shapes=[pltpu.SemaphoreType.DMA(())] * 3,
        compiler_params=pltpu.CompilerParams(collective_id=collective_id, has_side_effects=True),
    )(chunks)


def exchange_chunks(chunks, collective_id):
    count, length = chunks.shape
    padded = -(-length // 2048) * 2048
    slabs = jnp.pad(chunks, ((0, 0), (0, padded - length))).reshape(count, padded // 128, 128)
    return exchange(slabs, collective_id).reshape(count, padded)[:, :length]


def from_behind(block, axis, distance):
    devices = range(lax.axis_size(axis))
    route = [(i - distance, i) for i in devices if i - distance in devices]
    return lax.ppermute(block, axis, route)


def fourier_tables(length):
    indices = jnp.arange(length, dtype=jnp.int32)
    product = indices[:, None] * indices[None, :] % length
    angles = product.astype(jnp.float32) * (2.0 * math.pi / length)
    return (jnp.cos(angles).astype(jnp.bfloat16), jnp.sin(angles).astype(jnp.bfloat16))


def one_hot_rows(indices, width):
    return (indices[:, None] == jnp.arange(width, dtype=jnp.int32)[None, :]).astype(jnp.bfloat16)


def spread_kernel(weight_rows, row_pick, row_cell, col_cell, width, out_cols):
    picked = jnp.dot(
        one_hot_rows(row_pick, weight_rows.shape[0]), weight_rows,
        preferred_element_type=jnp.float32,
    ).astype(jnp.bfloat16)
    col = jnp.arange(out_cols, dtype=jnp.int32)
    repeat = one_hot_rows(col % width, width).T
    full = jnp.dot(picked, repeat, preferred_element_type=jnp.float32)
    mask = row_cell[:, None] == col_cell[None, :]
    return jnp.where(mask, full, 0.0).astype(jnp.bfloat16)


def patch_kernel_matrix(patch_conv_weight):
    band_count = patch_conv_weight.shape[0]
    width = patch_conv_weight.shape[3]
    row = jnp.arange(band_count * 256, dtype=jnp.int32)
    pick = (row // 256) * 16 + ((row // 16) % 4) * 4 + row % 4
    row_cell = ((row // 64) % 4) * 4 + (row // 4) % 4
    col = jnp.arange(16 * width, dtype=jnp.int32)
    col_cell = col // width
    weight_rows = patch_conv_weight.reshape(band_count * 16, width)
    return spread_kernel(weight_rows, pick, row_cell, col_cell, width, 16 * width)


def merging_kernel_matrix(merging_conv_weight):
    in_width = merging_conv_weight.shape[2]
    out_width = merging_conv_weight.shape[3]
    row = jnp.arange(16 * in_width, dtype=jnp.int32)
    pos = row // in_width
    pick = ((pos // 4) % 2 * 2 + pos % 2) * in_width + row % in_width
    row_cell = (pos // 8) * 2 + (pos // 2) % 2
    col = jnp.arange(4 * out_width, dtype=jnp.int32)
    col_cell = col // out_width
    weight_rows = merging_conv_weight.reshape(4 * in_width, out_width)
    return spread_kernel(weight_rows, pick, row_cell, col_cell, out_width, 4 * out_width)


def down_matrices(down_weight):
    nothing = jnp.zeros_like(down_weight[0, 0])
    in_width = down_weight.shape[2]
    out_width = down_weight.shape[3]

    def arrange(entries):
        return jnp.stack(
            [jnp.stack(entries[0], axis=0), jnp.stack(entries[1], axis=0)], axis=0
        ).reshape(4 * in_width, out_width)

    own_taps = arrange(
        [[down_weight[1, 1], down_weight[1, 2]], [down_weight[2, 1], down_weight[2, 2]]]
    )
    upper_taps = arrange([[nothing, nothing], [down_weight[0, 1], down_weight[0, 2]]])
    left_taps = arrange([[nothing, down_weight[1, 0]], [nothing, down_weight[2, 0]]])
    corner_taps = arrange([[nothing, nothing], [nothing, down_weight[0, 0]]])
    return (own_taps, upper_taps, left_taps, corner_taps)


def stem_layers(aerial_patch_grid, patch_conv_weight, patch_bias, merging_conv_weight, merge_bias):
    initial_layer = jnp.einsum(
        "zji,if->zjf",
        aerial_patch_grid,
        patch_kernel_matrix(patch_conv_weight),
        preferred_element_type=jnp.float32,
    )
    initial_layer = jax.nn.gelu(initial_layer + jnp.tile(patch_bias, 16), approximate=True).astype(
        jnp.bfloat16
    )
    layer_two = jnp.einsum(
        "zji,if->zjf",
        initial_layer,
        merging_kernel_matrix(merging_conv_weight),
        preferred_element_type=jnp.float32,
    )
    return jax.nn.gelu(layer_two + jnp.tile(merge_bias, 4), approximate=True).astype(jnp.bfloat16)


def rim_above(extended):
    return from_behind(extended[-1:], "tile", 1)


def down_conv(upper_rim, extended, down_weight, down_bias):
    stacked = jnp.concatenate([upper_rim, extended], axis=0)
    own_taps, upper_taps, left_taps, corner_taps = down_matrices(down_weight)
    summed = jnp.einsum(
        "rwk,kc->crw", stacked[1:, 1:], own_taps, preferred_element_type=jnp.float32
    )
    summed = summed + jnp.einsum(
        "rwk,kc->crw", stacked[:-1, 1:], upper_taps, preferred_element_type=jnp.float32
    )
    summed = summed + jnp.einsum(
        "rwk,kc->crw", stacked[1:, :-1], left_taps, preferred_element_type=jnp.float32
    )
    summed = summed + jnp.einsum(
        "rwk,kc->crw", stacked[:-1, :-1], corner_taps, preferred_element_type=jnp.float32
    )
    return (summed + down_bias[:, None, None]).astype(jnp.bfloat16)


def layer_norm(features, norm_gain):
    values = features.astype(jnp.float32)
    mean_value = jnp.mean(values, axis=0, keepdims=True)
    centered = values - mean_value
    variance = jnp.mean(centered * centered, axis=0, keepdims=True)
    return (norm_gain[:, None, None] * centered * lax.rsqrt(variance + EPSILON)).astype(
        jnp.bfloat16
    )


def filter_columns(row_spectrum, kernel, forward_h, inverse_h):
    spectrum = jnp.einsum(
        "puqh,chqw->cpuw", forward_h, row_spectrum, preferred_element_type=jnp.float32
    ).astype(jnp.bfloat16)
    spec_real = spectrum[:, 0].astype(jnp.float32)
    spec_imag = spectrum[:, 1].astype(jnp.float32)
    filter_real = kernel[:, 0].astype(jnp.float32)
    filter_imag = kernel[:, 1].astype(jnp.float32)
    weighted = jnp.stack(
        [
            filter_real * spec_real - filter_imag * spec_imag,
            filter_real * spec_imag + filter_imag * spec_real,
        ],
        axis=1,
    ).astype(jnp.bfloat16)
    return jnp.einsum(
        "qhpu,cpuw->chqw", inverse_h, weighted, preferred_element_type=jnp.float32
    ).astype(jnp.bfloat16)


def local(
    aerial_patch_grid,
    patch_conv_weight,
    patch_bias,
    merging_conv_weight,
    merge_bias,
    down_weight,
    down_bias,
    norm_gain,
    spectral_filter,
):
    section_index = lax.axis_index("section")
    field_cols = aerial_patch_grid.shape[1]
    channels = down_weight.shape[3]
    full_rows = spectral_filter.shape[2]
    half_channels = channels // 2
    cell_half = field_cols // 2
    image_part = lax.dynamic_slice_in_dim(
        aerial_patch_grid, section_index * cell_half, cell_half, 1
    )
    layer_two = stem_layers(
        image_part, patch_conv_weight, patch_bias, merging_conv_weight, merge_bias
    )
    left_column = from_behind(layer_two[:, -1:], "section", 1)
    extended = jnp.concatenate([left_column, layer_two], axis=1)
    upper_rim = rim_above(extended)
    feature_half = down_conv(upper_rim, extended, down_weight, down_bias)
    normed_half = layer_norm(feature_half, norm_gain)
    tiles = lax.axis_size("tile")
    group_width, tile_rows = channels // tiles, normed_half.shape[1]
    arrived = exchange_chunks(normed_half.reshape(tiles, -1), 0)
    fields = (
        arrived.reshape(tiles, group_width, tile_rows, cell_half)
        .transpose(1, 0, 2, 3)
        .reshape(group_width, tiles * tile_rows, cell_half)
    )
    swap = [(0, 1), (1, 0)]
    other_fields = lax.ppermute(fields, "section", swap)

    cos_h, sin_h = fourier_tables(full_rows)
    if full_rows == field_cols:
        cos_w, sin_w = cos_h, sin_h
    else:
        cos_w, sin_w = fourier_tables(field_cols)
    cos_part = lax.dynamic_slice_in_dim(cos_w, section_index * cell_half, cell_half, 1)
    sin_part = lax.dynamic_slice_in_dim(sin_w, section_index * cell_half, cell_half, 1)
    forward_table = jnp.stack([cos_part, -sin_part], axis=1)
    inverse_table = jnp.stack([cos_part, -sin_part], axis=0)
    forward_h = jnp.stack(
        [jnp.stack([cos_h, sin_h], axis=1), jnp.stack([-sin_h, cos_h], axis=1)], axis=0
    )
    inverse_h = jnp.stack(
        [jnp.stack([cos_h, -sin_h], axis=1), jnp.stack([sin_h, cos_h], axis=1)], axis=0
    )
    norm_scale = 1.0 / (full_rows * field_cols)
    kernel_part = lax.dynamic_slice_in_dim(
        spectral_filter, section_index * cell_half, cell_half, 3
    )
    own_start = section_index * cell_half
    other_start = (1 - section_index) * cell_half
    frequency_rows = jnp.einsum(
        "chx,xqw->chqw",
        fields,
        lax.dynamic_slice_in_dim(forward_table, own_start, cell_half, 0),
        preferred_element_type=jnp.float32,
    ) + jnp.einsum(
        "chx,xqw->chqw",
        other_fields,
        lax.dynamic_slice_in_dim(forward_table, other_start, cell_half, 0),
        preferred_element_type=jnp.float32,
    )
    back_rows = filter_columns(
        frequency_rows.astype(jnp.bfloat16), kernel_part, forward_h, inverse_h
    )
    other_rows = lax.ppermute(back_rows, "section", swap)
    result = jnp.einsum(
        "chqw,qwv->chv",
        back_rows,
        lax.dynamic_slice_in_dim(inverse_table, own_start, cell_half, 1),
        preferred_element_type=jnp.float32,
    ) + jnp.einsum(
        "chqw,qwv->chv",
        other_rows,
        lax.dynamic_slice_in_dim(inverse_table, other_start, cell_half, 1),
        preferred_element_type=jnp.float32,
    )
    filtered_fields = (result * norm_scale).astype(jnp.bfloat16)
    outgoing = (
        filtered_fields.reshape(group_width, tiles, tile_rows, cell_half)
        .transpose(1, 0, 2, 3)
        .reshape(tiles, -1)
    )
    rows_back = exchange_chunks(outgoing, 1).reshape(channels, tile_rows, cell_half)
    summed = (feature_half.astype(jnp.float32) + rows_back.astype(jnp.float32)).astype(
        jnp.bfloat16
    )
    kept = lax.dynamic_slice_in_dim(summed, section_index * half_channels, half_channels, 0)
    sent = lax.dynamic_slice_in_dim(
        summed, (1 - section_index) * half_channels, half_channels, 0
    )
    received = lax.ppermute(sent, "section", swap)
    return jnp.where(
        section_index == 0,
        jnp.concatenate([kept, received], axis=2),
        jnp.concatenate([received, kept], axis=2),
    )


def solution(mesh):
    return jax.shard_map(
        local,
        mesh=mesh,
        in_specs=(
            P("tile", None, None),
            P(),
            P(),
            P(),
            P(),
            P(),
            P(),
            P(),
            P("tile", None, None, None),
        ),
        out_specs=P("section", "tile", None),
        check_vma=False,
    )
```

```python
import math

import jax
import jax.numpy as jnp
from jax import lax
from jax.experimental import pallas as pl
from jax.experimental.pallas import tpu as pltpu
from jax.sharding import PartitionSpec as P

EPSILON = 1e-05
MESH_ID = pl.DeviceIdType.MESH


def exchange_kernel(x_ref, o_ref, send_sem, recv_sem, own_sem):
    count = x_ref.shape[0]
    me = lax.axis_index("tile")
    section = lax.axis_index("section")
    barrier = pltpu.get_barrier_semaphore()

    def greet(step, carry):
        peer = lax.rem(me + step, count)
        pl.semaphore_signal(barrier, 1, device_id=(section, peer), device_id_type=MESH_ID)
        return carry

    lax.fori_loop(1, count, greet, 0)
    pl.semaphore_wait(barrier, count - 1)
    own = pltpu.make_async_copy(x_ref.at[pl.ds(me, 1)], o_ref.at[pl.ds(me, 1)], own_sem)
    own.start()

    def send(step, carry):
        peer = lax.rem(me + step, count)
        pltpu.make_async_remote_copy(
            src_ref=x_ref.at[pl.ds(peer, 1)],
            dst_ref=o_ref.at[pl.ds(me, 1)],
            send_sem=send_sem,
            recv_sem=recv_sem,
            device_id=(section, peer),
            device_id_type=MESH_ID,
        ).start()
        return carry

    lax.fori_loop(1, count, send, 0)
    every = pltpu.make_async_remote_copy(
        src_ref=x_ref.at[pl.ds(0, count - 1)],
        dst_ref=o_ref.at[pl.ds(0, count - 1)],
        send_sem=send_sem,
        recv_sem=recv_sem,
        device_id=(section, lax.rem(me + 1, count)),
        device_id_type=MESH_ID,
    )
    every.wait_send()
    every.wait_recv()
    own.wait()


def exchange(chunks, collective_id):
    return pl.pallas_call(
        exchange_kernel,
        out_shape=jax.ShapeDtypeStruct(chunks.shape, chunks.dtype),
        in_specs=[pl.BlockSpec(memory_space=pl.ANY)],
        out_specs=pl.BlockSpec(memory_space=pl.ANY),
        scratch_shapes=[pltpu.SemaphoreType.DMA(())] * 3,
        compiler_params=pltpu.CompilerParams(collective_id=collective_id, has_side_effects=True),
    )(chunks)


def exchange_chunks(chunks, collective_id):
    count, length = chunks.shape
    padded = -(-length // 2048) * 2048
    slabs = jnp.pad(chunks, ((0, 0), (0, padded - length))).reshape(count, padded // 128, 128)
    return exchange(slabs, collective_id).reshape(count, padded)[:, :length]


def from_behind(block, axis, distance):
    devices = range(lax.axis_size(axis))
    route = [(i - distance, i) for i in devices if i - distance in devices]
    return lax.ppermute(block, axis, route)


def fourier_tables(length):
    indices = jnp.arange(length, dtype=jnp.int32)
    product = indices[:, None] * indices[None, :] % length
    angles = product.astype(jnp.float32) * (2.0 * math.pi / length)
    return lax.optimization_barrier(
        (jnp.cos(angles).astype(jnp.bfloat16), jnp.sin(angles).astype(jnp.bfloat16))
    )


def one_hot_rows(indices, width):
    return (indices[:, None] == jnp.arange(width, dtype=jnp.int32)[None, :]).astype(jnp.bfloat16)


def spread_kernel(weight_rows, row_pick, row_cell, col_cell, width, out_cols):
    picked = jnp.dot(
        one_hot_rows(row_pick, weight_rows.shape[0]), weight_rows,
        preferred_element_type=jnp.float32,
    ).astype(jnp.bfloat16)
    col = jnp.arange(out_cols, dtype=jnp.int32)
    repeat = one_hot_rows(col % width, width).T
    full = jnp.dot(picked, repeat, preferred_element_type=jnp.float32)
    mask = row_cell[:, None] == col_cell[None, :]
    return jnp.where(mask, full, 0.0).astype(jnp.bfloat16)


def patch_kernel_matrix(patch_conv_weight):
    band_count = patch_conv_weight.shape[0]
    width = patch_conv_weight.shape[3]
    row = jnp.arange(band_count * 256, dtype=jnp.int32)
    pick = (row // 256) * 16 + ((row // 16) % 4) * 4 + row % 4
    row_cell = ((row // 64) % 4) * 4 + (row // 4) % 4
    col = jnp.arange(16 * width, dtype=jnp.int32)
    col_cell = col // width
    weight_rows = patch_conv_weight.reshape(band_count * 16, width)
    return spread_kernel(weight_rows, pick, row_cell, col_cell, width, 16 * width)


def merging_kernel_matrix(merging_conv_weight):
    in_width = merging_conv_weight.shape[2]
    out_width = merging_conv_weight.shape[3]
    row = jnp.arange(16 * in_width, dtype=jnp.int32)
    pos = row // in_width
    pick = ((pos // 4) % 2 * 2 + pos % 2) * in_width + row % in_width
    row_cell = (pos // 8) * 2 + (pos // 2) % 2
    col = jnp.arange(4 * out_width, dtype=jnp.int32)
    col_cell = col // out_width
    weight_rows = merging_conv_weight.reshape(4 * in_width, out_width)
    return spread_kernel(weight_rows, pick, row_cell, col_cell, out_width, 4 * out_width)


def down_matrices(down_weight):
    in_width = down_weight.shape[2]
    out_width = down_weight.shape[3]
    padded = jnp.pad(down_weight, ((1, 0), (1, 0), (0, 0), (0, 0)))

    def taps(first, second):
        return padded[first : first + 2, second : second + 2].reshape(4 * in_width, out_width)

    return (taps(2, 2), taps(0, 2), taps(2, 0), taps(0, 0))


def stem_layers(aerial_patch_grid, patch_conv_weight, patch_bias, merging_conv_weight, merge_bias):
    initial_layer = jnp.einsum(
        "zji,if->zjf",
        aerial_patch_grid,
        patch_kernel_matrix(patch_conv_weight),
        preferred_element_type=jnp.float32,
    )
    initial_layer = jax.nn.gelu(initial_layer + jnp.tile(patch_bias, 16), approximate=True).astype(
        jnp.bfloat16
    )
    layer_two = jnp.einsum(
        "zji,if->zjf",
        initial_layer,
        merging_kernel_matrix(merging_conv_weight),
        preferred_element_type=jnp.float32,
    )
    return jax.nn.gelu(layer_two + jnp.tile(merge_bias, 4), approximate=True).astype(jnp.bfloat16)


def rim_above(extended):
    return from_behind(extended[-1:], "tile", 1)


def down_conv(upper_rim, extended, down_weight, down_bias):
    stacked = jnp.concatenate([upper_rim, extended], axis=0)
    own_taps, upper_taps, left_taps, corner_taps = down_matrices(down_weight)
    summed = jnp.einsum(
        "rwk,kc->crw", stacked[1:, 1:], own_taps, preferred_element_type=jnp.float32
    )
    summed = summed + jnp.einsum(
        "rwk,kc->crw", stacked[:-1, 1:], upper_taps, preferred_element_type=jnp.float32
    )
    summed = summed + jnp.einsum(
        "rwk,kc->crw", stacked[1:, :-1], left_taps, preferred_element_type=jnp.float32
    )
    summed = summed + jnp.einsum(
        "rwk,kc->crw", stacked[:-1, :-1], corner_taps, preferred_element_type=jnp.float32
    )
    return (summed + down_bias[:, None, None]).astype(jnp.bfloat16)


def layer_norm(features, norm_gain):
    values = features.astype(jnp.float32)
    mean_value = jnp.mean(values, axis=0, keepdims=True)
    centered = values - mean_value
    variance = jnp.mean(centered * centered, axis=0, keepdims=True)
    return (norm_gain[:, None, None] * centered * lax.rsqrt(variance + EPSILON)).astype(
        jnp.bfloat16
    )


def filter_columns(row_spectrum, kernel, forward_h, inverse_h):
    spectrum = jnp.einsum(
        "puqh,chqw->cpuw", forward_h, row_spectrum, preferred_element_type=jnp.float32
    ).astype(jnp.bfloat16)
    spec_real = spectrum[:, 0].astype(jnp.float32)
    spec_imag = spectrum[:, 1].astype(jnp.float32)
    filter_real = kernel[:, 0].astype(jnp.float32)
    filter_imag = kernel[:, 1].astype(jnp.float32)
    weighted = jnp.stack(
        [
            filter_real * spec_real - filter_imag * spec_imag,
            filter_real * spec_imag + filter_imag * spec_real,
        ],
        axis=1,
    ).astype(jnp.bfloat16)
    return jnp.einsum(
        "qhpu,cpuw->chqw", inverse_h, weighted, preferred_element_type=jnp.float32
    ).astype(jnp.bfloat16)


def local(
    aerial_patch_grid,
    patch_conv_weight,
    patch_bias,
    merging_conv_weight,
    merge_bias,
    down_weight,
    down_bias,
    norm_gain,
    spectral_filter,
):
    section_index = lax.axis_index("section")
    field_cols = aerial_patch_grid.shape[1]
    channels = down_weight.shape[3]
    full_rows = spectral_filter.shape[2]
    half_channels = channels // 2
    cell_half = field_cols // 2
    image_part = lax.dynamic_slice_in_dim(
        aerial_patch_grid, section_index * cell_half, cell_half, 1
    )
    layer_two = stem_layers(
        image_part, patch_conv_weight, patch_bias, merging_conv_weight, merge_bias
    )
    left_column = from_behind(layer_two[:, -1:], "section", 1)
    extended = jnp.concatenate([left_column, layer_two], axis=1)
    upper_rim = rim_above(extended)
    feature_half = down_conv(upper_rim, extended, down_weight, down_bias)
    normed_half = layer_norm(feature_half, norm_gain)
    tiles = lax.axis_size("tile")
    group_width, tile_rows = channels // tiles, normed_half.shape[1]
    arrived = exchange_chunks(normed_half.reshape(tiles, -1), 0)
    fields = (
        arrived.reshape(tiles, group_width, tile_rows, cell_half)
        .transpose(1, 0, 2, 3)
        .reshape(group_width, tiles * tile_rows, cell_half)
    )
    swap = [(0, 1), (1, 0)]
    other_fields = lax.ppermute(fields, "section", swap)

    cos_h, sin_h = fourier_tables(full_rows)
    if full_rows == field_cols:
        cos_w, sin_w = cos_h, sin_h
    else:
        cos_w, sin_w = fourier_tables(field_cols)
    cos_part = lax.dynamic_slice_in_dim(cos_w, section_index * cell_half, cell_half, 1)
    sin_part = lax.dynamic_slice_in_dim(sin_w, section_index * cell_half, cell_half, 1)
    forward_table = jnp.stack([cos_part, -sin_part], axis=1)
    inverse_table = jnp.stack([cos_part, -sin_part], axis=0)
    forward_h = jnp.stack(
        [jnp.stack([cos_h, sin_h], axis=1), jnp.stack([-sin_h, cos_h], axis=1)], axis=0
    )
    inverse_h = jnp.stack(
        [jnp.stack([cos_h, -sin_h], axis=1), jnp.stack([sin_h, cos_h], axis=1)], axis=0
    )
    norm_scale = 1.0 / (full_rows * field_cols)
    kernel_part = lax.dynamic_slice_in_dim(
        spectral_filter, section_index * cell_half, cell_half, 3
    )
    own_start = section_index * cell_half
    other_start = (1 - section_index) * cell_half
    frequency_rows = jnp.einsum(
        "chx,xqw->chqw",
        fields,
        lax.dynamic_slice_in_dim(forward_table, own_start, cell_half, 0),
        preferred_element_type=jnp.float32,
    ) + jnp.einsum(
        "chx,xqw->chqw",
        other_fields,
        lax.dynamic_slice_in_dim(forward_table, other_start, cell_half, 0),
        preferred_element_type=jnp.float32,
    )
    back_rows = filter_columns(
        frequency_rows.astype(jnp.bfloat16), kernel_part, forward_h, inverse_h
    )
    other_rows = lax.ppermute(back_rows, "section", swap)
    result = jnp.einsum(
        "chqw,qwv->chv",
        back_rows,
        lax.dynamic_slice_in_dim(inverse_table, own_start, cell_half, 1),
        preferred_element_type=jnp.float32,
    ) + jnp.einsum(
        "chqw,qwv->chv",
        other_rows,
        lax.dynamic_slice_in_dim(inverse_table, other_start, cell_half, 1),
        preferred_element_type=jnp.float32,
    )
    filtered_fields = (result * norm_scale).astype(jnp.bfloat16)
    outgoing = (
        filtered_fields.reshape(group_width, tiles, tile_rows, cell_half)
        .transpose(1, 0, 2, 3)
        .reshape(tiles, -1)
    )
    rows_back = exchange_chunks(outgoing, 1)
    summed = (
        feature_half.reshape(tiles, -1).astype(jnp.float32) + rows_back.astype(jnp.float32)
    ).astype(jnp.bfloat16).reshape(channels, tile_rows, cell_half)
    kept = lax.dynamic_slice_in_dim(summed, section_index * half_channels, half_channels, 0)
    sent = lax.dynamic_slice_in_dim(
        summed, (1 - section_index) * half_channels, half_channels, 0
    )
    received = lax.ppermute(sent, "section", swap)
    return jnp.where(
        section_index == 0,
        jnp.concatenate([kept, received], axis=2),
        jnp.concatenate([received, kept], axis=2),
    )


def solution(mesh):
    return jax.shard_map(
        local,
        mesh=mesh,
        in_specs=(
            P("tile", None, None),
            P(),
            P(),
            P(),
            P(),
            P(),
            P(),
            P(),
            P("tile", None, None, None),
        ),
        out_specs=P("section", "tile", None),
        check_vma=False,
    )
```

```python
import math

import jax
import jax.numpy as jnp
from jax import lax
from jax.experimental import pallas as pl
from jax.experimental.pallas import tpu as pltpu
from jax.sharding import PartitionSpec as P

EPSILON = 1e-05
MESH_ID = pl.DeviceIdType.MESH


def exchange_kernel(x_ref, o_ref, send_sem, recv_sem, own_sem):
    count = x_ref.shape[0]
    me = lax.axis_index("tile")
    section = lax.axis_index("section")
    barrier = pltpu.get_barrier_semaphore()

    def greet(step, carry):
        peer = lax.rem(me + step, count)
        pl.semaphore_signal(barrier, 1, device_id=(section, peer), device_id_type=MESH_ID)
        return carry

    lax.fori_loop(1, count, greet, 0)
    pl.semaphore_wait(barrier, count - 1)
    own = pltpu.make_async_copy(x_ref.at[pl.ds(me, 1)], o_ref.at[pl.ds(me, 1)], own_sem)
    own.start()

    def send(step, carry):
        peer = lax.rem(me + step, count)
        pltpu.make_async_remote_copy(
            src_ref=x_ref.at[pl.ds(peer, 1)],
            dst_ref=o_ref.at[pl.ds(me, 1)],
            send_sem=send_sem,
            recv_sem=recv_sem,
            device_id=(section, peer),
            device_id_type=MESH_ID,
        ).start()
        return carry

    lax.fori_loop(1, count, send, 0)
    every = pltpu.make_async_remote_copy(
        src_ref=x_ref.at[pl.ds(0, count - 1)],
        dst_ref=o_ref.at[pl.ds(0, count - 1)],
        send_sem=send_sem,
        recv_sem=recv_sem,
        device_id=(section, lax.rem(me + 1, count)),
        device_id_type=MESH_ID,
    )
    every.wait_send()
    every.wait_recv()
    own.wait()


def exchange(chunks, collective_id):
    return pl.pallas_call(
        exchange_kernel,
        out_shape=jax.ShapeDtypeStruct(chunks.shape, chunks.dtype),
        in_specs=[pl.BlockSpec(memory_space=pl.ANY)],
        out_specs=pl.BlockSpec(memory_space=pl.ANY),
        scratch_shapes=[pltpu.SemaphoreType.DMA(())] * 3,
        compiler_params=pltpu.CompilerParams(collective_id=collective_id, has_side_effects=True),
    )(chunks)


def exchange_chunks(chunks, collective_id):
    count, length = chunks.shape
    padded = -(-length // 2048) * 2048
    slabs = jnp.pad(chunks, ((0, 0), (0, padded - length))).reshape(count, padded // 128, 128)
    return exchange(slabs, collective_id).reshape(count, padded)[:, :length]


def from_behind(block, axis, distance):
    devices = range(lax.axis_size(axis))
    route = [(i - distance, i) for i in devices if i - distance in devices]
    return lax.ppermute(block, axis, route)


def fourier_tables(length):
    indices = jnp.arange(length, dtype=jnp.int32)
    product = indices[:, None] * indices[None, :] % length
    angles = product.astype(jnp.float32) * (2.0 * math.pi / length)
    return (jnp.cos(angles).astype(jnp.bfloat16), jnp.sin(angles).astype(jnp.bfloat16))


def one_hot_rows(indices, width):
    return (indices[:, None] == jnp.arange(width, dtype=jnp.int32)[None, :]).astype(jnp.bfloat16)


def spread_kernel(weight_rows, row_pick, row_cell, col_cell, width, out_cols):
    picked = jnp.dot(
        one_hot_rows(row_pick, weight_rows.shape[0]), weight_rows,
        preferred_element_type=jnp.float32,
    ).astype(jnp.bfloat16)
    col = jnp.arange(out_cols, dtype=jnp.int32)
    repeat = one_hot_rows(col % width, width).T
    full = jnp.dot(picked, repeat, preferred_element_type=jnp.float32)
    mask = row_cell[:, None] == col_cell[None, :]
    return jnp.where(mask, full, 0.0).astype(jnp.bfloat16)


def patch_kernel_matrix(patch_conv_weight):
    band_count = patch_conv_weight.shape[0]
    width = patch_conv_weight.shape[3]
    row = jnp.arange(band_count * 256, dtype=jnp.int32)
    pick = (row // 256) * 16 + ((row // 16) % 4) * 4 + row % 4
    row_cell = ((row // 64) % 4) * 4 + (row // 4) % 4
    col = jnp.arange(16 * width, dtype=jnp.int32)
    col_cell = col // width
    weight_rows = patch_conv_weight.reshape(band_count * 16, width)
    return spread_kernel(weight_rows, pick, row_cell, col_cell, width, 16 * width)


def merging_kernel_matrix(merging_conv_weight):
    in_width = merging_conv_weight.shape[2]
    out_width = merging_conv_weight.shape[3]
    row = jnp.arange(16 * in_width, dtype=jnp.int32)
    pos = row // in_width
    pick = ((pos // 4) % 2 * 2 + pos % 2) * in_width + row % in_width
    row_cell = (pos // 8) * 2 + (pos // 2) % 2
    col = jnp.arange(4 * out_width, dtype=jnp.int32)
    col_cell = col // out_width
    weight_rows = merging_conv_weight.reshape(4 * in_width, out_width)
    return spread_kernel(weight_rows, pick, row_cell, col_cell, out_width, 4 * out_width)


def down_matrices(down_weight):
    in_width = down_weight.shape[2]
    out_width = down_weight.shape[3]
    padded = jnp.pad(down_weight, ((1, 0), (1, 0), (0, 0), (0, 0)))

    def taps(first, second):
        return padded[first : first + 2, second : second + 2].reshape(4 * in_width, out_width)

    return (taps(2, 2), taps(0, 2), taps(2, 0), taps(0, 0))


def stem_layers(aerial_patch_grid, patch_conv_weight, patch_bias, merging_conv_weight, merge_bias):
    initial_layer = jnp.einsum(
        "zji,if->zjf",
        aerial_patch_grid,
        patch_kernel_matrix(patch_conv_weight),
        preferred_element_type=jnp.float32,
    )
    initial_layer = jax.nn.gelu(initial_layer + jnp.tile(patch_bias, 16), approximate=True).astype(
        jnp.bfloat16
    )
    layer_two = jnp.einsum(
        "zji,if->zjf",
        initial_layer,
        merging_kernel_matrix(merging_conv_weight),
        preferred_element_type=jnp.float32,
    )
    return jax.nn.gelu(layer_two + jnp.tile(merge_bias, 4), approximate=True).astype(jnp.bfloat16)


def rim_above(extended):
    return from_behind(extended[-1:], "tile", 1)


def down_conv(upper_rim, extended, down_weight, down_bias):
    stacked = jnp.concatenate([upper_rim, extended], axis=0)
    own_taps, upper_taps, left_taps, corner_taps = down_matrices(down_weight)
    summed = jnp.einsum(
        "rwk,kc->crw", stacked[1:, 1:], own_taps, preferred_element_type=jnp.float32
    )
    summed = summed + jnp.einsum(
        "rwk,kc->crw", stacked[:-1, 1:], upper_taps, preferred_element_type=jnp.float32
    )
    summed = summed + jnp.einsum(
        "rwk,kc->crw", stacked[1:, :-1], left_taps, preferred_element_type=jnp.float32
    )
    summed = summed + jnp.einsum(
        "rwk,kc->crw", stacked[:-1, :-1], corner_taps, preferred_element_type=jnp.float32
    )
    return (summed + down_bias[:, None, None]).astype(jnp.bfloat16)


def layer_norm(features, norm_gain):
    values = features.astype(jnp.float32)
    mean_value = jnp.mean(values, axis=0, keepdims=True)
    centered = values - mean_value
    variance = jnp.mean(centered * centered, axis=0, keepdims=True)
    return (norm_gain[:, None, None] * centered * lax.rsqrt(variance + EPSILON)).astype(
        jnp.bfloat16
    )


def filter_columns(row_spectrum, kernel, forward_h, inverse_h):
    spectrum = jnp.einsum(
        "puqh,chqw->cpuw", forward_h, row_spectrum, preferred_element_type=jnp.float32
    ).astype(jnp.bfloat16)
    spec_real = spectrum[:, 0].astype(jnp.float32)
    spec_imag = spectrum[:, 1].astype(jnp.float32)
    filter_real = kernel[:, 0].astype(jnp.float32)
    filter_imag = kernel[:, 1].astype(jnp.float32)
    weighted = jnp.stack(
        [
            filter_real * spec_real - filter_imag * spec_imag,
            filter_real * spec_imag + filter_imag * spec_real,
        ],
        axis=1,
    ).astype(jnp.bfloat16)
    return jnp.einsum(
        "qhpu,cpuw->chqw", inverse_h, weighted, preferred_element_type=jnp.float32
    ).astype(jnp.bfloat16)


def local(
    aerial_patch_grid,
    patch_conv_weight,
    patch_bias,
    merging_conv_weight,
    merge_bias,
    down_weight,
    down_bias,
    norm_gain,
    spectral_filter,
):
    section_index = lax.axis_index("section")
    field_cols = aerial_patch_grid.shape[1]
    channels = down_weight.shape[3]
    full_rows = spectral_filter.shape[2]
    half_channels = channels // 2
    cell_half = field_cols // 2
    image_part = lax.dynamic_slice_in_dim(
        aerial_patch_grid, section_index * cell_half, cell_half, 1
    )
    layer_two = stem_layers(
        image_part, patch_conv_weight, patch_bias, merging_conv_weight, merge_bias
    )
    left_column = from_behind(layer_two[:, -1:], "section", 1)
    extended = jnp.concatenate([left_column, layer_two], axis=1)
    upper_rim = rim_above(extended)
    feature_half = down_conv(upper_rim, extended, down_weight, down_bias)
    normed_half = layer_norm(feature_half, norm_gain)
    tiles = lax.axis_size("tile")
    group_width, tile_rows = channels // tiles, normed_half.shape[1]
    arrived = exchange_chunks(normed_half.reshape(tiles, -1), 0)
    fields = (
        arrived.reshape(tiles, group_width, tile_rows, cell_half)
        .transpose(1, 0, 2, 3)
        .reshape(group_width, tiles * tile_rows, cell_half)
    )
    swap = [(0, 1), (1, 0)]
    other_fields = lax.ppermute(fields, "section", swap)

    cos_h, sin_h = fourier_tables(full_rows)
    if full_rows == field_cols:
        cos_w, sin_w = cos_h, sin_h
    else:
        cos_w, sin_w = fourier_tables(field_cols)
    cos_part = lax.dynamic_slice_in_dim(cos_w, section_index * cell_half, cell_half, 1)
    sin_part = lax.dynamic_slice_in_dim(sin_w, section_index * cell_half, cell_half, 1)
    forward_table = jnp.stack([cos_part, -sin_part], axis=1)
    inverse_table = jnp.stack([cos_part, -sin_part], axis=0)
    forward_h = jnp.stack(
        [jnp.stack([cos_h, sin_h], axis=1), jnp.stack([-sin_h, cos_h], axis=1)], axis=0
    )
    inverse_h = jnp.stack(
        [jnp.stack([cos_h, -sin_h], axis=1), jnp.stack([sin_h, cos_h], axis=1)], axis=0
    )
    norm_scale = 1.0 / (full_rows * field_cols)
    kernel_part = lax.dynamic_slice_in_dim(
        spectral_filter, section_index * cell_half, cell_half, 3
    )
    own_start = section_index * cell_half
    other_start = (1 - section_index) * cell_half
    frequency_rows = jnp.einsum(
        "chx,xqw->chqw",
        fields,
        lax.dynamic_slice_in_dim(forward_table, own_start, cell_half, 0),
        preferred_element_type=jnp.float32,
    ) + jnp.einsum(
        "chx,xqw->chqw",
        other_fields,
        lax.dynamic_slice_in_dim(forward_table, other_start, cell_half, 0),
        preferred_element_type=jnp.float32,
    )
    back_rows = filter_columns(
        frequency_rows.astype(jnp.bfloat16), kernel_part, forward_h, inverse_h
    )
    other_rows = lax.ppermute(back_rows, "section", swap)
    result = jnp.einsum(
        "chqw,qwv->chv",
        back_rows,
        lax.dynamic_slice_in_dim(inverse_table, own_start, cell_half, 1),
        preferred_element_type=jnp.float32,
    ) + jnp.einsum(
        "chqw,qwv->chv",
        other_rows,
        lax.dynamic_slice_in_dim(inverse_table, other_start, cell_half, 1),
        preferred_element_type=jnp.float32,
    )
    filtered_fields = (result * norm_scale).astype(jnp.bfloat16)
    outgoing = (
        filtered_fields.reshape(group_width, tiles, tile_rows, cell_half)
        .transpose(1, 0, 2, 3)
        .reshape(tiles, -1)
    )
    rows_back = exchange_chunks(outgoing, 1)
    summed = (
        feature_half.reshape(tiles, -1).astype(jnp.float32) + rows_back.astype(jnp.float32)
    ).astype(jnp.bfloat16).reshape(channels, tile_rows, cell_half)
    kept = lax.dynamic_slice_in_dim(summed, section_index * half_channels, half_channels, 0)
    sent = lax.dynamic_slice_in_dim(
        summed, (1 - section_index) * half_channels, half_channels, 0
    )
    received = lax.ppermute(sent, "section", swap)
    return jnp.where(
        section_index == 0,
        jnp.concatenate([kept, received], axis=2),
        jnp.concatenate([received, kept], axis=2),
    )


def solution(mesh):
    return jax.shard_map(
        local,
        mesh=mesh,
        in_specs=(
            P("tile", None, None),
            P(),
            P(),
            P(),
            P(),
            P(),
            P(),
            P(),
            P("tile", None, None, None),
        ),
        out_specs=P("section", "tile", None),
        check_vma=False,
    )
```

```python
import math

import jax
import jax.numpy as jnp
from jax import lax
from jax.experimental import pallas as pl
from jax.experimental.pallas import tpu as pltpu
from jax.sharding import PartitionSpec as P

EPSILON = 1e-05
MESH_ID = pl.DeviceIdType.MESH


def start_exchange(x_ref, o_ref, send_sem, recv_sem, own_sem):
    count = x_ref.shape[0]
    me = lax.axis_index("tile")
    section = lax.axis_index("section")
    barrier = pltpu.get_barrier_semaphore()

    def greet(step, carry):
        peer = lax.rem(me + step, count)
        pl.semaphore_signal(barrier, 1, device_id=(section, peer), device_id_type=MESH_ID)
        return carry

    lax.fori_loop(1, count, greet, 0)
    pl.semaphore_wait(barrier, count - 1)
    own = pltpu.make_async_copy(x_ref.at[pl.ds(me, 1)], o_ref.at[pl.ds(me, 1)], own_sem)
    own.start()

    def send(step, carry):
        peer = lax.rem(me + step, count)
        pltpu.make_async_remote_copy(
            src_ref=x_ref.at[pl.ds(peer, 1)],
            dst_ref=o_ref.at[pl.ds(me, 1)],
            send_sem=send_sem,
            recv_sem=recv_sem,
            device_id=(section, peer),
            device_id_type=MESH_ID,
        ).start()
        return carry

    lax.fori_loop(1, count, send, 0)
    every = pltpu.make_async_remote_copy(
        src_ref=x_ref.at[pl.ds(0, count - 1)],
        dst_ref=o_ref.at[pl.ds(0, count - 1)],
        send_sem=send_sem,
        recv_sem=recv_sem,
        device_id=(section, lax.rem(me + 1, count)),
        device_id_type=MESH_ID,
    )
    return every, own


def finish_exchange(every, own):
    every.wait_send()
    every.wait_recv()
    own.wait()


def exchange_kernel(x_ref, o_ref, send_sem, recv_sem, own_sem):
    finish_exchange(*start_exchange(x_ref, o_ref, send_sem, recv_sem, own_sem))


def exchange_tables_kernel(x_ref, o_ref, cos_ref, sin_ref, send_sem, recv_sem, own_sem):
    pending = start_exchange(x_ref, o_ref, send_sem, recv_sem, own_sem)
    length = cos_ref.shape[0]
    block = 16

    def rows(index, carry):
        first = pl.multiple_of(index * block, block)
        row = lax.broadcasted_iota(jnp.int32, (block, length), 0) + first
        col = lax.broadcasted_iota(jnp.int32, (block, length), 1)
        angles = lax.rem(row * col, length).astype(jnp.float32) * (2.0 * math.pi / length)
        cos_ref[pl.ds(first, block), :] = jnp.cos(angles).astype(cos_ref.dtype)
        sin_ref[pl.ds(first, block), :] = jnp.sin(angles).astype(sin_ref.dtype)
        return carry

    lax.fori_loop(0, length // block, rows, 0)
    finish_exchange(*pending)


def exchange(chunks, collective_id):
    return pl.pallas_call(
        exchange_kernel,
        out_shape=jax.ShapeDtypeStruct(chunks.shape, chunks.dtype),
        in_specs=[pl.BlockSpec(memory_space=pl.ANY)],
        out_specs=pl.BlockSpec(memory_space=pl.ANY),
        scratch_shapes=[pltpu.SemaphoreType.DMA(())] * 3,
        compiler_params=pltpu.CompilerParams(collective_id=collective_id, has_side_effects=True),
    )(chunks)


def exchange_with_tables(chunks, collective_id, length):
    table = jax.ShapeDtypeStruct((length, length), jnp.bfloat16)
    return pl.pallas_call(
        exchange_tables_kernel,
        out_shape=(jax.ShapeDtypeStruct(chunks.shape, chunks.dtype), table, table),
        in_specs=[pl.BlockSpec(memory_space=pl.ANY)],
        out_specs=(
            pl.BlockSpec(memory_space=pl.ANY),
            pl.BlockSpec(memory_space=pltpu.VMEM),
            pl.BlockSpec(memory_space=pltpu.VMEM),
        ),
        scratch_shapes=[pltpu.SemaphoreType.DMA(())] * 3,
        compiler_params=pltpu.CompilerParams(collective_id=collective_id, has_side_effects=True),
    )(chunks)


def pad_chunks(chunks):
    count, length = chunks.shape
    padded = -(-length // 2048) * 2048
    slabs = jnp.pad(chunks, ((0, 0), (0, padded - length)))
    return slabs.reshape(count, padded // 128, 128), length


def unpad_chunks(slabs, length):
    return slabs.reshape(slabs.shape[0], -1)[:, :length]


def exchange_chunks(chunks, collective_id):
    count, length = chunks.shape
    padded = -(-length // 2048) * 2048
    slabs = jnp.pad(chunks, ((0, 0), (0, padded - length))).reshape(count, padded // 128, 128)
    return exchange(slabs, collective_id).reshape(count, padded)[:, :length]


def from_behind(block, axis, distance):
    devices = range(lax.axis_size(axis))
    route = [(i - distance, i) for i in devices if i - distance in devices]
    return lax.ppermute(block, axis, route)


def fourier_tables(length):
    indices = jnp.arange(length, dtype=jnp.int32)
    product = indices[:, None] * indices[None, :] % length
    angles = product.astype(jnp.float32) * (2.0 * math.pi / length)
    return (jnp.cos(angles).astype(jnp.bfloat16), jnp.sin(angles).astype(jnp.bfloat16))


def one_hot_rows(indices, width):
    return (indices[:, None] == jnp.arange(width, dtype=jnp.int32)[None, :]).astype(jnp.bfloat16)


def spread_kernel(weight_rows, row_pick, row_cell, col_cell, width, out_cols):
    picked = jnp.dot(
        one_hot_rows(row_pick, weight_rows.shape[0]), weight_rows,
        preferred_element_type=jnp.float32,
    ).astype(jnp.bfloat16)
    col = jnp.arange(out_cols, dtype=jnp.int32)
    repeat = one_hot_rows(col % width, width).T
    full = jnp.dot(picked, repeat, preferred_element_type=jnp.float32)
    mask = row_cell[:, None] == col_cell[None, :]
    return jnp.where(mask, full, 0.0).astype(jnp.bfloat16)


def patch_kernel_matrix(patch_conv_weight):
    band_count = patch_conv_weight.shape[0]
    width = patch_conv_weight.shape[3]
    row = jnp.arange(band_count * 256, dtype=jnp.int32)
    pick = (row // 256) * 16 + ((row // 16) % 4) * 4 + row % 4
    row_cell = ((row // 64) % 4) * 4 + (row // 4) % 4
    col = jnp.arange(16 * width, dtype=jnp.int32)
    col_cell = col // width
    weight_rows = patch_conv_weight.reshape(band_count * 16, width)
    return spread_kernel(weight_rows, pick, row_cell, col_cell, width, 16 * width)


def merging_kernel_matrix(merging_conv_weight):
    in_width = merging_conv_weight.shape[2]
    out_width = merging_conv_weight.shape[3]
    row = jnp.arange(16 * in_width, dtype=jnp.int32)
    pos = row // in_width
    pick = ((pos // 4) % 2 * 2 + pos % 2) * in_width + row % in_width
    row_cell = (pos // 8) * 2 + (pos // 2) % 2
    col = jnp.arange(4 * out_width, dtype=jnp.int32)
    col_cell = col // out_width
    weight_rows = merging_conv_weight.reshape(4 * in_width, out_width)
    return spread_kernel(weight_rows, pick, row_cell, col_cell, out_width, 4 * out_width)


def down_matrices(down_weight):
    nothing = jnp.zeros_like(down_weight[0, 0])
    in_width = down_weight.shape[2]
    out_width = down_weight.shape[3]

    def arrange(entries):
        return jnp.stack(
            [jnp.stack(entries[0], axis=0), jnp.stack(entries[1], axis=0)], axis=0
        ).reshape(4 * in_width, out_width)

    own_taps = arrange(
        [[down_weight[1, 1], down_weight[1, 2]], [down_weight[2, 1], down_weight[2, 2]]]
    )
    upper_taps = arrange([[nothing, nothing], [down_weight[0, 1], down_weight[0, 2]]])
    left_taps = arrange([[nothing, down_weight[1, 0]], [nothing, down_weight[2, 0]]])
    corner_taps = arrange([[nothing, nothing], [nothing, down_weight[0, 0]]])
    return (own_taps, upper_taps, left_taps, corner_taps)


def stem_layers(aerial_patch_grid, patch_conv_weight, patch_bias, merging_conv_weight, merge_bias):
    initial_layer = jnp.einsum(
        "zji,if->zjf",
        aerial_patch_grid,
        patch_kernel_matrix(patch_conv_weight),
        preferred_element_type=jnp.float32,
    )
    initial_layer = jax.nn.gelu(initial_layer + jnp.tile(patch_bias, 16), approximate=True).astype(
        jnp.bfloat16
    )
    layer_two = jnp.einsum(
        "zji,if->zjf",
        initial_layer,
        merging_kernel_matrix(merging_conv_weight),
        preferred_element_type=jnp.float32,
    )
    return jax.nn.gelu(layer_two + jnp.tile(merge_bias, 4), approximate=True).astype(jnp.bfloat16)


def rim_above(extended):
    return from_behind(extended[-1:], "tile", 1)


def down_conv(upper_rim, extended, down_weight, down_bias):
    stacked = jnp.concatenate([upper_rim, extended], axis=0)
    own_taps, upper_taps, left_taps, corner_taps = down_matrices(down_weight)
    summed = jnp.einsum(
        "rwk,kc->crw", stacked[1:, 1:], own_taps, preferred_element_type=jnp.float32
    )
    summed = summed + jnp.einsum(
        "rwk,kc->crw", stacked[:-1, 1:], upper_taps, preferred_element_type=jnp.float32
    )
    summed = summed + jnp.einsum(
        "rwk,kc->crw", stacked[1:, :-1], left_taps, preferred_element_type=jnp.float32
    )
    summed = summed + jnp.einsum(
        "rwk,kc->crw", stacked[:-1, :-1], corner_taps, preferred_element_type=jnp.float32
    )
    return (summed + down_bias[:, None, None]).astype(jnp.bfloat16)


def layer_norm(features, norm_gain):
    values = features.astype(jnp.float32)
    mean_value = jnp.mean(values, axis=0, keepdims=True)
    centered = values - mean_value
    variance = jnp.mean(centered * centered, axis=0, keepdims=True)
    return (norm_gain[:, None, None] * centered * lax.rsqrt(variance + EPSILON)).astype(
        jnp.bfloat16
    )


def filter_columns(row_spectrum, kernel, forward_h, inverse_h):
    spectrum = jnp.einsum(
        "puqh,chqw->cpuw", forward_h, row_spectrum, preferred_element_type=jnp.float32
    ).astype(jnp.bfloat16)
    spec_real = spectrum[:, 0].astype(jnp.float32)
    spec_imag = spectrum[:, 1].astype(jnp.float32)
    filter_real = kernel[:, 0].astype(jnp.float32)
    filter_imag = kernel[:, 1].astype(jnp.float32)
    weighted = jnp.stack(
        [
            filter_real * spec_real - filter_imag * spec_imag,
            filter_real * spec_imag + filter_imag * spec_real,
        ],
        axis=1,
    ).astype(jnp.bfloat16)
    return jnp.einsum(
        "qhpu,cpuw->chqw", inverse_h, weighted, preferred_element_type=jnp.float32
    ).astype(jnp.bfloat16)


def local(
    aerial_patch_grid,
    patch_conv_weight,
    patch_bias,
    merging_conv_weight,
    merge_bias,
    down_weight,
    down_bias,
    norm_gain,
    spectral_filter,
):
    section_index = lax.axis_index("section")
    field_cols = aerial_patch_grid.shape[1]
    channels = down_weight.shape[3]
    full_rows = spectral_filter.shape[2]
    half_channels = channels // 2
    cell_half = field_cols // 2
    image_part = lax.dynamic_slice_in_dim(
        aerial_patch_grid, section_index * cell_half, cell_half, 1
    )
    layer_two = stem_layers(
        image_part, patch_conv_weight, patch_bias, merging_conv_weight, merge_bias
    )
    left_column = from_behind(layer_two[:, -1:], "section", 1)
    extended = jnp.concatenate([left_column, layer_two], axis=1)
    upper_rim = rim_above(extended)
    feature_half = down_conv(upper_rim, extended, down_weight, down_bias)
    normed_half = layer_norm(feature_half, norm_gain)
    tiles = lax.axis_size("tile")
    group_width, tile_rows = channels // tiles, normed_half.shape[1]
    slabs, length = pad_chunks(normed_half.reshape(tiles, -1))
    slabs, cos_h, sin_h = exchange_with_tables(slabs, 0, full_rows)
    arrived = unpad_chunks(slabs, length)
    fields = (
        arrived.reshape(tiles, group_width, tile_rows, cell_half)
        .transpose(1, 0, 2, 3)
        .reshape(group_width, tiles * tile_rows, cell_half)
    )
    swap = [(0, 1), (1, 0)]
    other_fields = lax.ppermute(fields, "section", swap)

    if full_rows == field_cols:
        cos_w, sin_w = cos_h, sin_h
    else:
        cos_w, sin_w = fourier_tables(field_cols)
    cos_part = lax.dynamic_slice_in_dim(cos_w, section_index * cell_half, cell_half, 1)
    sin_part = lax.dynamic_slice_in_dim(sin_w, section_index * cell_half, cell_half, 1)
    forward_table = jnp.stack([cos_part, -sin_part], axis=1)
    inverse_table = jnp.stack([cos_part, -sin_part], axis=0)
    forward_h = jnp.stack(
        [jnp.stack([cos_h, sin_h], axis=1), jnp.stack([-sin_h, cos_h], axis=1)], axis=0
    )
    inverse_h = jnp.stack(
        [jnp.stack([cos_h, -sin_h], axis=1), jnp.stack([sin_h, cos_h], axis=1)], axis=0
    )
    norm_scale = 1.0 / (full_rows * field_cols)
    kernel_part = lax.dynamic_slice_in_dim(
        spectral_filter, section_index * cell_half, cell_half, 3
    )
    own_start = section_index * cell_half
    other_start = (1 - section_index) * cell_half
    frequency_rows = jnp.einsum(
        "chx,xqw->chqw",
        fields,
        lax.dynamic_slice_in_dim(forward_table, own_start, cell_half, 0),
        preferred_element_type=jnp.float32,
    ) + jnp.einsum(
        "chx,xqw->chqw",
        other_fields,
        lax.dynamic_slice_in_dim(forward_table, other_start, cell_half, 0),
        preferred_element_type=jnp.float32,
    )
    back_rows = filter_columns(
        frequency_rows.astype(jnp.bfloat16), kernel_part, forward_h, inverse_h
    )
    other_rows = lax.ppermute(back_rows, "section", swap)
    result = jnp.einsum(
        "chqw,qwv->chv",
        back_rows,
        lax.dynamic_slice_in_dim(inverse_table, own_start, cell_half, 1),
        preferred_element_type=jnp.float32,
    ) + jnp.einsum(
        "chqw,qwv->chv",
        other_rows,
        lax.dynamic_slice_in_dim(inverse_table, other_start, cell_half, 1),
        preferred_element_type=jnp.float32,
    )
    filtered_fields = (result * norm_scale).astype(jnp.bfloat16)
    outgoing = (
        filtered_fields.reshape(group_width, tiles, tile_rows, cell_half)
        .transpose(1, 0, 2, 3)
        .reshape(tiles, -1)
    )
    rows_back = exchange_chunks(outgoing, 1).reshape(channels, tile_rows, cell_half)
    summed = (feature_half.astype(jnp.float32) + rows_back.astype(jnp.float32)).astype(
        jnp.bfloat16
    )
    kept = lax.dynamic_slice_in_dim(summed, section_index * half_channels, half_channels, 0)
    sent = lax.dynamic_slice_in_dim(
        summed, (1 - section_index) * half_channels, half_channels, 0
    )
    received = lax.ppermute(sent, "section", swap)
    return jnp.where(
        section_index == 0,
        jnp.concatenate([kept, received], axis=2),
        jnp.concatenate([received, kept], axis=2),
    )


def solution(mesh):
    return jax.shard_map(
        local,
        mesh=mesh,
        in_specs=(
            P("tile", None, None),
            P(),
            P(),
            P(),
            P(),
            P(),
            P(),
            P(),
            P("tile", None, None, None),
        ),
        out_specs=P("section", "tile", None),
        check_vma=False,
    )
```

```python
import math

import jax
import jax.numpy as jnp
from jax import lax
from jax.experimental import pallas as pl
from jax.experimental.pallas import tpu as pltpu
from jax.sharding import PartitionSpec as P

EPSILON = 1e-05
MESH_ID = pl.DeviceIdType.MESH


def start_exchange(x_ref, o_ref, send_sem, recv_sem, own_sem):
    count = x_ref.shape[0]
    me = lax.axis_index("tile")
    section = lax.axis_index("section")
    barrier = pltpu.get_barrier_semaphore()

    def greet(step, carry):
        peer = lax.rem(me + step, count)
        pl.semaphore_signal(barrier, 1, device_id=(section, peer), device_id_type=MESH_ID)
        return carry

    lax.fori_loop(1, count, greet, 0)
    pl.semaphore_wait(barrier, count - 1)
    own = pltpu.make_async_copy(x_ref.at[pl.ds(me, 1)], o_ref.at[pl.ds(me, 1)], own_sem)
    own.start()

    def send(step, carry):
        peer = lax.rem(me + step, count)
        pltpu.make_async_remote_copy(
            src_ref=x_ref.at[pl.ds(peer, 1)],
            dst_ref=o_ref.at[pl.ds(me, 1)],
            send_sem=send_sem,
            recv_sem=recv_sem,
            device_id=(section, peer),
            device_id_type=MESH_ID,
        ).start()
        return carry

    lax.fori_loop(1, count, send, 0)
    every = pltpu.make_async_remote_copy(
        src_ref=x_ref.at[pl.ds(0, count - 1)],
        dst_ref=o_ref.at[pl.ds(0, count - 1)],
        send_sem=send_sem,
        recv_sem=recv_sem,
        device_id=(section, lax.rem(me + 1, count)),
        device_id_type=MESH_ID,
    )
    return every, own


def finish_exchange(every, own):
    every.wait_send()
    every.wait_recv()
    own.wait()


def exchange_kernel(x_ref, o_ref, send_sem, recv_sem, own_sem):
    finish_exchange(*start_exchange(x_ref, o_ref, send_sem, recv_sem, own_sem))


def exchange_tables_kernel(x_ref, o_ref, cos_ref, sin_ref, send_sem, recv_sem, own_sem):
    pending = start_exchange(x_ref, o_ref, send_sem, recv_sem, own_sem)
    length = cos_ref.shape[0]
    block = 16

    def rows(index, carry):
        first = pl.multiple_of(index * block, block)
        row = lax.broadcasted_iota(jnp.int32, (block, length), 0) + first
        col = lax.broadcasted_iota(jnp.int32, (block, length), 1)
        angles = lax.rem(row * col, length).astype(jnp.float32) * (2.0 * math.pi / length)
        cos_ref[pl.ds(first, block), :] = jnp.cos(angles).astype(cos_ref.dtype)
        sin_ref[pl.ds(first, block), :] = jnp.sin(angles).astype(sin_ref.dtype)
        return carry

    lax.fori_loop(0, length // block, rows, 0)
    finish_exchange(*pending)


def exchange(chunks, collective_id):
    return pl.pallas_call(
        exchange_kernel,
        out_shape=jax.ShapeDtypeStruct(chunks.shape, chunks.dtype),
        in_specs=[pl.BlockSpec(memory_space=pl.ANY)],
        out_specs=pl.BlockSpec(memory_space=pl.ANY),
        scratch_shapes=[pltpu.SemaphoreType.DMA(())] * 3,
        compiler_params=pltpu.CompilerParams(collective_id=collective_id, has_side_effects=True),
    )(chunks)


def exchange_with_tables(chunks, collective_id, length):
    table = jax.ShapeDtypeStruct((length, length), jnp.bfloat16)
    return pl.pallas_call(
        exchange_tables_kernel,
        out_shape=(jax.ShapeDtypeStruct(chunks.shape, chunks.dtype), table, table),
        in_specs=[pl.BlockSpec(memory_space=pl.ANY)],
        out_specs=(
            pl.BlockSpec(memory_space=pl.ANY),
            pl.BlockSpec(memory_space=pltpu.VMEM),
            pl.BlockSpec(memory_space=pltpu.VMEM),
        ),
        scratch_shapes=[pltpu.SemaphoreType.DMA(())] * 3,
        compiler_params=pltpu.CompilerParams(collective_id=collective_id, has_side_effects=True),
    )(chunks)


def pad_chunks(chunks):
    count, length = chunks.shape
    padded = -(-length // 2048) * 2048
    slabs = jnp.pad(chunks, ((0, 0), (0, padded - length)))
    return slabs.reshape(count, padded // 128, 128), length


def unpad_chunks(slabs, length):
    return slabs.reshape(slabs.shape[0], -1)[:, :length]


def exchange_chunks(chunks, collective_id):
    count, length = chunks.shape
    padded = -(-length // 2048) * 2048
    slabs = jnp.pad(chunks, ((0, 0), (0, padded - length))).reshape(count, padded // 128, 128)
    return exchange(slabs, collective_id).reshape(count, padded)[:, :length]


def from_behind(block, axis, distance):
    devices = range(lax.axis_size(axis))
    route = [(i - distance, i) for i in devices if i - distance in devices]
    return lax.ppermute(block, axis, route)


def fourier_tables(length):
    indices = jnp.arange(length, dtype=jnp.int32)
    product = indices[:, None] * indices[None, :] % length
    angles = product.astype(jnp.float32) * (2.0 * math.pi / length)
    return (jnp.cos(angles).astype(jnp.bfloat16), jnp.sin(angles).astype(jnp.bfloat16))


def one_hot_rows(indices, width):
    return (indices[:, None] == jnp.arange(width, dtype=jnp.int32)[None, :]).astype(jnp.bfloat16)


def spread_kernel(weight_rows, row_pick, row_cell, col_cell, width, out_cols):
    picked = jnp.dot(
        one_hot_rows(row_pick, weight_rows.shape[0]), weight_rows,
        preferred_element_type=jnp.float32,
    ).astype(jnp.bfloat16)
    col = jnp.arange(out_cols, dtype=jnp.int32)
    repeat = one_hot_rows(col % width, width).T
    full = jnp.dot(picked, repeat, preferred_element_type=jnp.float32)
    mask = row_cell[:, None] == col_cell[None, :]
    return jnp.where(mask, full, 0.0).astype(jnp.bfloat16)


def patch_kernel_matrix(patch_conv_weight):
    band_count = patch_conv_weight.shape[0]
    width = patch_conv_weight.shape[3]
    row = jnp.arange(band_count * 256, dtype=jnp.int32)
    pick = (row // 256) * 16 + ((row // 16) % 4) * 4 + row % 4
    row_cell = ((row // 64) % 4) * 4 + (row // 4) % 4
    col = jnp.arange(16 * width, dtype=jnp.int32)
    col_cell = col // width
    weight_rows = patch_conv_weight.reshape(band_count * 16, width)
    return spread_kernel(weight_rows, pick, row_cell, col_cell, width, 16 * width)


def merging_kernel_matrix(merging_conv_weight):
    in_width = merging_conv_weight.shape[2]
    out_width = merging_conv_weight.shape[3]
    row = jnp.arange(16 * in_width, dtype=jnp.int32)
    pos = row // in_width
    pick = ((pos // 4) % 2 * 2 + pos % 2) * in_width + row % in_width
    row_cell = (pos // 8) * 2 + (pos // 2) % 2
    col = jnp.arange(4 * out_width, dtype=jnp.int32)
    col_cell = col // out_width
    weight_rows = merging_conv_weight.reshape(4 * in_width, out_width)
    return spread_kernel(weight_rows, pick, row_cell, col_cell, out_width, 4 * out_width)


def down_matrices(down_weight):
    nothing = jnp.zeros_like(down_weight[0, 0])
    in_width = down_weight.shape[2]
    out_width = down_weight.shape[3]

    def arrange(entries):
        return jnp.stack(
            [jnp.stack(entries[0], axis=0), jnp.stack(entries[1], axis=0)], axis=0
        ).reshape(4 * in_width, out_width)

    own_taps = arrange(
        [[down_weight[1, 1], down_weight[1, 2]], [down_weight[2, 1], down_weight[2, 2]]]
    )
    upper_taps = arrange([[nothing, nothing], [down_weight[0, 1], down_weight[0, 2]]])
    left_taps = arrange([[nothing, down_weight[1, 0]], [nothing, down_weight[2, 0]]])
    corner_taps = arrange([[nothing, nothing], [nothing, down_weight[0, 0]]])
    return (own_taps, upper_taps, left_taps, corner_taps)


def stem_layers(aerial_patch_grid, patch_conv_weight, patch_bias, merging_conv_weight, merge_bias):
    initial_layer = jnp.einsum(
        "zji,if->zjf",
        aerial_patch_grid,
        patch_kernel_matrix(patch_conv_weight),
        preferred_element_type=jnp.float32,
    )
    initial_layer = jax.nn.gelu(initial_layer + jnp.tile(patch_bias, 16), approximate=True).astype(
        jnp.bfloat16
    )
    layer_two = jnp.einsum(
        "zji,if->zjf",
        initial_layer,
        merging_kernel_matrix(merging_conv_weight),
        preferred_element_type=jnp.float32,
    )
    return jax.nn.gelu(layer_two + jnp.tile(merge_bias, 4), approximate=True).astype(jnp.bfloat16)


def down_conv(stacked, down_weight, down_bias):
    own_taps, upper_taps, left_taps, corner_taps = down_matrices(down_weight)
    summed = jnp.einsum(
        "rwk,kc->crw", stacked[1:, 1:], own_taps, preferred_element_type=jnp.float32
    )
    summed = summed + jnp.einsum(
        "rwk,kc->crw", stacked[:-1, 1:], upper_taps, preferred_element_type=jnp.float32
    )
    summed = summed + jnp.einsum(
        "rwk,kc->crw", stacked[1:, :-1], left_taps, preferred_element_type=jnp.float32
    )
    summed = summed + jnp.einsum(
        "rwk,kc->crw", stacked[:-1, :-1], corner_taps, preferred_element_type=jnp.float32
    )
    return (summed + down_bias[:, None, None]).astype(jnp.bfloat16)


def layer_norm(features, norm_gain):
    values = features.astype(jnp.float32)
    mean_value = jnp.mean(values, axis=0, keepdims=True)
    centered = values - mean_value
    variance = jnp.mean(centered * centered, axis=0, keepdims=True)
    return (norm_gain[:, None, None] * centered * lax.rsqrt(variance + EPSILON)).astype(
        jnp.bfloat16
    )


def filter_columns(row_spectrum, kernel, forward_h, inverse_h):
    spectrum = jnp.einsum(
        "puqh,chqw->cpuw", forward_h, row_spectrum, preferred_element_type=jnp.float32
    ).astype(jnp.bfloat16)
    spec_real = spectrum[:, 0].astype(jnp.float32)
    spec_imag = spectrum[:, 1].astype(jnp.float32)
    filter_real = kernel[:, 0].astype(jnp.float32)
    filter_imag = kernel[:, 1].astype(jnp.float32)
    weighted = jnp.stack(
        [
            filter_real * spec_real - filter_imag * spec_imag,
            filter_real * spec_imag + filter_imag * spec_real,
        ],
        axis=1,
    ).astype(jnp.bfloat16)
    return jnp.einsum(
        "qhpu,cpuw->chqw", inverse_h, weighted, preferred_element_type=jnp.float32
    ).astype(jnp.bfloat16)


def local(
    aerial_patch_grid,
    patch_conv_weight,
    patch_bias,
    merging_conv_weight,
    merge_bias,
    down_weight,
    down_bias,
    norm_gain,
    spectral_filter,
):
    section_index = lax.axis_index("section")
    field_cols = aerial_patch_grid.shape[1]
    channels = down_weight.shape[3]
    full_rows = spectral_filter.shape[2]
    half_channels = channels // 2
    cell_half = field_cols // 2
    tile_index = lax.axis_index("tile")
    grid = jnp.pad(aerial_patch_grid, ((0, 0), (1, 0), (0, 0)))
    own_part = lax.dynamic_slice_in_dim(grid, section_index * cell_half, cell_half + 1, 1)
    image_part = jnp.concatenate([from_behind(own_part[-1:], "tile", 1), own_part], axis=0)
    layer_two = stem_layers(
        image_part, patch_conv_weight, patch_bias, merging_conv_weight, merge_bias
    )
    row_ok = (jnp.arange(layer_two.shape[0]) > 0) | (tile_index > 0)
    col_ok = (jnp.arange(layer_two.shape[1]) > 0) | (section_index > 0)
    stacked = jnp.where(row_ok[:, None, None] & col_ok[None, :, None], layer_two, 0)
    feature_half = down_conv(stacked, down_weight, down_bias)
    normed_half = layer_norm(feature_half, norm_gain)
    tiles = lax.axis_size("tile")
    group_width, tile_rows = channels // tiles, normed_half.shape[1]
    slabs, length = pad_chunks(normed_half.reshape(tiles, -1))
    slabs, cos_h, sin_h = exchange_with_tables(slabs, 0, full_rows)
    arrived = unpad_chunks(slabs, length)
    fields = (
        arrived.reshape(tiles, group_width, tile_rows, cell_half)
        .transpose(1, 0, 2, 3)
        .reshape(group_width, tiles * tile_rows, cell_half)
    )
    swap = [(0, 1), (1, 0)]
    other_fields = lax.ppermute(fields, "section", swap)

    if full_rows == field_cols:
        cos_w, sin_w = cos_h, sin_h
    else:
        cos_w, sin_w = fourier_tables(field_cols)
    cos_part = lax.dynamic_slice_in_dim(cos_w, section_index * cell_half, cell_half, 1)
    sin_part = lax.dynamic_slice_in_dim(sin_w, section_index * cell_half, cell_half, 1)
    forward_table = jnp.stack([cos_part, -sin_part], axis=1)
    inverse_table = jnp.stack([cos_part, -sin_part], axis=0)
    forward_h = jnp.stack(
        [jnp.stack([cos_h, sin_h], axis=1), jnp.stack([-sin_h, cos_h], axis=1)], axis=0
    )
    inverse_h = jnp.stack(
        [jnp.stack([cos_h, -sin_h], axis=1), jnp.stack([sin_h, cos_h], axis=1)], axis=0
    )
    norm_scale = 1.0 / (full_rows * field_cols)
    kernel_part = lax.dynamic_slice_in_dim(
        spectral_filter, section_index * cell_half, cell_half, 3
    )
    own_start = section_index * cell_half
    other_start = (1 - section_index) * cell_half
    frequency_rows = jnp.einsum(
        "chx,xqw->chqw",
        fields,
        lax.dynamic_slice_in_dim(forward_table, own_start, cell_half, 0),
        preferred_element_type=jnp.float32,
    ) + jnp.einsum(
        "chx,xqw->chqw",
        other_fields,
        lax.dynamic_slice_in_dim(forward_table, other_start, cell_half, 0),
        preferred_element_type=jnp.float32,
    )
    back_rows = filter_columns(
        frequency_rows.astype(jnp.bfloat16), kernel_part, forward_h, inverse_h
    )
    other_rows = lax.ppermute(back_rows, "section", swap)
    result = jnp.einsum(
        "chqw,qwv->chv",
        back_rows,
        lax.dynamic_slice_in_dim(inverse_table, own_start, cell_half, 1),
        preferred_element_type=jnp.float32,
    ) + jnp.einsum(
        "chqw,qwv->chv",
        other_rows,
        lax.dynamic_slice_in_dim(inverse_table, other_start, cell_half, 1),
        preferred_element_type=jnp.float32,
    )
    filtered_fields = (result * norm_scale).astype(jnp.bfloat16)
    outgoing = (
        filtered_fields.reshape(group_width, tiles, tile_rows, cell_half)
        .transpose(1, 0, 2, 3)
        .reshape(tiles, -1)
    )
    rows_back = exchange_chunks(outgoing, 1).reshape(channels, tile_rows, cell_half)
    summed = (feature_half.astype(jnp.float32) + rows_back.astype(jnp.float32)).astype(
        jnp.bfloat16
    )
    kept = lax.dynamic_slice_in_dim(summed, section_index * half_channels, half_channels, 0)
    sent = lax.dynamic_slice_in_dim(
        summed, (1 - section_index) * half_channels, half_channels, 0
    )
    received = lax.ppermute(sent, "section", swap)
    return jnp.where(
        section_index == 0,
        jnp.concatenate([kept, received], axis=2),
        jnp.concatenate([received, kept], axis=2),
    )


def solution(mesh):
    return jax.shard_map(
        local,
        mesh=mesh,
        in_specs=(
            P("tile", None, None),
            P(),
            P(),
            P(),
            P(),
            P(),
            P(),
            P(),
            P("tile", None, None, None),
        ),
        out_specs=P("section", "tile", None),
        check_vma=False,
    )
```

```python
import math

import jax
import jax.numpy as jnp
from jax import lax
from jax.experimental import pallas as pl
from jax.experimental.pallas import tpu as pltpu
from jax.sharding import PartitionSpec as P

EPSILON = 1e-05
MESH_ID = pl.DeviceIdType.MESH


def start_exchange(x_ref, o_ref, send_sem, recv_sem, own_sem):
    count = x_ref.shape[0]
    me = lax.axis_index("tile")
    section = lax.axis_index("section")
    barrier = pltpu.get_barrier_semaphore()

    def greet(step, carry):
        peer = lax.rem(me + step, count)
        pl.semaphore_signal(barrier, 1, device_id=(section, peer), device_id_type=MESH_ID)
        return carry

    lax.fori_loop(1, count, greet, 0)
    pl.semaphore_wait(barrier, count - 1)
    own = pltpu.make_async_copy(x_ref.at[pl.ds(me, 1)], o_ref.at[pl.ds(me, 1)], own_sem)
    own.start()

    def send(step, carry):
        peer = lax.rem(me + step, count)
        pltpu.make_async_remote_copy(
            src_ref=x_ref.at[pl.ds(peer, 1)],
            dst_ref=o_ref.at[pl.ds(me, 1)],
            send_sem=send_sem,
            recv_sem=recv_sem,
            device_id=(section, peer),
            device_id_type=MESH_ID,
        ).start()
        return carry

    lax.fori_loop(1, count, send, 0)
    every = pltpu.make_async_remote_copy(
        src_ref=x_ref.at[pl.ds(0, count - 1)],
        dst_ref=o_ref.at[pl.ds(0, count - 1)],
        send_sem=send_sem,
        recv_sem=recv_sem,
        device_id=(section, lax.rem(me + 1, count)),
        device_id_type=MESH_ID,
    )
    return every, own


def finish_exchange(every, own):
    every.wait_send()
    every.wait_recv()
    own.wait()


def exchange_kernel(x_ref, o_ref, send_sem, recv_sem, own_sem):
    finish_exchange(*start_exchange(x_ref, o_ref, send_sem, recv_sem, own_sem))


def exchange_tables_kernel(x_ref, o_ref, cos_ref, sin_ref, send_sem, recv_sem, own_sem):
    pending = start_exchange(x_ref, o_ref, send_sem, recv_sem, own_sem)
    length = cos_ref.shape[0]
    block = 16

    def rows(index, carry):
        first = pl.multiple_of(index * block, block)
        row = lax.broadcasted_iota(jnp.int32, (block, length), 0) + first
        col = lax.broadcasted_iota(jnp.int32, (block, length), 1)
        angles = lax.rem(row * col, length).astype(jnp.float32) * (2.0 * math.pi / length)
        cos_ref[pl.ds(first, block), :] = jnp.cos(angles).astype(cos_ref.dtype)
        sin_ref[pl.ds(first, block), :] = jnp.sin(angles).astype(sin_ref.dtype)
        return carry

    lax.fori_loop(0, length // block, rows, 0)
    finish_exchange(*pending)


def exchange(chunks, collective_id):
    return pl.pallas_call(
        exchange_kernel,
        out_shape=jax.ShapeDtypeStruct(chunks.shape, chunks.dtype),
        in_specs=[pl.BlockSpec(memory_space=pl.ANY)],
        out_specs=pl.BlockSpec(memory_space=pl.ANY),
        scratch_shapes=[pltpu.SemaphoreType.DMA(())] * 3,
        compiler_params=pltpu.CompilerParams(collective_id=collective_id, has_side_effects=True),
    )(chunks)


def exchange_with_tables(chunks, collective_id, length):
    table = jax.ShapeDtypeStruct((length, length), jnp.bfloat16)
    return pl.pallas_call(
        exchange_tables_kernel,
        out_shape=(jax.ShapeDtypeStruct(chunks.shape, chunks.dtype), table, table),
        in_specs=[pl.BlockSpec(memory_space=pl.ANY)],
        out_specs=(
            pl.BlockSpec(memory_space=pl.ANY),
            pl.BlockSpec(memory_space=pltpu.VMEM),
            pl.BlockSpec(memory_space=pltpu.VMEM),
        ),
        scratch_shapes=[pltpu.SemaphoreType.DMA(())] * 3,
        compiler_params=pltpu.CompilerParams(collective_id=collective_id, has_side_effects=True),
    )(chunks)


def pad_chunks(chunks):
    count, length = chunks.shape
    padded = -(-length // 2048) * 2048
    slabs = jnp.pad(chunks, ((0, 0), (0, padded - length)))
    return slabs.reshape(count, padded // 128, 128), length


def unpad_chunks(slabs, length):
    return slabs.reshape(slabs.shape[0], -1)[:, :length]


def exchange_chunks(chunks, collective_id):
    count, length = chunks.shape
    padded = -(-length // 2048) * 2048
    slabs = jnp.pad(chunks, ((0, 0), (0, padded - length))).reshape(count, padded // 128, 128)
    return exchange(slabs, collective_id).reshape(count, padded)[:, :length]


def from_behind(block, axis, distance):
    devices = range(lax.axis_size(axis))
    route = [(i - distance, i) for i in devices if i - distance in devices]
    return lax.ppermute(block, axis, route)


def fourier_tables(length):
    indices = jnp.arange(length, dtype=jnp.int32)
    product = indices[:, None] * indices[None, :] % length
    angles = product.astype(jnp.float32) * (2.0 * math.pi / length)
    return (jnp.cos(angles).astype(jnp.bfloat16), jnp.sin(angles).astype(jnp.bfloat16))


def one_hot_rows(indices, width):
    return (indices[:, None] == jnp.arange(width, dtype=jnp.int32)[None, :]).astype(jnp.bfloat16)


def spread_kernel(weight_rows, row_pick, row_cell, col_cell, width, out_cols):
    picked = jnp.dot(
        one_hot_rows(row_pick, weight_rows.shape[0]), weight_rows,
        preferred_element_type=jnp.float32,
    ).astype(jnp.bfloat16)
    col = jnp.arange(out_cols, dtype=jnp.int32)
    repeat = one_hot_rows(col % width, width).T
    full = jnp.dot(picked, repeat, preferred_element_type=jnp.float32)
    mask = row_cell[:, None] == col_cell[None, :]
    return jnp.where(mask, full, 0.0).astype(jnp.bfloat16)


def patch_kernel_matrix(patch_conv_weight):
    band_count = patch_conv_weight.shape[0]
    width = patch_conv_weight.shape[3]
    row = jnp.arange(band_count * 256, dtype=jnp.int32)
    pick = (row // 256) * 16 + ((row // 16) % 4) * 4 + row % 4
    row_cell = ((row // 64) % 4) * 4 + (row // 4) % 4
    col = jnp.arange(16 * width, dtype=jnp.int32)
    col_cell = col // width
    weight_rows = patch_conv_weight.reshape(band_count * 16, width)
    return spread_kernel(weight_rows, pick, row_cell, col_cell, width, 16 * width)


def merging_kernel_matrix(merging_conv_weight):
    in_width = merging_conv_weight.shape[2]
    out_width = merging_conv_weight.shape[3]
    row = jnp.arange(16 * in_width, dtype=jnp.int32)
    pos = row // in_width
    pick = ((pos // 4) % 2 * 2 + pos % 2) * in_width + row % in_width
    row_cell = (pos // 8) * 2 + (pos // 2) % 2
    col = jnp.arange(4 * out_width, dtype=jnp.int32)
    col_cell = col // out_width
    weight_rows = merging_conv_weight.reshape(4 * in_width, out_width)
    return spread_kernel(weight_rows, pick, row_cell, col_cell, out_width, 4 * out_width)


def down_matrices(down_weight):
    nothing = jnp.zeros_like(down_weight[0, 0])
    in_width = down_weight.shape[2]
    out_width = down_weight.shape[3]

    def arrange(entries):
        return jnp.stack(
            [jnp.stack(entries[0], axis=0), jnp.stack(entries[1], axis=0)], axis=0
        ).reshape(4 * in_width, out_width)

    own_taps = arrange(
        [[down_weight[1, 1], down_weight[1, 2]], [down_weight[2, 1], down_weight[2, 2]]]
    )
    upper_taps = arrange([[nothing, nothing], [down_weight[0, 1], down_weight[0, 2]]])
    left_taps = arrange([[nothing, down_weight[1, 0]], [nothing, down_weight[2, 0]]])
    corner_taps = arrange([[nothing, nothing], [nothing, down_weight[0, 0]]])
    return (own_taps, upper_taps, left_taps, corner_taps)


def stem_layers(aerial_patch_grid, patch_conv_weight, patch_bias, merging_conv_weight, merge_bias):
    initial_layer = jnp.einsum(
        "zji,if->zjf",
        aerial_patch_grid,
        patch_kernel_matrix(patch_conv_weight),
        preferred_element_type=jnp.float32,
    )
    initial_layer = jax.nn.gelu(initial_layer + jnp.tile(patch_bias, 16), approximate=True).astype(
        jnp.bfloat16
    )
    layer_two = jnp.einsum(
        "zji,if->zjf",
        initial_layer,
        merging_kernel_matrix(merging_conv_weight),
        preferred_element_type=jnp.float32,
    )
    return jax.nn.gelu(layer_two + jnp.tile(merge_bias, 4), approximate=True).astype(jnp.bfloat16)


def down_conv(stacked, down_weight, down_bias):
    own_taps, upper_taps, left_taps, corner_taps = down_matrices(down_weight)
    summed = jnp.einsum(
        "rwk,kc->crw", stacked[1:, 1:], own_taps, preferred_element_type=jnp.float32
    )
    summed = summed + jnp.einsum(
        "rwk,kc->crw", stacked[:-1, 1:], upper_taps, preferred_element_type=jnp.float32
    )
    summed = summed + jnp.einsum(
        "rwk,kc->crw", stacked[1:, :-1], left_taps, preferred_element_type=jnp.float32
    )
    summed = summed + jnp.einsum(
        "rwk,kc->crw", stacked[:-1, :-1], corner_taps, preferred_element_type=jnp.float32
    )
    return (summed + down_bias[:, None, None]).astype(jnp.bfloat16)


def layer_norm(features, norm_gain):
    values = features.astype(jnp.float32)
    mean_value = jnp.mean(values, axis=0, keepdims=True)
    centered = values - mean_value
    variance = jnp.mean(centered * centered, axis=0, keepdims=True)
    return (norm_gain[:, None, None] * centered * lax.rsqrt(variance + EPSILON)).astype(
        jnp.bfloat16
    )


def filter_columns(row_spectrum, kernel, forward_h, inverse_h):
    spectrum = jnp.einsum(
        "puqh,chqw->cpuw", forward_h, row_spectrum, preferred_element_type=jnp.float32
    ).astype(jnp.bfloat16)
    spec_real = spectrum[:, 0].astype(jnp.float32)
    spec_imag = spectrum[:, 1].astype(jnp.float32)
    filter_real = kernel[:, 0].astype(jnp.float32)
    filter_imag = kernel[:, 1].astype(jnp.float32)
    weighted = jnp.stack(
        [
            filter_real * spec_real - filter_imag * spec_imag,
            filter_real * spec_imag + filter_imag * spec_real,
        ],
        axis=1,
    ).astype(jnp.bfloat16)
    return jnp.einsum(
        "qhpu,cpuw->chqw", inverse_h, weighted, preferred_element_type=jnp.float32
    ).astype(jnp.bfloat16)


def local(
    aerial_patch_grid,
    patch_conv_weight,
    patch_bias,
    merging_conv_weight,
    merge_bias,
    down_weight,
    down_bias,
    norm_gain,
    spectral_filter,
):
    section_index = lax.axis_index("section")
    field_cols = aerial_patch_grid.shape[1]
    channels = down_weight.shape[3]
    full_rows = spectral_filter.shape[2]
    half_channels = channels // 2
    cell_half = field_cols // 2
    tile_index = lax.axis_index("tile")
    grid = jnp.pad(aerial_patch_grid, ((0, 0), (1, 0), (0, 0)))
    own_part = lax.dynamic_slice_in_dim(grid, section_index * cell_half, cell_half + 1, 1)
    band_count = patch_conv_weight.shape[0]
    patch_halves = own_part[-1:].reshape(1, cell_half + 1, band_count, 2, -1)
    lower_half = patch_halves[:, :, :, 1].reshape(1, cell_half + 1, -1)
    lower_half = from_behind(lower_half, "tile", 1).reshape(patch_halves[:, :, :, 1:].shape)
    rim = jnp.concatenate([jnp.zeros_like(lower_half), lower_half], axis=3)
    image_part = jnp.concatenate([rim.reshape(own_part[-1:].shape), own_part], axis=0)
    layer_two = stem_layers(
        image_part, patch_conv_weight, patch_bias, merging_conv_weight, merge_bias
    )
    row_ok = (jnp.arange(layer_two.shape[0]) > 0) | (tile_index > 0)
    col_ok = (jnp.arange(layer_two.shape[1]) > 0) | (section_index > 0)
    stacked = jnp.where(row_ok[:, None, None] & col_ok[None, :, None], layer_two, 0)
    feature_half = down_conv(stacked, down_weight, down_bias)
    normed_half = layer_norm(feature_half, norm_gain)
    tiles = lax.axis_size("tile")
    group_width, tile_rows = channels // tiles, normed_half.shape[1]
    slabs, length = pad_chunks(normed_half.reshape(tiles, -1))
    slabs, cos_h, sin_h = exchange_with_tables(slabs, 0, full_rows)
    arrived = unpad_chunks(slabs, length)
    fields = (
        arrived.reshape(tiles, group_width, tile_rows, cell_half)
        .transpose(1, 0, 2, 3)
        .reshape(group_width, tiles * tile_rows, cell_half)
    )
    swap = [(0, 1), (1, 0)]
    other_fields = lax.ppermute(fields, "section", swap)

    if full_rows == field_cols:
        cos_w, sin_w = cos_h, sin_h
    else:
        cos_w, sin_w = fourier_tables(field_cols)
    cos_part = lax.dynamic_slice_in_dim(cos_w, section_index * cell_half, cell_half, 1)
    sin_part = lax.dynamic_slice_in_dim(sin_w, section_index * cell_half, cell_half, 1)
    forward_table = jnp.stack([cos_part, -sin_part], axis=1)
    inverse_table = jnp.stack([cos_part, -sin_part], axis=0)
    forward_h = jnp.stack(
        [jnp.stack([cos_h, sin_h], axis=1), jnp.stack([-sin_h, cos_h], axis=1)], axis=0
    )
    inverse_h = jnp.stack(
        [jnp.stack([cos_h, -sin_h], axis=1), jnp.stack([sin_h, cos_h], axis=1)], axis=0
    )
    norm_scale = 1.0 / (full_rows * field_cols)
    kernel_part = lax.dynamic_slice_in_dim(
        spectral_filter, section_index * cell_half, cell_half, 3
    )
    own_start = section_index * cell_half
    other_start = (1 - section_index) * cell_half
    frequency_rows = jnp.einsum(
        "chx,xqw->chqw",
        fields,
        lax.dynamic_slice_in_dim(forward_table, own_start, cell_half, 0),
        preferred_element_type=jnp.float32,
    ) + jnp.einsum(
        "chx,xqw->chqw",
        other_fields,
        lax.dynamic_slice_in_dim(forward_table, other_start, cell_half, 0),
        preferred_element_type=jnp.float32,
    )
    back_rows = filter_columns(
        frequency_rows.astype(jnp.bfloat16), kernel_part, forward_h, inverse_h
    )
    other_rows = lax.ppermute(back_rows, "section", swap)
    result = jnp.einsum(
        "chqw,qwv->chv",
        back_rows,
        lax.dynamic_slice_in_dim(inverse_table, own_start, cell_half, 1),
        preferred_element_type=jnp.float32,
    ) + jnp.einsum(
        "chqw,qwv->chv",
        other_rows,
        lax.dynamic_slice_in_dim(inverse_table, other_start, cell_half, 1),
        preferred_element_type=jnp.float32,
    )
    filtered_fields = (result * norm_scale).astype(jnp.bfloat16)
    outgoing = (
        filtered_fields.reshape(group_width, tiles, tile_rows, cell_half)
        .transpose(1, 0, 2, 3)
        .reshape(tiles, -1)
    )
    rows_back = exchange_chunks(outgoing, 1).reshape(channels, tile_rows, cell_half)
    summed = (feature_half.astype(jnp.float32) + rows_back.astype(jnp.float32)).astype(
        jnp.bfloat16
    )
    kept = lax.dynamic_slice_in_dim(summed, section_index * half_channels, half_channels, 0)
    sent = lax.dynamic_slice_in_dim(
        summed, (1 - section_index) * half_channels, half_channels, 0
    )
    received = lax.ppermute(sent, "section", swap)
    return jnp.where(
        section_index == 0,
        jnp.concatenate([kept, received], axis=2),
        jnp.concatenate([received, kept], axis=2),
    )


def solution(mesh):
    return jax.shard_map(
        local,
        mesh=mesh,
        in_specs=(
            P("tile", None, None),
            P(),
            P(),
            P(),
            P(),
            P(),
            P(),
            P(),
            P("tile", None, None, None),
        ),
        out_specs=P("section", "tile", None),
        check_vma=False,
    )
```

```python
import math

import jax
import jax.numpy as jnp
from jax import lax
from jax.experimental import pallas as pl
from jax.experimental.pallas import tpu as pltpu
from jax.sharding import PartitionSpec as P

EPSILON = 1e-05
MESH_ID = pl.DeviceIdType.MESH


def start_exchange(x_ref, o_ref, send_sem, recv_sem, own_sem):
    count = x_ref.shape[0]
    me = lax.axis_index("tile")
    section = lax.axis_index("section")
    barrier = pltpu.get_barrier_semaphore()

    def greet(step, carry):
        peer = lax.rem(me + step, count)
        pl.semaphore_signal(barrier, 1, device_id=(section, peer), device_id_type=MESH_ID)
        return carry

    lax.fori_loop(1, count, greet, 0)
    pl.semaphore_wait(barrier, count - 1)
    own = pltpu.make_async_copy(x_ref.at[pl.ds(me, 1)], o_ref.at[pl.ds(me, 1)], own_sem)
    own.start()

    def send(step, carry):
        peer = lax.rem(me + step, count)
        pltpu.make_async_remote_copy(
            src_ref=x_ref.at[pl.ds(peer, 1)],
            dst_ref=o_ref.at[pl.ds(me, 1)],
            send_sem=send_sem,
            recv_sem=recv_sem,
            device_id=(section, peer),
            device_id_type=MESH_ID,
        ).start()
        return carry

    lax.fori_loop(1, count, send, 0)
    every = pltpu.make_async_remote_copy(
        src_ref=x_ref.at[pl.ds(0, count - 1)],
        dst_ref=o_ref.at[pl.ds(0, count - 1)],
        send_sem=send_sem,
        recv_sem=recv_sem,
        device_id=(section, lax.rem(me + 1, count)),
        device_id_type=MESH_ID,
    )
    return every, own


def finish_exchange(every, own):
    every.wait_send()
    every.wait_recv()
    own.wait()


def exchange_kernel(x_ref, o_ref, send_sem, recv_sem, own_sem):
    finish_exchange(*start_exchange(x_ref, o_ref, send_sem, recv_sem, own_sem))


def exchange_tables_kernel(x_ref, o_ref, cos_ref, sin_ref, send_sem, recv_sem, own_sem):
    pending = start_exchange(x_ref, o_ref, send_sem, recv_sem, own_sem)
    length = cos_ref.shape[0]
    block = 16

    def rows(index, carry):
        first = pl.multiple_of(index * block, block)
        row = lax.broadcasted_iota(jnp.int32, (block, length), 0) + first
        col = lax.broadcasted_iota(jnp.int32, (block, length), 1)
        angles = lax.rem(row * col, length).astype(jnp.float32) * (2.0 * math.pi / length)
        cos_ref[pl.ds(first, block), :] = jnp.cos(angles).astype(cos_ref.dtype)
        sin_ref[pl.ds(first, block), :] = jnp.sin(angles).astype(sin_ref.dtype)
        return carry

    lax.fori_loop(0, length // block, rows, 0)
    finish_exchange(*pending)


def exchange(chunks, collective_id):
    return pl.pallas_call(
        exchange_kernel,
        out_shape=jax.ShapeDtypeStruct(chunks.shape, chunks.dtype),
        in_specs=[pl.BlockSpec(memory_space=pl.ANY)],
        out_specs=pl.BlockSpec(memory_space=pl.ANY),
        scratch_shapes=[pltpu.SemaphoreType.DMA(())] * 3,
        compiler_params=pltpu.CompilerParams(collective_id=collective_id, has_side_effects=True),
    )(chunks)


def exchange_with_tables(chunks, collective_id, length):
    table = jax.ShapeDtypeStruct((length, length), jnp.bfloat16)
    return pl.pallas_call(
        exchange_tables_kernel,
        out_shape=(jax.ShapeDtypeStruct(chunks.shape, chunks.dtype), table, table),
        in_specs=[pl.BlockSpec(memory_space=pl.ANY)],
        out_specs=(
            pl.BlockSpec(memory_space=pl.ANY),
            pl.BlockSpec(memory_space=pltpu.VMEM),
            pl.BlockSpec(memory_space=pltpu.VMEM),
        ),
        scratch_shapes=[pltpu.SemaphoreType.DMA(())] * 3,
        compiler_params=pltpu.CompilerParams(collective_id=collective_id, has_side_effects=True),
    )(chunks)


def pad_chunks(chunks):
    count, length = chunks.shape
    padded = -(-length // 2048) * 2048
    slabs = jnp.pad(chunks, ((0, 0), (0, padded - length)))
    return slabs.reshape(count, padded // 128, 128), length


def unpad_chunks(slabs, length):
    return slabs.reshape(slabs.shape[0], -1)[:, :length]


def exchange_chunks(chunks, collective_id):
    count, length = chunks.shape
    padded = -(-length // 2048) * 2048
    slabs = jnp.pad(chunks, ((0, 0), (0, padded - length))).reshape(count, padded // 128, 128)
    return exchange(slabs, collective_id).reshape(count, padded)[:, :length]


def from_behind(block, axis, distance):
    devices = range(lax.axis_size(axis))
    route = [(i - distance, i) for i in devices if i - distance in devices]
    return lax.ppermute(block, axis, route)


def fourier_tables(length):
    indices = jnp.arange(length, dtype=jnp.int32)
    product = indices[:, None] * indices[None, :] % length
    angles = product.astype(jnp.float32) * (2.0 * math.pi / length)
    return (jnp.cos(angles).astype(jnp.bfloat16), jnp.sin(angles).astype(jnp.bfloat16))


def one_hot_rows(indices, width):
    return (indices[:, None] == jnp.arange(width, dtype=jnp.int32)[None, :]).astype(jnp.bfloat16)


def spread_kernel(weight_rows, row_pick, row_cell, col_cell, width, out_cols):
    picked = jnp.dot(
        one_hot_rows(row_pick, weight_rows.shape[0]), weight_rows,
        preferred_element_type=jnp.float32,
    ).astype(jnp.bfloat16)
    col = jnp.arange(out_cols, dtype=jnp.int32)
    repeat = one_hot_rows(col % width, width).T
    full = jnp.dot(picked, repeat, preferred_element_type=jnp.float32)
    mask = row_cell[:, None] == col_cell[None, :]
    return jnp.where(mask, full, 0.0).astype(jnp.bfloat16)


def patch_kernel_matrix(patch_conv_weight):
    band_count = patch_conv_weight.shape[0]
    width = patch_conv_weight.shape[3]
    row = jnp.arange(band_count * 256, dtype=jnp.int32)
    pick = (row // 256) * 16 + ((row // 16) % 4) * 4 + row % 4
    row_cell = ((row // 64) % 4) * 4 + (row // 4) % 4
    col = jnp.arange(16 * width, dtype=jnp.int32)
    col_cell = col // width
    weight_rows = patch_conv_weight.reshape(band_count * 16, width)
    return spread_kernel(weight_rows, pick, row_cell, col_cell, width, 16 * width)


def merging_kernel_matrix(merging_conv_weight):
    in_width = merging_conv_weight.shape[2]
    out_width = merging_conv_weight.shape[3]
    row = jnp.arange(16 * in_width, dtype=jnp.int32)
    pos = row // in_width
    pick = ((pos // 4) % 2 * 2 + pos % 2) * in_width + row % in_width
    row_cell = (pos // 8) * 2 + (pos // 2) % 2
    col = jnp.arange(4 * out_width, dtype=jnp.int32)
    col_cell = col // out_width
    weight_rows = merging_conv_weight.reshape(4 * in_width, out_width)
    return spread_kernel(weight_rows, pick, row_cell, col_cell, out_width, 4 * out_width)


def down_matrices(down_weight):
    nothing = jnp.zeros_like(down_weight[0, 0])
    in_width = down_weight.shape[2]
    out_width = down_weight.shape[3]

    def arrange(entries):
        return jnp.stack(
            [jnp.stack(entries[0], axis=0), jnp.stack(entries[1], axis=0)], axis=0
        ).reshape(4 * in_width, out_width)

    own_taps = arrange(
        [[down_weight[1, 1], down_weight[1, 2]], [down_weight[2, 1], down_weight[2, 2]]]
    )
    upper_taps = arrange([[nothing, nothing], [down_weight[0, 1], down_weight[0, 2]]])
    left_taps = arrange([[nothing, down_weight[1, 0]], [nothing, down_weight[2, 0]]])
    corner_taps = arrange([[nothing, nothing], [nothing, down_weight[0, 0]]])
    return (own_taps, upper_taps, left_taps, corner_taps)


def stem_layers(aerial_patch_grid, patch_matrix, patch_bias, merging_matrix, merge_bias):
    initial_layer = jnp.einsum(
        "zji,if->zjf",
        aerial_patch_grid,
        patch_matrix,
        preferred_element_type=jnp.float32,
    )
    initial_layer = jax.nn.gelu(initial_layer + jnp.tile(patch_bias, 16), approximate=True).astype(
        jnp.bfloat16
    )
    layer_two = jnp.einsum(
        "zji,if->zjf",
        initial_layer,
        merging_matrix,
        preferred_element_type=jnp.float32,
    )
    return jax.nn.gelu(layer_two + jnp.tile(merge_bias, 4), approximate=True).astype(jnp.bfloat16)


def down_conv(stacked, down_weight, down_bias):
    own_taps, upper_taps, left_taps, corner_taps = down_matrices(down_weight)
    summed = jnp.einsum(
        "rwk,kc->crw", stacked[1:, 1:], own_taps, preferred_element_type=jnp.float32
    )
    summed = summed + jnp.einsum(
        "rwk,kc->crw", stacked[:-1, 1:], upper_taps, preferred_element_type=jnp.float32
    )
    summed = summed + jnp.einsum(
        "rwk,kc->crw", stacked[1:, :-1], left_taps, preferred_element_type=jnp.float32
    )
    summed = summed + jnp.einsum(
        "rwk,kc->crw", stacked[:-1, :-1], corner_taps, preferred_element_type=jnp.float32
    )
    return (summed + down_bias[:, None, None]).astype(jnp.bfloat16)


def layer_norm(features, norm_gain):
    values = features.astype(jnp.float32)
    mean_value = jnp.mean(values, axis=0, keepdims=True)
    centered = values - mean_value
    variance = jnp.mean(centered * centered, axis=0, keepdims=True)
    return (norm_gain[:, None, None] * centered * lax.rsqrt(variance + EPSILON)).astype(
        jnp.bfloat16
    )


def filter_columns(row_spectrum, kernel, forward_h, inverse_h):
    spectrum = jnp.einsum(
        "puqh,chqw->cpuw", forward_h, row_spectrum, preferred_element_type=jnp.float32
    ).astype(jnp.bfloat16)
    spec_real = spectrum[:, 0].astype(jnp.float32)
    spec_imag = spectrum[:, 1].astype(jnp.float32)
    filter_real = kernel[:, 0].astype(jnp.float32)
    filter_imag = kernel[:, 1].astype(jnp.float32)
    weighted = jnp.stack(
        [
            filter_real * spec_real - filter_imag * spec_imag,
            filter_real * spec_imag + filter_imag * spec_real,
        ],
        axis=1,
    ).astype(jnp.bfloat16)
    return jnp.einsum(
        "qhpu,cpuw->chqw", inverse_h, weighted, preferred_element_type=jnp.float32
    ).astype(jnp.bfloat16)


def local(
    aerial_patch_grid,
    patch_conv_weight,
    patch_bias,
    merging_conv_weight,
    merge_bias,
    down_weight,
    down_bias,
    norm_gain,
    spectral_filter,
):
    section_index = lax.axis_index("section")
    field_cols = aerial_patch_grid.shape[1]
    channels = down_weight.shape[3]
    full_rows = spectral_filter.shape[2]
    half_channels = channels // 2
    cell_half = field_cols // 2
    tile_index = lax.axis_index("tile")
    grid = jnp.pad(aerial_patch_grid, ((0, 0), (1, 0), (0, 0)))
    own_part = lax.dynamic_slice_in_dim(grid, section_index * cell_half, cell_half + 1, 1)
    patch_matrix = patch_kernel_matrix(patch_conv_weight)
    merging_matrix = merging_kernel_matrix(merging_conv_weight)
    own_two = stem_layers(own_part, patch_matrix, patch_bias, merging_matrix, merge_bias)
    last_row, own_two = lax.optimization_barrier((own_part[-1:], own_two))
    rim_two = stem_layers(
        from_behind(last_row, "tile", 1), patch_matrix, patch_bias, merging_matrix, merge_bias
    )
    layer_two = jnp.concatenate([rim_two, own_two], axis=0)
    row_ok = (jnp.arange(layer_two.shape[0]) > 0) | (tile_index > 0)
    col_ok = (jnp.arange(layer_two.shape[1]) > 0) | (section_index > 0)
    stacked = jnp.where(row_ok[:, None, None] & col_ok[None, :, None], layer_two, 0)
    feature_half = down_conv(stacked, down_weight, down_bias)
    normed_half = layer_norm(feature_half, norm_gain)
    tiles = lax.axis_size("tile")
    group_width, tile_rows = channels // tiles, normed_half.shape[1]
    slabs, length = pad_chunks(normed_half.reshape(tiles, -1))
    slabs, cos_h, sin_h = exchange_with_tables(slabs, 0, full_rows)
    arrived = unpad_chunks(slabs, length)
    fields = (
        arrived.reshape(tiles, group_width, tile_rows, cell_half)
        .transpose(1, 0, 2, 3)
        .reshape(group_width, tiles * tile_rows, cell_half)
    )
    swap = [(0, 1), (1, 0)]
    other_fields = lax.ppermute(fields, "section", swap)

    if full_rows == field_cols:
        cos_w, sin_w = cos_h, sin_h
    else:
        cos_w, sin_w = fourier_tables(field_cols)
    cos_part = lax.dynamic_slice_in_dim(cos_w, section_index * cell_half, cell_half, 1)
    sin_part = lax.dynamic_slice_in_dim(sin_w, section_index * cell_half, cell_half, 1)
    forward_table = jnp.stack([cos_part, -sin_part], axis=1)
    inverse_table = jnp.stack([cos_part, -sin_part], axis=0)
    forward_h = jnp.stack(
        [jnp.stack([cos_h, sin_h], axis=1), jnp.stack([-sin_h, cos_h], axis=1)], axis=0
    )
    inverse_h = jnp.stack(
        [jnp.stack([cos_h, -sin_h], axis=1), jnp.stack([sin_h, cos_h], axis=1)], axis=0
    )
    norm_scale = 1.0 / (full_rows * field_cols)
    kernel_part = lax.dynamic_slice_in_dim(
        spectral_filter, section_index * cell_half, cell_half, 3
    )
    own_start = section_index * cell_half
    other_start = (1 - section_index) * cell_half
    frequency_rows = jnp.einsum(
        "chx,xqw->chqw",
        fields,
        lax.dynamic_slice_in_dim(forward_table, own_start, cell_half, 0),
        preferred_element_type=jnp.float32,
    ) + jnp.einsum(
        "chx,xqw->chqw",
        other_fields,
        lax.dynamic_slice_in_dim(forward_table, other_start, cell_half, 0),
        preferred_element_type=jnp.float32,
    )
    back_rows = filter_columns(
        frequency_rows.astype(jnp.bfloat16), kernel_part, forward_h, inverse_h
    )
    other_rows = lax.ppermute(back_rows, "section", swap)
    result = jnp.einsum(
        "chqw,qwv->chv",
        back_rows,
        lax.dynamic_slice_in_dim(inverse_table, own_start, cell_half, 1),
        preferred_element_type=jnp.float32,
    ) + jnp.einsum(
        "chqw,qwv->chv",
        other_rows,
        lax.dynamic_slice_in_dim(inverse_table, other_start, cell_half, 1),
        preferred_element_type=jnp.float32,
    )
    filtered_fields = (result * norm_scale).astype(jnp.bfloat16)
    outgoing = (
        filtered_fields.reshape(group_width, tiles, tile_rows, cell_half)
        .transpose(1, 0, 2, 3)
        .reshape(tiles, -1)
    )
    rows_back = exchange_chunks(outgoing, 1).reshape(channels, tile_rows, cell_half)
    summed = (feature_half.astype(jnp.float32) + rows_back.astype(jnp.float32)).astype(
        jnp.bfloat16
    )
    kept = lax.dynamic_slice_in_dim(summed, section_index * half_channels, half_channels, 0)
    sent = lax.dynamic_slice_in_dim(
        summed, (1 - section_index) * half_channels, half_channels, 0
    )
    received = lax.ppermute(sent, "section", swap)
    return jnp.where(
        section_index == 0,
        jnp.concatenate([kept, received], axis=2),
        jnp.concatenate([received, kept], axis=2),
    )


def solution(mesh):
    return jax.shard_map(
        local,
        mesh=mesh,
        in_specs=(
            P("tile", None, None),
            P(),
            P(),
            P(),
            P(),
            P(),
            P(),
            P(),
            P("tile", None, None, None),
        ),
        out_specs=P("section", "tile", None),
        check_vma=False,
    )
```

```python
import math

import jax
import jax.numpy as jnp
from jax import lax
from jax.experimental import pallas as pl
from jax.experimental.pallas import tpu as pltpu
from jax.sharding import PartitionSpec as P

EPSILON = 1e-05
MESH_ID = pl.DeviceIdType.MESH


def start_exchange(x_ref, o_ref, send_sem, recv_sem, own_sem):
    count = x_ref.shape[0]
    me = lax.axis_index("tile")
    section = lax.axis_index("section")
    barrier = pltpu.get_barrier_semaphore()

    def greet(step, carry):
        peer = lax.rem(me + step, count)
        pl.semaphore_signal(barrier, 1, device_id=(section, peer), device_id_type=MESH_ID)
        return carry

    lax.fori_loop(1, count, greet, 0)
    pl.semaphore_wait(barrier, count - 1)
    own = pltpu.make_async_copy(x_ref.at[pl.ds(me, 1)], o_ref.at[pl.ds(me, 1)], own_sem)
    own.start()

    def send(step, carry):
        peer = lax.rem(me + step, count)
        pltpu.make_async_remote_copy(
            src_ref=x_ref.at[pl.ds(peer, 1)],
            dst_ref=o_ref.at[pl.ds(me, 1)],
            send_sem=send_sem,
            recv_sem=recv_sem,
            device_id=(section, peer),
            device_id_type=MESH_ID,
        ).start()
        return carry

    lax.fori_loop(1, count, send, 0)
    every = pltpu.make_async_remote_copy(
        src_ref=x_ref.at[pl.ds(0, count - 1)],
        dst_ref=o_ref.at[pl.ds(0, count - 1)],
        send_sem=send_sem,
        recv_sem=recv_sem,
        device_id=(section, lax.rem(me + 1, count)),
        device_id_type=MESH_ID,
    )
    return every, own


def finish_exchange(every, own):
    every.wait_send()
    every.wait_recv()
    own.wait()


def exchange_kernel(x_ref, o_ref, send_sem, recv_sem, own_sem):
    finish_exchange(*start_exchange(x_ref, o_ref, send_sem, recv_sem, own_sem))


def exchange_tables_kernel(x_ref, o_ref, cos_ref, sin_ref, send_sem, recv_sem, own_sem):
    pending = start_exchange(x_ref, o_ref, send_sem, recv_sem, own_sem)
    length = cos_ref.shape[0]
    block = 16

    def rows(index, carry):
        first = pl.multiple_of(index * block, block)
        row = lax.broadcasted_iota(jnp.int32, (block, length), 0) + first
        col = lax.broadcasted_iota(jnp.int32, (block, length), 1)
        angles = lax.rem(row * col, length).astype(jnp.float32) * (2.0 * math.pi / length)
        cos_ref[pl.ds(first, block), :] = jnp.cos(angles).astype(cos_ref.dtype)
        sin_ref[pl.ds(first, block), :] = jnp.sin(angles).astype(sin_ref.dtype)
        return carry

    lax.fori_loop(0, length // block, rows, 0)
    finish_exchange(*pending)


def exchange(chunks, collective_id):
    return pl.pallas_call(
        exchange_kernel,
        out_shape=jax.ShapeDtypeStruct(chunks.shape, chunks.dtype),
        in_specs=[pl.BlockSpec(memory_space=pl.ANY)],
        out_specs=pl.BlockSpec(memory_space=pl.ANY),
        scratch_shapes=[pltpu.SemaphoreType.DMA(())] * 3,
        compiler_params=pltpu.CompilerParams(collective_id=collective_id, has_side_effects=True),
    )(chunks)


def exchange_with_tables(chunks, collective_id, length):
    table = jax.ShapeDtypeStruct((length, length), jnp.bfloat16)
    return pl.pallas_call(
        exchange_tables_kernel,
        out_shape=(jax.ShapeDtypeStruct(chunks.shape, chunks.dtype), table, table),
        in_specs=[pl.BlockSpec(memory_space=pl.ANY)],
        out_specs=(
            pl.BlockSpec(memory_space=pl.ANY),
            pl.BlockSpec(memory_space=pltpu.VMEM),
            pl.BlockSpec(memory_space=pltpu.VMEM),
        ),
        scratch_shapes=[pltpu.SemaphoreType.DMA(())] * 3,
        compiler_params=pltpu.CompilerParams(collective_id=collective_id, has_side_effects=True),
    )(chunks)


def pad_chunks(chunks):
    count, length = chunks.shape
    padded = -(-length // 2048) * 2048
    slabs = jnp.pad(chunks, ((0, 0), (0, padded - length)))
    return slabs.reshape(count, padded // 128, 128), length


def unpad_chunks(slabs, length):
    return slabs.reshape(slabs.shape[0], -1)[:, :length]


def exchange_chunks(chunks, collective_id):
    count, length = chunks.shape
    padded = -(-length // 2048) * 2048
    slabs = jnp.pad(chunks, ((0, 0), (0, padded - length))).reshape(count, padded // 128, 128)
    return exchange(slabs, collective_id).reshape(count, padded)[:, :length]


def from_behind(block, axis, distance):
    devices = range(lax.axis_size(axis))
    route = [(i - distance, i) for i in devices if i - distance in devices]
    return lax.ppermute(block, axis, route)


def fourier_tables(length):
    indices = jnp.arange(length, dtype=jnp.int32)
    product = indices[:, None] * indices[None, :] % length
    angles = product.astype(jnp.float32) * (2.0 * math.pi / length)
    return (jnp.cos(angles).astype(jnp.bfloat16), jnp.sin(angles).astype(jnp.bfloat16))


def one_hot_rows(indices, width):
    return (indices[:, None] == jnp.arange(width, dtype=jnp.int32)[None, :]).astype(jnp.bfloat16)


def spread_kernel(weight_rows, row_pick, row_cell, col_cell, width, out_cols):
    picked = jnp.dot(
        one_hot_rows(row_pick, weight_rows.shape[0]), weight_rows,
        preferred_element_type=jnp.float32,
    ).astype(jnp.bfloat16)
    col = jnp.arange(out_cols, dtype=jnp.int32)
    repeat = one_hot_rows(col % width, width).T
    full = jnp.dot(picked, repeat, preferred_element_type=jnp.float32)
    mask = row_cell[:, None] == col_cell[None, :]
    return jnp.where(mask, full, 0.0).astype(jnp.bfloat16)


def patch_kernel_matrix(patch_conv_weight):
    band_count = patch_conv_weight.shape[0]
    width = patch_conv_weight.shape[3]
    row = jnp.arange(band_count * 128, dtype=jnp.int32)
    pixel_row = (row % 128) // 16
    pixel_col = row % 16
    pick = (row // 128) * 16 + (pixel_row % 4) * 4 + pixel_col % 4
    row_cell = (pixel_row // 4) * 4 + pixel_col // 4
    col_cell = jnp.arange(8 * width, dtype=jnp.int32) // width
    weight_rows = patch_conv_weight.reshape(band_count * 16, width)
    return spread_kernel(weight_rows, pick, row_cell, col_cell, width, 8 * width)


def merging_kernel_matrix(merging_conv_weight):
    in_width = merging_conv_weight.shape[2]
    out_width = merging_conv_weight.shape[3]
    row = jnp.arange(8 * in_width, dtype=jnp.int32)
    cell = row // in_width
    pick = ((cell // 4) * 2 + cell % 2) * in_width + row % in_width
    row_cell = (cell % 4) // 2
    col_cell = jnp.arange(2 * out_width, dtype=jnp.int32) // out_width
    weight_rows = merging_conv_weight.reshape(4 * in_width, out_width)
    return spread_kernel(weight_rows, pick, row_cell, col_cell, out_width, 2 * out_width)


def down_matrices(down_weight):
    nothing = jnp.zeros_like(down_weight[0, 0])
    in_width = down_weight.shape[2]
    out_width = down_weight.shape[3]

    def arrange(entries):
        return jnp.stack(
            [jnp.stack(entries[0], axis=0), jnp.stack(entries[1], axis=0)], axis=0
        ).reshape(4 * in_width, out_width)

    own_taps = arrange(
        [[down_weight[1, 1], down_weight[1, 2]], [down_weight[2, 1], down_weight[2, 2]]]
    )
    upper_taps = arrange([[nothing, nothing], [down_weight[0, 1], down_weight[0, 2]]])
    left_taps = arrange([[nothing, down_weight[1, 0]], [nothing, down_weight[2, 0]]])
    corner_taps = arrange([[nothing, nothing], [nothing, down_weight[0, 0]]])
    return (own_taps, upper_taps, left_taps, corner_taps)


def stem_layers(aerial_patch_grid, patch_conv_weight, patch_bias, merging_conv_weight, merge_bias):
    band_count = patch_conv_weight.shape[0]
    patch_matrix = patch_kernel_matrix(patch_conv_weight)
    merging_matrix = merging_kernel_matrix(merging_conv_weight)
    halves = []
    for half in range(2):
        pixels = jnp.concatenate(
            [
                aerial_patch_grid[..., band * 256 + half * 128 : band * 256 + half * 128 + 128]
                for band in range(band_count)
            ],
            axis=-1,
        )
        initial_layer = jnp.einsum(
            "zji,if->zjf", pixels, patch_matrix, preferred_element_type=jnp.float32
        )
        initial_layer = jax.nn.gelu(
            initial_layer + jnp.tile(patch_bias, 8), approximate=True
        ).astype(jnp.bfloat16)
        layer_two = jnp.einsum(
            "zji,if->zjf", initial_layer, merging_matrix, preferred_element_type=jnp.float32
        )
        halves.append(
            jax.nn.gelu(layer_two + jnp.tile(merge_bias, 2), approximate=True).astype(jnp.bfloat16)
        )
    return jnp.concatenate(halves, axis=-1)


def down_conv(stacked, down_weight, down_bias):
    own_taps, upper_taps, left_taps, corner_taps = down_matrices(down_weight)
    summed = jnp.einsum(
        "rwk,kc->crw", stacked[1:, 1:], own_taps, preferred_element_type=jnp.float32
    )
    summed = summed + jnp.einsum(
        "rwk,kc->crw", stacked[:-1, 1:], upper_taps, preferred_element_type=jnp.float32
    )
    summed = summed + jnp.einsum(
        "rwk,kc->crw", stacked[1:, :-1], left_taps, preferred_element_type=jnp.float32
    )
    summed = summed + jnp.einsum(
        "rwk,kc->crw", stacked[:-1, :-1], corner_taps, preferred_element_type=jnp.float32
    )
    return (summed + down_bias[:, None, None]).astype(jnp.bfloat16)


def layer_norm(features, norm_gain):
    values = features.astype(jnp.float32)
    mean_value = jnp.mean(values, axis=0, keepdims=True)
    centered = values - mean_value
    variance = jnp.mean(centered * centered, axis=0, keepdims=True)
    return (norm_gain[:, None, None] * centered * lax.rsqrt(variance + EPSILON)).astype(
        jnp.bfloat16
    )


def filter_columns(row_spectrum, kernel, forward_h, inverse_h):
    spectrum = jnp.einsum(
        "puqh,chqw->cpuw", forward_h, row_spectrum, preferred_element_type=jnp.float32
    ).astype(jnp.bfloat16)
    spec_real = spectrum[:, 0].astype(jnp.float32)
    spec_imag = spectrum[:, 1].astype(jnp.float32)
    filter_real = kernel[:, 0].astype(jnp.float32)
    filter_imag = kernel[:, 1].astype(jnp.float32)
    weighted = jnp.stack(
        [
            filter_real * spec_real - filter_imag * spec_imag,
            filter_real * spec_imag + filter_imag * spec_real,
        ],
        axis=1,
    ).astype(jnp.bfloat16)
    return jnp.einsum(
        "qhpu,cpuw->chqw", inverse_h, weighted, preferred_element_type=jnp.float32
    ).astype(jnp.bfloat16)


def local(
    aerial_patch_grid,
    patch_conv_weight,
    patch_bias,
    merging_conv_weight,
    merge_bias,
    down_weight,
    down_bias,
    norm_gain,
    spectral_filter,
):
    section_index = lax.axis_index("section")
    field_cols = aerial_patch_grid.shape[1]
    channels = down_weight.shape[3]
    full_rows = spectral_filter.shape[2]
    half_channels = channels // 2
    cell_half = field_cols // 2
    tile_index = lax.axis_index("tile")
    grid = jnp.pad(aerial_patch_grid, ((0, 0), (1, 0), (0, 0)))
    own_part = lax.dynamic_slice_in_dim(grid, section_index * cell_half, cell_half + 1, 1)
    image_part = jnp.concatenate([from_behind(own_part[-1:], "tile", 1), own_part], axis=0)
    layer_two = stem_layers(
        image_part, patch_conv_weight, patch_bias, merging_conv_weight, merge_bias
    )
    row_ok = (jnp.arange(layer_two.shape[0]) > 0) | (tile_index > 0)
    col_ok = (jnp.arange(layer_two.shape[1]) > 0) | (section_index > 0)
    stacked = jnp.where(row_ok[:, None, None] & col_ok[None, :, None], layer_two, 0)
    feature_half = down_conv(stacked, down_weight, down_bias)
    normed_half = layer_norm(feature_half, norm_gain)
    tiles = lax.axis_size("tile")
    group_width, tile_rows = channels // tiles, normed_half.shape[1]
    slabs, length = pad_chunks(normed_half.reshape(tiles, -1))
    slabs, cos_h, sin_h = exchange_with_tables(slabs, 0, full_rows)
    arrived = unpad_chunks(slabs, length)
    fields = (
        arrived.reshape(tiles, group_width, tile_rows, cell_half)
        .transpose(1, 0, 2, 3)
        .reshape(group_width, tiles * tile_rows, cell_half)
    )
    swap = [(0, 1), (1, 0)]
    other_fields = lax.ppermute(fields, "section", swap)

    if full_rows == field_cols:
        cos_w, sin_w = cos_h, sin_h
    else:
        cos_w, sin_w = fourier_tables(field_cols)
    cos_part = lax.dynamic_slice_in_dim(cos_w, section_index * cell_half, cell_half, 1)
    sin_part = lax.dynamic_slice_in_dim(sin_w, section_index * cell_half, cell_half, 1)
    forward_table = jnp.stack([cos_part, -sin_part], axis=1)
    inverse_table = jnp.stack([cos_part, -sin_part], axis=0)
    forward_h = jnp.stack(
        [jnp.stack([cos_h, sin_h], axis=1), jnp.stack([-sin_h, cos_h], axis=1)], axis=0
    )
    inverse_h = jnp.stack(
        [jnp.stack([cos_h, -sin_h], axis=1), jnp.stack([sin_h, cos_h], axis=1)], axis=0
    )
    norm_scale = 1.0 / (full_rows * field_cols)
    kernel_part = lax.dynamic_slice_in_dim(
        spectral_filter, section_index * cell_half, cell_half, 3
    )
    own_start = section_index * cell_half
    other_start = (1 - section_index) * cell_half
    frequency_rows = jnp.einsum(
        "chx,xqw->chqw",
        fields,
        lax.dynamic_slice_in_dim(forward_table, own_start, cell_half, 0),
        preferred_element_type=jnp.float32,
    ) + jnp.einsum(
        "chx,xqw->chqw",
        other_fields,
        lax.dynamic_slice_in_dim(forward_table, other_start, cell_half, 0),
        preferred_element_type=jnp.float32,
    )
    back_rows = filter_columns(
        frequency_rows.astype(jnp.bfloat16), kernel_part, forward_h, inverse_h
    )
    other_rows = lax.ppermute(back_rows, "section", swap)
    result = jnp.einsum(
        "chqw,qwv->chv",
        back_rows,
        lax.dynamic_slice_in_dim(inverse_table, own_start, cell_half, 1),
        preferred_element_type=jnp.float32,
    ) + jnp.einsum(
        "chqw,qwv->chv",
        other_rows,
        lax.dynamic_slice_in_dim(inverse_table, other_start, cell_half, 1),
        preferred_element_type=jnp.float32,
    )
    filtered_fields = (result * norm_scale).astype(jnp.bfloat16)
    outgoing = (
        filtered_fields.reshape(group_width, tiles, tile_rows, cell_half)
        .transpose(1, 0, 2, 3)
        .reshape(tiles, -1)
    )
    rows_back = exchange_chunks(outgoing, 1).reshape(channels, tile_rows, cell_half)
    summed = (feature_half.astype(jnp.float32) + rows_back.astype(jnp.float32)).astype(
        jnp.bfloat16
    )
    kept = lax.dynamic_slice_in_dim(summed, section_index * half_channels, half_channels, 0)
    sent = lax.dynamic_slice_in_dim(
        summed, (1 - section_index) * half_channels, half_channels, 0
    )
    received = lax.ppermute(sent, "section", swap)
    return jnp.where(
        section_index == 0,
        jnp.concatenate([kept, received], axis=2),
        jnp.concatenate([received, kept], axis=2),
    )


def solution(mesh):
    return jax.shard_map(
        local,
        mesh=mesh,
        in_specs=(
            P("tile", None, None),
            P(),
            P(),
            P(),
            P(),
            P(),
            P(),
            P(),
            P("tile", None, None, None),
        ),
        out_specs=P("section", "tile", None),
        check_vma=False,
    )
```

```python
import math

import jax
import jax.numpy as jnp
from jax import lax
from jax.experimental import pallas as pl
from jax.experimental.pallas import tpu as pltpu
from jax.sharding import PartitionSpec as P

EPSILON = 1e-05
MESH_ID = pl.DeviceIdType.MESH


def start_exchange(x_ref, o_ref, send_sem, recv_sem, own_sem):
    count = x_ref.shape[0]
    me = lax.axis_index("tile")
    section = lax.axis_index("section")
    barrier = pltpu.get_barrier_semaphore()

    def greet(step, carry):
        peer = lax.rem(me + step, count)
        pl.semaphore_signal(barrier, 1, device_id=(section, peer), device_id_type=MESH_ID)
        return carry

    lax.fori_loop(1, count, greet, 0)
    pl.semaphore_wait(barrier, count - 1)
    own = pltpu.make_async_copy(x_ref.at[pl.ds(me, 1)], o_ref.at[pl.ds(me, 1)], own_sem)
    own.start()

    def send(step, carry):
        peer = lax.rem(me + step, count)
        pltpu.make_async_remote_copy(
            src_ref=x_ref.at[pl.ds(peer, 1)],
            dst_ref=o_ref.at[pl.ds(me, 1)],
            send_sem=send_sem,
            recv_sem=recv_sem,
            device_id=(section, peer),
            device_id_type=MESH_ID,
        ).start()
        return carry

    lax.fori_loop(1, count, send, 0)
    every = pltpu.make_async_remote_copy(
        src_ref=x_ref.at[pl.ds(0, count - 1)],
        dst_ref=o_ref.at[pl.ds(0, count - 1)],
        send_sem=send_sem,
        recv_sem=recv_sem,
        device_id=(section, lax.rem(me + 1, count)),
        device_id_type=MESH_ID,
    )
    return every, own


def finish_exchange(every, own):
    every.wait_send()
    every.wait_recv()
    own.wait()


def exchange_kernel(x_ref, o_ref, send_sem, recv_sem, own_sem):
    finish_exchange(*start_exchange(x_ref, o_ref, send_sem, recv_sem, own_sem))


def exchange_tables_kernel(
    x_ref, filter_ref, o_ref, cos_ref, sin_ref, part_ref, send_sem, recv_sem, own_sem
):
    pending = start_exchange(x_ref, o_ref, send_sem, recv_sem, own_sem)
    section = lax.axis_index("section")
    width = part_ref.shape[1]
    step = 64

    for half in range(filter_ref.shape[1] // width):

        @pl.when(section == half)
        def _():
            def move(index, carry):
                first = pl.multiple_of(index * step, step)
                part_ref[pl.ds(first, step), :] = filter_ref[
                    pl.ds(first, step), half * width : (half + 1) * width
                ]
                return carry

            lax.fori_loop(0, part_ref.shape[0] // step, move, 0)

    length = cos_ref.shape[0]
    block = 16

    def rows(index, carry):
        first = pl.multiple_of(index * block, block)
        row = lax.broadcasted_iota(jnp.int32, (block, length), 0) + first
        col = lax.broadcasted_iota(jnp.int32, (block, length), 1)
        angles = lax.rem(row * col, length).astype(jnp.float32) * (2.0 * math.pi / length)
        cos_ref[pl.ds(first, block), :] = jnp.cos(angles).astype(cos_ref.dtype)
        sin_ref[pl.ds(first, block), :] = jnp.sin(angles).astype(sin_ref.dtype)
        return carry

    lax.fori_loop(0, length // block, rows, 0)
    finish_exchange(*pending)


def exchange(chunks, collective_id):
    return pl.pallas_call(
        exchange_kernel,
        out_shape=jax.ShapeDtypeStruct(chunks.shape, chunks.dtype),
        in_specs=[pl.BlockSpec(memory_space=pl.ANY)],
        out_specs=pl.BlockSpec(memory_space=pl.ANY),
        scratch_shapes=[pltpu.SemaphoreType.DMA(())] * 3,
        compiler_params=pltpu.CompilerParams(collective_id=collective_id, has_side_effects=True),
    )(chunks)


def exchange_with_tables(chunks, filter_rows, collective_id, length):
    table = jax.ShapeDtypeStruct((length, length), jnp.bfloat16)
    part = jax.ShapeDtypeStruct(
        (filter_rows.shape[0], filter_rows.shape[1] // 2), filter_rows.dtype
    )
    return pl.pallas_call(
        exchange_tables_kernel,
        out_shape=(jax.ShapeDtypeStruct(chunks.shape, chunks.dtype), table, table, part),
        in_specs=[pl.BlockSpec(memory_space=pl.ANY), pl.BlockSpec(memory_space=pltpu.VMEM)],
        out_specs=(
            pl.BlockSpec(memory_space=pl.ANY),
            pl.BlockSpec(memory_space=pltpu.VMEM),
            pl.BlockSpec(memory_space=pltpu.VMEM),
            pl.BlockSpec(memory_space=pltpu.VMEM),
        ),
        scratch_shapes=[pltpu.SemaphoreType.DMA(())] * 3,
        compiler_params=pltpu.CompilerParams(collective_id=collective_id, has_side_effects=True),
    )(chunks, filter_rows)


def pad_chunks(chunks):
    count, length = chunks.shape
    padded = -(-length // 2048) * 2048
    slabs = jnp.pad(chunks, ((0, 0), (0, padded - length)))
    return slabs.reshape(count, padded // 128, 128), length


def unpad_chunks(slabs, length):
    return slabs.reshape(slabs.shape[0], -1)[:, :length]


def exchange_chunks(chunks, collective_id):
    count, length = chunks.shape
    padded = -(-length // 2048) * 2048
    slabs = jnp.pad(chunks, ((0, 0), (0, padded - length))).reshape(count, padded // 128, 128)
    return exchange(slabs, collective_id).reshape(count, padded)[:, :length]


def from_behind(block, axis, distance):
    devices = range(lax.axis_size(axis))
    route = [(i - distance, i) for i in devices if i - distance in devices]
    return lax.ppermute(block, axis, route)


def fourier_tables(length):
    indices = jnp.arange(length, dtype=jnp.int32)
    product = indices[:, None] * indices[None, :] % length
    angles = product.astype(jnp.float32) * (2.0 * math.pi / length)
    return (jnp.cos(angles).astype(jnp.bfloat16), jnp.sin(angles).astype(jnp.bfloat16))


def one_hot_rows(indices, width):
    return (indices[:, None] == jnp.arange(width, dtype=jnp.int32)[None, :]).astype(jnp.bfloat16)


def spread_kernel(weight_rows, row_pick, row_cell, col_cell, width, out_cols):
    picked = jnp.dot(
        one_hot_rows(row_pick, weight_rows.shape[0]), weight_rows,
        preferred_element_type=jnp.float32,
    ).astype(jnp.bfloat16)
    col = jnp.arange(out_cols, dtype=jnp.int32)
    repeat = one_hot_rows(col % width, width).T
    full = jnp.dot(picked, repeat, preferred_element_type=jnp.float32)
    mask = row_cell[:, None] == col_cell[None, :]
    return jnp.where(mask, full, 0.0).astype(jnp.bfloat16)


def patch_kernel_matrix(patch_conv_weight):
    band_count = patch_conv_weight.shape[0]
    width = patch_conv_weight.shape[3]
    row = jnp.arange(band_count * 128, dtype=jnp.int32)
    pixel_row = (row % 128) // 16
    pixel_col = row % 16
    pick = (row // 128) * 16 + (pixel_row % 4) * 4 + pixel_col % 4
    row_cell = (pixel_row // 4) * 4 + pixel_col // 4
    col_cell = jnp.arange(8 * width, dtype=jnp.int32) // width
    weight_rows = patch_conv_weight.reshape(band_count * 16, width)
    return spread_kernel(weight_rows, pick, row_cell, col_cell, width, 8 * width)


def merging_kernel_matrix(merging_conv_weight):
    in_width = merging_conv_weight.shape[2]
    out_width = merging_conv_weight.shape[3]
    row = jnp.arange(8 * in_width, dtype=jnp.int32)
    cell = row // in_width
    pick = ((cell // 4) * 2 + cell % 2) * in_width + row % in_width
    row_cell = (cell % 4) // 2
    col_cell = jnp.arange(2 * out_width, dtype=jnp.int32) // out_width
    weight_rows = merging_conv_weight.reshape(4 * in_width, out_width)
    return spread_kernel(weight_rows, pick, row_cell, col_cell, out_width, 2 * out_width)


def down_matrices(down_weight):
    nothing = jnp.zeros_like(down_weight[0, 0])
    in_width = down_weight.shape[2]
    out_width = down_weight.shape[3]

    def arrange(entries):
        return jnp.stack(
            [jnp.stack(entries[0], axis=0), jnp.stack(entries[1], axis=0)], axis=0
        ).reshape(4 * in_width, out_width)

    own_taps = arrange(
        [[down_weight[1, 1], down_weight[1, 2]], [down_weight[2, 1], down_weight[2, 2]]]
    )
    upper_taps = arrange([[nothing, nothing], [down_weight[0, 1], down_weight[0, 2]]])
    left_taps = arrange([[nothing, down_weight[1, 0]], [nothing, down_weight[2, 0]]])
    corner_taps = arrange([[nothing, nothing], [nothing, down_weight[0, 0]]])
    return (own_taps, upper_taps, left_taps, corner_taps)


def stem_layers(aerial_patch_grid, patch_conv_weight, patch_bias, merging_conv_weight, merge_bias):
    band_count = patch_conv_weight.shape[0]
    patch_matrix = patch_kernel_matrix(patch_conv_weight)
    merging_matrix = merging_kernel_matrix(merging_conv_weight)
    halves = []
    for half in range(2):
        pixels = jnp.concatenate(
            [
                aerial_patch_grid[..., band * 256 + half * 128 : band * 256 + half * 128 + 128]
                for band in range(band_count)
            ],
            axis=-1,
        )
        initial_layer = jnp.einsum(
            "zji,if->zjf", pixels, patch_matrix, preferred_element_type=jnp.float32
        )
        initial_layer = jax.nn.gelu(
            initial_layer + jnp.tile(patch_bias, 8), approximate=True
        ).astype(jnp.bfloat16)
        layer_two = jnp.einsum(
            "zji,if->zjf", initial_layer, merging_matrix, preferred_element_type=jnp.float32
        )
        halves.append(
            jax.nn.gelu(layer_two + jnp.tile(merge_bias, 2), approximate=True).astype(jnp.bfloat16)
        )
    return jnp.concatenate(halves, axis=-1)


def down_conv(stacked, down_weight, down_bias):
    own_taps, upper_taps, left_taps, corner_taps = down_matrices(down_weight)
    summed = jnp.einsum(
        "rwk,kc->crw", stacked[1:, 1:], own_taps, preferred_element_type=jnp.float32
    )
    summed = summed + jnp.einsum(
        "rwk,kc->crw", stacked[:-1, 1:], upper_taps, preferred_element_type=jnp.float32
    )
    summed = summed + jnp.einsum(
        "rwk,kc->crw", stacked[1:, :-1], left_taps, preferred_element_type=jnp.float32
    )
    summed = summed + jnp.einsum(
        "rwk,kc->crw", stacked[:-1, :-1], corner_taps, preferred_element_type=jnp.float32
    )
    return (summed + down_bias[:, None, None]).astype(jnp.bfloat16)


def layer_norm(features, norm_gain):
    values = features.astype(jnp.float32)
    mean_value = jnp.mean(values, axis=0, keepdims=True)
    centered = values - mean_value
    variance = jnp.mean(centered * centered, axis=0, keepdims=True)
    return (norm_gain[:, None, None] * centered * lax.rsqrt(variance + EPSILON)).astype(
        jnp.bfloat16
    )


def filter_columns(row_spectrum, kernel, forward_h, inverse_h):
    spectrum = jnp.einsum(
        "puqh,chqw->cpuw", forward_h, row_spectrum, preferred_element_type=jnp.float32
    ).astype(jnp.bfloat16)
    spec_real = spectrum[:, 0].astype(jnp.float32)
    spec_imag = spectrum[:, 1].astype(jnp.float32)
    filter_real = kernel[:, 0].astype(jnp.float32)
    filter_imag = kernel[:, 1].astype(jnp.float32)
    weighted = jnp.stack(
        [
            filter_real * spec_real - filter_imag * spec_imag,
            filter_real * spec_imag + filter_imag * spec_real,
        ],
        axis=1,
    ).astype(jnp.bfloat16)
    return jnp.einsum(
        "qhpu,cpuw->chqw", inverse_h, weighted, preferred_element_type=jnp.float32
    ).astype(jnp.bfloat16)


def local(
    aerial_patch_grid,
    patch_conv_weight,
    patch_bias,
    merging_conv_weight,
    merge_bias,
    down_weight,
    down_bias,
    norm_gain,
    spectral_filter,
):
    section_index = lax.axis_index("section")
    field_cols = aerial_patch_grid.shape[1]
    channels = down_weight.shape[3]
    full_rows = spectral_filter.shape[2]
    half_channels = channels // 2
    cell_half = field_cols // 2
    tile_index = lax.axis_index("tile")
    grid = jnp.pad(aerial_patch_grid, ((0, 0), (1, 0), (0, 0)))
    own_part = lax.dynamic_slice_in_dim(grid, section_index * cell_half, cell_half + 1, 1)
    image_part = jnp.concatenate([from_behind(own_part[-1:], "tile", 1), own_part], axis=0)
    layer_two = stem_layers(
        image_part, patch_conv_weight, patch_bias, merging_conv_weight, merge_bias
    )
    row_ok = (jnp.arange(layer_two.shape[0]) > 0) | (tile_index > 0)
    col_ok = (jnp.arange(layer_two.shape[1]) > 0) | (section_index > 0)
    stacked = jnp.where(row_ok[:, None, None] & col_ok[None, :, None], layer_two, 0)
    feature_half = down_conv(stacked, down_weight, down_bias)
    normed_half = layer_norm(feature_half, norm_gain)
    tiles = lax.axis_size("tile")
    group_width, tile_rows = channels // tiles, normed_half.shape[1]
    slabs, length = pad_chunks(normed_half.reshape(tiles, -1))
    filter_rows = spectral_filter.reshape(-1, field_cols)
    slabs, cos_h, sin_h, kernel_part = exchange_with_tables(slabs, filter_rows, 0, full_rows)
    kernel_part = kernel_part.reshape(spectral_filter.shape[:3] + (cell_half,))
    arrived = unpad_chunks(slabs, length)
    fields = (
        arrived.reshape(tiles, group_width, tile_rows, cell_half)
        .transpose(1, 0, 2, 3)
        .reshape(group_width, tiles * tile_rows, cell_half)
    )
    swap = [(0, 1), (1, 0)]
    other_fields = lax.ppermute(fields, "section", swap)

    if full_rows == field_cols:
        cos_w, sin_w = cos_h, sin_h
    else:
        cos_w, sin_w = fourier_tables(field_cols)
    cos_part = lax.dynamic_slice_in_dim(cos_w, section_index * cell_half, cell_half, 1)
    sin_part = lax.dynamic_slice_in_dim(sin_w, section_index * cell_half, cell_half, 1)
    forward_table = jnp.stack([cos_part, -sin_part], axis=1)
    inverse_table = jnp.stack([cos_part, -sin_part], axis=0)
    forward_h = jnp.stack(
        [jnp.stack([cos_h, sin_h], axis=1), jnp.stack([-sin_h, cos_h], axis=1)], axis=0
    )
    inverse_h = jnp.stack(
        [jnp.stack([cos_h, -sin_h], axis=1), jnp.stack([sin_h, cos_h], axis=1)], axis=0
    )
    norm_scale = 1.0 / (full_rows * field_cols)
    own_start = section_index * cell_half
    other_start = (1 - section_index) * cell_half
    frequency_rows = jnp.einsum(
        "chx,xqw->chqw",
        fields,
        lax.dynamic_slice_in_dim(forward_table, own_start, cell_half, 0),
        preferred_element_type=jnp.float32,
    ) + jnp.einsum(
        "chx,xqw->chqw",
        other_fields,
        lax.dynamic_slice_in_dim(forward_table, other_start, cell_half, 0),
        preferred_element_type=jnp.float32,
    )
    back_rows = filter_columns(
        frequency_rows.astype(jnp.bfloat16), kernel_part, forward_h, inverse_h
    )
    other_rows = lax.ppermute(back_rows, "section", swap)
    result = jnp.einsum(
        "chqw,qwv->chv",
        back_rows,
        lax.dynamic_slice_in_dim(inverse_table, own_start, cell_half, 1),
        preferred_element_type=jnp.float32,
    ) + jnp.einsum(
        "chqw,qwv->chv",
        other_rows,
        lax.dynamic_slice_in_dim(inverse_table, other_start, cell_half, 1),
        preferred_element_type=jnp.float32,
    )
    filtered_fields = (result * norm_scale).astype(jnp.bfloat16)
    outgoing = (
        filtered_fields.reshape(group_width, tiles, tile_rows, cell_half)
        .transpose(1, 0, 2, 3)
        .reshape(tiles, -1)
    )
    rows_back = exchange_chunks(outgoing, 1).reshape(channels, tile_rows, cell_half)
    summed = (feature_half.astype(jnp.float32) + rows_back.astype(jnp.float32)).astype(
        jnp.bfloat16
    )
    kept = lax.dynamic_slice_in_dim(summed, section_index * half_channels, half_channels, 0)
    sent = lax.dynamic_slice_in_dim(
        summed, (1 - section_index) * half_channels, half_channels, 0
    )
    received = lax.ppermute(sent, "section", swap)
    return jnp.where(
        section_index == 0,
        jnp.concatenate([kept, received], axis=2),
        jnp.concatenate([received, kept], axis=2),
    )


def solution(mesh):
    return jax.shard_map(
        local,
        mesh=mesh,
        in_specs=(
            P("tile", None, None),
            P(),
            P(),
            P(),
            P(),
            P(),
            P(),
            P(),
            P("tile", None, None, None),
        ),
        out_specs=P("section", "tile", None),
        check_vma=False,
    )
```

```python
import math

import jax
import jax.numpy as jnp
from jax import lax
from jax.experimental import pallas as pl
from jax.experimental.pallas import tpu as pltpu
from jax.sharding import PartitionSpec as P

EPSILON = 1e-05
MESH_ID = pl.DeviceIdType.MESH


def start_exchange(x_ref, o_ref, send_sem, recv_sem, own_sem):
    count = x_ref.shape[0]
    me = lax.axis_index("tile")
    section = lax.axis_index("section")
    barrier = pltpu.get_barrier_semaphore()

    def greet(step, carry):
        peer = lax.rem(me + step, count)
        pl.semaphore_signal(barrier, 1, device_id=(section, peer), device_id_type=MESH_ID)
        return carry

    lax.fori_loop(1, count, greet, 0)
    pl.semaphore_wait(barrier, count - 1)
    own = pltpu.make_async_copy(x_ref.at[pl.ds(me, 1)], o_ref.at[pl.ds(me, 1)], own_sem)
    own.start()

    def send(step, carry):
        peer = lax.rem(me + step, count)
        pltpu.make_async_remote_copy(
            src_ref=x_ref.at[pl.ds(peer, 1)],
            dst_ref=o_ref.at[pl.ds(me, 1)],
            send_sem=send_sem,
            recv_sem=recv_sem,
            device_id=(section, peer),
            device_id_type=MESH_ID,
        ).start()
        return carry

    lax.fori_loop(1, count, send, 0)
    every = pltpu.make_async_remote_copy(
        src_ref=x_ref.at[pl.ds(0, count - 1)],
        dst_ref=o_ref.at[pl.ds(0, count - 1)],
        send_sem=send_sem,
        recv_sem=recv_sem,
        device_id=(section, lax.rem(me + 1, count)),
        device_id_type=MESH_ID,
    )
    return every, own


def finish_exchange(every, own):
    every.wait_send()
    every.wait_recv()
    own.wait()


def exchange_kernel(x_ref, o_ref, send_sem, recv_sem, own_sem):
    finish_exchange(*start_exchange(x_ref, o_ref, send_sem, recv_sem, own_sem))


def exchange_tables_kernel(
    x_ref,
    filter_ref,
    o_ref,
    cos_ref,
    sin_ref,
    part_ref,
    cos_part_ref,
    sin_part_ref,
    send_sem,
    recv_sem,
    own_sem,
):
    pending = start_exchange(x_ref, o_ref, send_sem, recv_sem, own_sem)
    section = lax.axis_index("section")
    width = part_ref.shape[1]
    step = 64

    for half in range(filter_ref.shape[1] // width):

        @pl.when(section == half)
        def _():
            def move(index, carry):
                first = pl.multiple_of(index * step, step)
                part_ref[pl.ds(first, step), :] = filter_ref[
                    pl.ds(first, step), half * width : (half + 1) * width
                ]
                return carry

            lax.fori_loop(0, part_ref.shape[0] // step, move, 0)

    length = cos_ref.shape[0]
    block = 16

    def rows(index, carry):
        first = pl.multiple_of(index * block, block)
        row = lax.broadcasted_iota(jnp.int32, (block, length), 0) + first
        col = lax.broadcasted_iota(jnp.int32, (block, length), 1)
        angles = lax.rem(row * col, length).astype(jnp.float32) * (2.0 * math.pi / length)
        cos_ref[pl.ds(first, block), :] = jnp.cos(angles).astype(cos_ref.dtype)
        sin_ref[pl.ds(first, block), :] = jnp.sin(angles).astype(sin_ref.dtype)
        return carry

    lax.fori_loop(0, length // block, rows, 0)
    cols, half = cos_part_ref.shape

    def part_rows(index, carry):
        first = pl.multiple_of(index * block, block)
        row = lax.broadcasted_iota(jnp.int32, (block, half), 0) + first
        col = lax.broadcasted_iota(jnp.int32, (block, half), 1) + section * half
        angles = lax.rem(row * col, cols).astype(jnp.float32) * (2.0 * math.pi / cols)
        cos_part_ref[pl.ds(first, block), :] = jnp.cos(angles).astype(cos_part_ref.dtype)
        sin_part_ref[pl.ds(first, block), :] = jnp.sin(angles).astype(sin_part_ref.dtype)
        return carry

    lax.fori_loop(0, cols // block, part_rows, 0)
    finish_exchange(*pending)


def exchange(chunks, collective_id):
    return pl.pallas_call(
        exchange_kernel,
        out_shape=jax.ShapeDtypeStruct(chunks.shape, chunks.dtype),
        in_specs=[pl.BlockSpec(memory_space=pl.ANY)],
        out_specs=pl.BlockSpec(memory_space=pl.ANY),
        scratch_shapes=[pltpu.SemaphoreType.DMA(())] * 3,
        compiler_params=pltpu.CompilerParams(collective_id=collective_id, has_side_effects=True),
    )(chunks)


def exchange_with_tables(chunks, filter_rows, collective_id, length):
    table = jax.ShapeDtypeStruct((length, length), jnp.bfloat16)
    part = jax.ShapeDtypeStruct(
        (filter_rows.shape[0], filter_rows.shape[1] // 2), filter_rows.dtype
    )
    return pl.pallas_call(
        exchange_tables_kernel,
        out_shape=(jax.ShapeDtypeStruct(chunks.shape, chunks.dtype), table, table, part)
        + (jax.ShapeDtypeStruct((filter_rows.shape[1], part.shape[1]), jnp.bfloat16),) * 2,
        in_specs=[pl.BlockSpec(memory_space=pl.ANY), pl.BlockSpec(memory_space=pltpu.VMEM)],
        out_specs=(
            pl.BlockSpec(memory_space=pl.ANY),
            pl.BlockSpec(memory_space=pltpu.VMEM),
            pl.BlockSpec(memory_space=pltpu.VMEM),
            pl.BlockSpec(memory_space=pltpu.VMEM),
            pl.BlockSpec(memory_space=pltpu.VMEM),
            pl.BlockSpec(memory_space=pltpu.VMEM),
        ),
        scratch_shapes=[pltpu.SemaphoreType.DMA(())] * 3,
        compiler_params=pltpu.CompilerParams(collective_id=collective_id, has_side_effects=True),
    )(chunks, filter_rows)


def pad_chunks(chunks):
    count, length = chunks.shape
    padded = -(-length // 2048) * 2048
    slabs = jnp.pad(chunks, ((0, 0), (0, padded - length)))
    return slabs.reshape(count, padded // 128, 128), length


def unpad_chunks(slabs, length):
    return slabs.reshape(slabs.shape[0], -1)[:, :length]


def exchange_chunks(chunks, collective_id):
    count, length = chunks.shape
    padded = -(-length // 2048) * 2048
    slabs = jnp.pad(chunks, ((0, 0), (0, padded - length))).reshape(count, padded // 128, 128)
    return exchange(slabs, collective_id).reshape(count, padded)[:, :length]


def from_behind(block, axis, distance):
    devices = range(lax.axis_size(axis))
    route = [(i - distance, i) for i in devices if i - distance in devices]
    return lax.ppermute(block, axis, route)


def fourier_tables(length):
    indices = jnp.arange(length, dtype=jnp.int32)
    product = indices[:, None] * indices[None, :] % length
    angles = product.astype(jnp.float32) * (2.0 * math.pi / length)
    return (jnp.cos(angles).astype(jnp.bfloat16), jnp.sin(angles).astype(jnp.bfloat16))


def one_hot_rows(indices, width):
    return (indices[:, None] == jnp.arange(width, dtype=jnp.int32)[None, :]).astype(jnp.bfloat16)


def spread_kernel(weight_rows, row_pick, row_cell, col_cell, width, out_cols):
    picked = jnp.dot(
        one_hot_rows(row_pick, weight_rows.shape[0]), weight_rows,
        preferred_element_type=jnp.float32,
    ).astype(jnp.bfloat16)
    col = jnp.arange(out_cols, dtype=jnp.int32)
    repeat = one_hot_rows(col % width, width).T
    full = jnp.dot(picked, repeat, preferred_element_type=jnp.float32)
    mask = row_cell[:, None] == col_cell[None, :]
    return jnp.where(mask, full, 0.0).astype(jnp.bfloat16)


def patch_kernel_matrix(patch_conv_weight):
    band_count = patch_conv_weight.shape[0]
    width = patch_conv_weight.shape[3]
    row = jnp.arange(band_count * 128, dtype=jnp.int32)
    pixel_row = (row % 128) // 16
    pixel_col = row % 16
    pick = (row // 128) * 16 + (pixel_row % 4) * 4 + pixel_col % 4
    row_cell = (pixel_row // 4) * 4 + pixel_col // 4
    col_cell = jnp.arange(8 * width, dtype=jnp.int32) // width
    weight_rows = patch_conv_weight.reshape(band_count * 16, width)
    return spread_kernel(weight_rows, pick, row_cell, col_cell, width, 8 * width)


def merging_kernel_matrix(merging_conv_weight):
    in_width = merging_conv_weight.shape[2]
    out_width = merging_conv_weight.shape[3]
    row = jnp.arange(8 * in_width, dtype=jnp.int32)
    cell = row // in_width
    pick = ((cell // 4) * 2 + cell % 2) * in_width + row % in_width
    row_cell = (cell % 4) // 2
    col_cell = jnp.arange(2 * out_width, dtype=jnp.int32) // out_width
    weight_rows = merging_conv_weight.reshape(4 * in_width, out_width)
    return spread_kernel(weight_rows, pick, row_cell, col_cell, out_width, 2 * out_width)


def down_matrices(down_weight):
    nothing = jnp.zeros_like(down_weight[0, 0])
    in_width = down_weight.shape[2]
    out_width = down_weight.shape[3]

    def arrange(entries):
        return jnp.stack(
            [jnp.stack(entries[0], axis=0), jnp.stack(entries[1], axis=0)], axis=0
        ).reshape(4 * in_width, out_width)

    own_taps = arrange(
        [[down_weight[1, 1], down_weight[1, 2]], [down_weight[2, 1], down_weight[2, 2]]]
    )
    upper_taps = arrange([[nothing, nothing], [down_weight[0, 1], down_weight[0, 2]]])
    left_taps = arrange([[nothing, down_weight[1, 0]], [nothing, down_weight[2, 0]]])
    corner_taps = arrange([[nothing, nothing], [nothing, down_weight[0, 0]]])
    return (own_taps, upper_taps, left_taps, corner_taps)


def stem_layers(aerial_patch_grid, patch_conv_weight, patch_bias, merging_conv_weight, merge_bias):
    band_count = patch_conv_weight.shape[0]
    patch_matrix = patch_kernel_matrix(patch_conv_weight)
    merging_matrix = merging_kernel_matrix(merging_conv_weight)
    halves = []
    for half in range(2):
        pixels = jnp.concatenate(
            [
                aerial_patch_grid[..., band * 256 + half * 128 : band * 256 + half * 128 + 128]
                for band in range(band_count)
            ],
            axis=-1,
        )
        initial_layer = jnp.einsum(
            "zji,if->zjf", pixels, patch_matrix, preferred_element_type=jnp.float32
        )
        initial_layer = jax.nn.gelu(
            initial_layer + jnp.tile(patch_bias, 8), approximate=True
        ).astype(jnp.bfloat16)
        layer_two = jnp.einsum(
            "zji,if->zjf", initial_layer, merging_matrix, preferred_element_type=jnp.float32
        )
        halves.append(
            jax.nn.gelu(layer_two + jnp.tile(merge_bias, 2), approximate=True).astype(jnp.bfloat16)
        )
    return jnp.concatenate(halves, axis=-1)


def down_conv(stacked, down_weight, down_bias):
    own_taps, upper_taps, left_taps, corner_taps = down_matrices(down_weight)
    summed = jnp.einsum(
        "rwk,kc->crw", stacked[1:, 1:], own_taps, preferred_element_type=jnp.float32
    )
    summed = summed + jnp.einsum(
        "rwk,kc->crw", stacked[:-1, 1:], upper_taps, preferred_element_type=jnp.float32
    )
    summed = summed + jnp.einsum(
        "rwk,kc->crw", stacked[1:, :-1], left_taps, preferred_element_type=jnp.float32
    )
    summed = summed + jnp.einsum(
        "rwk,kc->crw", stacked[:-1, :-1], corner_taps, preferred_element_type=jnp.float32
    )
    return (summed + down_bias[:, None, None]).astype(jnp.bfloat16)


def layer_norm(features, norm_gain):
    values = features.astype(jnp.float32)
    mean_value = jnp.mean(values, axis=0, keepdims=True)
    centered = values - mean_value
    variance = jnp.mean(centered * centered, axis=0, keepdims=True)
    return (norm_gain[:, None, None] * centered * lax.rsqrt(variance + EPSILON)).astype(
        jnp.bfloat16
    )


def filter_columns(row_spectrum, kernel, forward_h, inverse_h):
    spectrum = jnp.einsum(
        "puqh,chqw->cpuw", forward_h, row_spectrum, preferred_element_type=jnp.float32
    ).astype(jnp.bfloat16)
    spec_real = spectrum[:, 0].astype(jnp.float32)
    spec_imag = spectrum[:, 1].astype(jnp.float32)
    filter_real = kernel[:, 0].astype(jnp.float32)
    filter_imag = kernel[:, 1].astype(jnp.float32)
    weighted = jnp.stack(
        [
            filter_real * spec_real - filter_imag * spec_imag,
            filter_real * spec_imag + filter_imag * spec_real,
        ],
        axis=1,
    ).astype(jnp.bfloat16)
    return jnp.einsum(
        "qhpu,cpuw->chqw", inverse_h, weighted, preferred_element_type=jnp.float32
    ).astype(jnp.bfloat16)


def local(
    aerial_patch_grid,
    patch_conv_weight,
    patch_bias,
    merging_conv_weight,
    merge_bias,
    down_weight,
    down_bias,
    norm_gain,
    spectral_filter,
):
    section_index = lax.axis_index("section")
    field_cols = aerial_patch_grid.shape[1]
    channels = down_weight.shape[3]
    full_rows = spectral_filter.shape[2]
    half_channels = channels // 2
    cell_half = field_cols // 2
    tile_index = lax.axis_index("tile")
    grid = jnp.pad(aerial_patch_grid, ((0, 0), (1, 0), (0, 0)))
    own_part = lax.dynamic_slice_in_dim(grid, section_index * cell_half, cell_half + 1, 1)
    image_part = jnp.concatenate([from_behind(own_part[-1:], "tile", 1), own_part], axis=0)
    layer_two = stem_layers(
        image_part, patch_conv_weight, patch_bias, merging_conv_weight, merge_bias
    )
    row_ok = (jnp.arange(layer_two.shape[0]) > 0) | (tile_index > 0)
    col_ok = (jnp.arange(layer_two.shape[1]) > 0) | (section_index > 0)
    stacked = jnp.where(row_ok[:, None, None] & col_ok[None, :, None], layer_two, 0)
    feature_half = down_conv(stacked, down_weight, down_bias)
    normed_half = layer_norm(feature_half, norm_gain)
    tiles = lax.axis_size("tile")
    group_width, tile_rows = channels // tiles, normed_half.shape[1]
    slabs, length = pad_chunks(normed_half.reshape(tiles, -1))
    filter_rows = spectral_filter.reshape(-1, field_cols)
    slabs, cos_h, sin_h, kernel_part, cos_part, sin_part = exchange_with_tables(
        slabs, filter_rows, 0, full_rows
    )
    kernel_part = kernel_part.reshape(spectral_filter.shape[:3] + (cell_half,))
    arrived = unpad_chunks(slabs, length)
    fields = (
        arrived.reshape(tiles, group_width, tile_rows, cell_half)
        .transpose(1, 0, 2, 3)
        .reshape(group_width, tiles * tile_rows, cell_half)
    )
    swap = [(0, 1), (1, 0)]
    other_fields = lax.ppermute(fields, "section", swap)

    forward_table = jnp.stack([cos_part, -sin_part], axis=1)
    inverse_table = jnp.stack([cos_part, -sin_part], axis=0)
    forward_h = jnp.stack(
        [jnp.stack([cos_h, sin_h], axis=1), jnp.stack([-sin_h, cos_h], axis=1)], axis=0
    )
    inverse_h = jnp.stack(
        [jnp.stack([cos_h, -sin_h], axis=1), jnp.stack([sin_h, cos_h], axis=1)], axis=0
    )
    norm_scale = 1.0 / (full_rows * field_cols)
    own_start = section_index * cell_half
    other_start = (1 - section_index) * cell_half
    frequency_rows = jnp.einsum(
        "chx,xqw->chqw",
        fields,
        lax.dynamic_slice_in_dim(forward_table, own_start, cell_half, 0),
        preferred_element_type=jnp.float32,
    ) + jnp.einsum(
        "chx,xqw->chqw",
        other_fields,
        lax.dynamic_slice_in_dim(forward_table, other_start, cell_half, 0),
        preferred_element_type=jnp.float32,
    )
    back_rows = filter_columns(
        frequency_rows.astype(jnp.bfloat16), kernel_part, forward_h, inverse_h
    )
    other_rows = lax.ppermute(back_rows, "section", swap)
    result = jnp.einsum(
        "chqw,qwv->chv",
        back_rows,
        lax.dynamic_slice_in_dim(inverse_table, own_start, cell_half, 1),
        preferred_element_type=jnp.float32,
    ) + jnp.einsum(
        "chqw,qwv->chv",
        other_rows,
        lax.dynamic_slice_in_dim(inverse_table, other_start, cell_half, 1),
        preferred_element_type=jnp.float32,
    )
    filtered_fields = (result * norm_scale).astype(jnp.bfloat16)
    outgoing = (
        filtered_fields.reshape(group_width, tiles, tile_rows, cell_half)
        .transpose(1, 0, 2, 3)
        .reshape(tiles, -1)
    )
    rows_back = exchange_chunks(outgoing, 1).reshape(channels, tile_rows, cell_half)
    summed = (feature_half.astype(jnp.float32) + rows_back.astype(jnp.float32)).astype(
        jnp.bfloat16
    )
    kept = lax.dynamic_slice_in_dim(summed, section_index * half_channels, half_channels, 0)
    sent = lax.dynamic_slice_in_dim(
        summed, (1 - section_index) * half_channels, half_channels, 0
    )
    received = lax.ppermute(sent, "section", swap)
    return jnp.where(
        section_index == 0,
        jnp.concatenate([kept, received], axis=2),
        jnp.concatenate([received, kept], axis=2),
    )


def solution(mesh):
    return jax.shard_map(
        local,
        mesh=mesh,
        in_specs=(
            P("tile", None, None),
            P(),
            P(),
            P(),
            P(),
            P(),
            P(),
            P(),
            P("tile", None, None, None),
        ),
        out_specs=P("section", "tile", None),
        check_vma=False,
    )
```

```python
import math

import jax
import jax.numpy as jnp
from jax import lax
from jax.experimental import pallas as pl
from jax.experimental.pallas import tpu as pltpu
from jax.sharding import PartitionSpec as P

EPSILON = 1e-05
MESH_ID = pl.DeviceIdType.MESH


def start_exchange(x_ref, o_ref, send_sem, recv_sem, own_sem):
    count = x_ref.shape[0]
    me = lax.axis_index("tile")
    section = lax.axis_index("section")
    barrier = pltpu.get_barrier_semaphore()

    def greet(step, carry):
        peer = lax.rem(me + step, count)
        pl.semaphore_signal(barrier, 1, device_id=(section, peer), device_id_type=MESH_ID)
        return carry

    lax.fori_loop(1, count, greet, 0)
    pl.semaphore_wait(barrier, count - 1)
    own = pltpu.make_async_copy(x_ref.at[pl.ds(me, 1)], o_ref.at[pl.ds(me, 1)], own_sem)
    own.start()

    def send(step, carry):
        peer = lax.rem(me + step, count)
        pltpu.make_async_remote_copy(
            src_ref=x_ref.at[pl.ds(peer, 1)],
            dst_ref=o_ref.at[pl.ds(me, 1)],
            send_sem=send_sem,
            recv_sem=recv_sem,
            device_id=(section, peer),
            device_id_type=MESH_ID,
        ).start()
        return carry

    lax.fori_loop(1, count, send, 0)
    every = pltpu.make_async_remote_copy(
        src_ref=x_ref.at[pl.ds(0, count - 1)],
        dst_ref=o_ref.at[pl.ds(0, count - 1)],
        send_sem=send_sem,
        recv_sem=recv_sem,
        device_id=(section, lax.rem(me + 1, count)),
        device_id_type=MESH_ID,
    )
    return every, own


def finish_exchange(every, own):
    every.wait_send()
    every.wait_recv()
    own.wait()


def exchange_kernel(x_ref, o_ref, send_sem, recv_sem, own_sem):
    finish_exchange(*start_exchange(x_ref, o_ref, send_sem, recv_sem, own_sem))


def exchange_tables_kernel(
    x_ref,
    filter_ref,
    o_ref,
    cos_ref,
    sin_ref,
    negated_ref,
    part_ref,
    cos_part_ref,
    negated_part_ref,
    send_sem,
    recv_sem,
    own_sem,
):
    pending = start_exchange(x_ref, o_ref, send_sem, recv_sem, own_sem)
    section = lax.axis_index("section")
    width = part_ref.shape[1]
    step = 64

    for half in range(filter_ref.shape[1] // width):

        @pl.when(section == half)
        def _():
            def move(index, carry):
                first = pl.multiple_of(index * step, step)
                part_ref[pl.ds(first, step), :] = filter_ref[
                    pl.ds(first, step), half * width : (half + 1) * width
                ]
                return carry

            lax.fori_loop(0, part_ref.shape[0] // step, move, 0)

    length = cos_ref.shape[0]
    block = 16

    def rows(index, carry):
        first = pl.multiple_of(index * block, block)
        row = lax.broadcasted_iota(jnp.int32, (block, length), 0) + first
        col = lax.broadcasted_iota(jnp.int32, (block, length), 1)
        angles = lax.rem(row * col, length).astype(jnp.float32) * (2.0 * math.pi / length)
        cos_ref[pl.ds(first, block), :] = jnp.cos(angles).astype(cos_ref.dtype)
        sines = jnp.sin(angles)
        sin_ref[pl.ds(first, block), :] = sines.astype(sin_ref.dtype)
        negated_ref[pl.ds(first, block), :] = (-sines).astype(negated_ref.dtype)
        return carry

    lax.fori_loop(0, length // block, rows, 0)
    cols, half = cos_part_ref.shape

    def part_rows(index, carry):
        first = pl.multiple_of(index * block, block)
        row = lax.broadcasted_iota(jnp.int32, (block, half), 0) + first
        col = lax.broadcasted_iota(jnp.int32, (block, half), 1) + section * half
        angles = lax.rem(row * col, cols).astype(jnp.float32) * (2.0 * math.pi / cols)
        cos_part_ref[pl.ds(first, block), :] = jnp.cos(angles).astype(cos_part_ref.dtype)
        negated_part_ref[pl.ds(first, block), :] = (-jnp.sin(angles)).astype(negated_part_ref.dtype)
        return carry

    lax.fori_loop(0, cols // block, part_rows, 0)
    finish_exchange(*pending)


def exchange(chunks, collective_id):
    return pl.pallas_call(
        exchange_kernel,
        out_shape=jax.ShapeDtypeStruct(chunks.shape, chunks.dtype),
        in_specs=[pl.BlockSpec(memory_space=pl.ANY)],
        out_specs=pl.BlockSpec(memory_space=pl.ANY),
        scratch_shapes=[pltpu.SemaphoreType.DMA(())] * 3,
        compiler_params=pltpu.CompilerParams(collective_id=collective_id, has_side_effects=True),
    )(chunks)


def exchange_with_tables(chunks, filter_rows, collective_id, length):
    table = jax.ShapeDtypeStruct((length, length), jnp.bfloat16)
    part = jax.ShapeDtypeStruct(
        (filter_rows.shape[0], filter_rows.shape[1] // 2), filter_rows.dtype
    )
    return pl.pallas_call(
        exchange_tables_kernel,
        out_shape=(jax.ShapeDtypeStruct(chunks.shape, chunks.dtype), table, table, table, part)
        + (jax.ShapeDtypeStruct((filter_rows.shape[1], part.shape[1]), jnp.bfloat16),) * 2,
        in_specs=[pl.BlockSpec(memory_space=pl.ANY), pl.BlockSpec(memory_space=pltpu.VMEM)],
        out_specs=(
            pl.BlockSpec(memory_space=pl.ANY),
            pl.BlockSpec(memory_space=pltpu.VMEM),
            pl.BlockSpec(memory_space=pltpu.VMEM),
            pl.BlockSpec(memory_space=pltpu.VMEM),
            pl.BlockSpec(memory_space=pltpu.VMEM),
            pl.BlockSpec(memory_space=pltpu.VMEM),
            pl.BlockSpec(memory_space=pltpu.VMEM),
        ),
        scratch_shapes=[pltpu.SemaphoreType.DMA(())] * 3,
        compiler_params=pltpu.CompilerParams(collective_id=collective_id, has_side_effects=True),
    )(chunks, filter_rows)


def pad_chunks(chunks):
    count, length = chunks.shape
    padded = -(-length // 2048) * 2048
    slabs = jnp.pad(chunks, ((0, 0), (0, padded - length)))
    return slabs.reshape(count, padded // 128, 128), length


def unpad_chunks(slabs, length):
    return slabs.reshape(slabs.shape[0], -1)[:, :length]


def exchange_chunks(chunks, collective_id):
    count, length = chunks.shape
    padded = -(-length // 2048) * 2048
    slabs = jnp.pad(chunks, ((0, 0), (0, padded - length))).reshape(count, padded // 128, 128)
    return exchange(slabs, collective_id).reshape(count, padded)[:, :length]


def from_behind(block, axis, distance):
    devices = range(lax.axis_size(axis))
    route = [(i - distance, i) for i in devices if i - distance in devices]
    return lax.ppermute(block, axis, route)


def fourier_tables(length):
    indices = jnp.arange(length, dtype=jnp.int32)
    product = indices[:, None] * indices[None, :] % length
    angles = product.astype(jnp.float32) * (2.0 * math.pi / length)
    return (jnp.cos(angles).astype(jnp.bfloat16), jnp.sin(angles).astype(jnp.bfloat16))


def one_hot_rows(indices, width):
    return (indices[:, None] == jnp.arange(width, dtype=jnp.int32)[None, :]).astype(jnp.bfloat16)


def spread_kernel(weight_rows, row_pick, row_cell, col_cell, width, out_cols):
    picked = jnp.dot(
        one_hot_rows(row_pick, weight_rows.shape[0]), weight_rows,
        preferred_element_type=jnp.float32,
    ).astype(jnp.bfloat16)
    col = jnp.arange(out_cols, dtype=jnp.int32)
    repeat = one_hot_rows(col % width, width).T
    full = jnp.dot(picked, repeat, preferred_element_type=jnp.float32)
    mask = row_cell[:, None] == col_cell[None, :]
    return jnp.where(mask, full, 0.0).astype(jnp.bfloat16)


def patch_kernel_matrix(patch_conv_weight):
    band_count = patch_conv_weight.shape[0]
    width = patch_conv_weight.shape[3]
    row = jnp.arange(band_count * 128, dtype=jnp.int32)
    pixel_row = (row % 128) // 16
    pixel_col = row % 16
    pick = (row // 128) * 16 + (pixel_row % 4) * 4 + pixel_col % 4
    row_cell = (pixel_row // 4) * 4 + pixel_col // 4
    col_cell = jnp.arange(8 * width, dtype=jnp.int32) // width
    weight_rows = patch_conv_weight.reshape(band_count * 16, width)
    return spread_kernel(weight_rows, pick, row_cell, col_cell, width, 8 * width)


def merging_kernel_matrix(merging_conv_weight):
    in_width = merging_conv_weight.shape[2]
    out_width = merging_conv_weight.shape[3]
    row = jnp.arange(8 * in_width, dtype=jnp.int32)
    cell = row // in_width
    pick = ((cell // 4) * 2 + cell % 2) * in_width + row % in_width
    row_cell = (cell % 4) // 2
    col_cell = jnp.arange(2 * out_width, dtype=jnp.int32) // out_width
    weight_rows = merging_conv_weight.reshape(4 * in_width, out_width)
    return spread_kernel(weight_rows, pick, row_cell, col_cell, out_width, 2 * out_width)


def down_matrices(down_weight):
    nothing = jnp.zeros_like(down_weight[0, 0])
    in_width = down_weight.shape[2]
    out_width = down_weight.shape[3]

    def arrange(entries):
        return jnp.stack(
            [jnp.stack(entries[0], axis=0), jnp.stack(entries[1], axis=0)], axis=0
        ).reshape(4 * in_width, out_width)

    own_taps = arrange(
        [[down_weight[1, 1], down_weight[1, 2]], [down_weight[2, 1], down_weight[2, 2]]]
    )
    upper_taps = arrange([[nothing, nothing], [down_weight[0, 1], down_weight[0, 2]]])
    left_taps = arrange([[nothing, down_weight[1, 0]], [nothing, down_weight[2, 0]]])
    corner_taps = arrange([[nothing, nothing], [nothing, down_weight[0, 0]]])
    return (own_taps, upper_taps, left_taps, corner_taps)


def stem_layers(aerial_patch_grid, patch_conv_weight, patch_bias, merging_conv_weight, merge_bias):
    band_count = patch_conv_weight.shape[0]
    patch_matrix = patch_kernel_matrix(patch_conv_weight)
    merging_matrix = merging_kernel_matrix(merging_conv_weight)
    halves = []
    for half in range(2):
        pixels = jnp.concatenate(
            [
                aerial_patch_grid[..., band * 256 + half * 128 : band * 256 + half * 128 + 128]
                for band in range(band_count)
            ],
            axis=-1,
        )
        initial_layer = jnp.einsum(
            "zji,if->zjf", pixels, patch_matrix, preferred_element_type=jnp.float32
        )
        initial_layer = jax.nn.gelu(
            initial_layer + jnp.tile(patch_bias, 8), approximate=True
        ).astype(jnp.bfloat16)
        layer_two = jnp.einsum(
            "zji,if->zjf", initial_layer, merging_matrix, preferred_element_type=jnp.float32
        )
        halves.append(
            jax.nn.gelu(layer_two + jnp.tile(merge_bias, 2), approximate=True).astype(jnp.bfloat16)
        )
    return jnp.concatenate(halves, axis=-1)


def down_conv(stacked, down_weight, down_bias):
    own_taps, upper_taps, left_taps, corner_taps = down_matrices(down_weight)
    summed = jnp.einsum(
        "rwk,kc->crw", stacked[1:, 1:], own_taps, preferred_element_type=jnp.float32
    )
    summed = summed + jnp.einsum(
        "rwk,kc->crw", stacked[:-1, 1:], upper_taps, preferred_element_type=jnp.float32
    )
    summed = summed + jnp.einsum(
        "rwk,kc->crw", stacked[1:, :-1], left_taps, preferred_element_type=jnp.float32
    )
    summed = summed + jnp.einsum(
        "rwk,kc->crw", stacked[:-1, :-1], corner_taps, preferred_element_type=jnp.float32
    )
    return (summed + down_bias[:, None, None]).astype(jnp.bfloat16)


def layer_norm(features, norm_gain):
    values = features.astype(jnp.float32)
    mean_value = jnp.mean(values, axis=0, keepdims=True)
    centered = values - mean_value
    variance = jnp.mean(centered * centered, axis=0, keepdims=True)
    return (norm_gain[:, None, None] * centered * lax.rsqrt(variance + EPSILON)).astype(
        jnp.bfloat16
    )


def filter_columns(row_spectrum, kernel, forward_h, inverse_h):
    spectrum = jnp.einsum(
        "puqh,chqw->cpuw", forward_h, row_spectrum, preferred_element_type=jnp.float32
    ).astype(jnp.bfloat16)
    spec_real = spectrum[:, 0].astype(jnp.float32)
    spec_imag = spectrum[:, 1].astype(jnp.float32)
    filter_real = kernel[:, 0].astype(jnp.float32)
    filter_imag = kernel[:, 1].astype(jnp.float32)
    weighted = jnp.stack(
        [
            filter_real * spec_real - filter_imag * spec_imag,
            filter_real * spec_imag + filter_imag * spec_real,
        ],
        axis=1,
    ).astype(jnp.bfloat16)
    return jnp.einsum(
        "qhpu,cpuw->chqw", inverse_h, weighted, preferred_element_type=jnp.float32
    ).astype(jnp.bfloat16)


def local(
    aerial_patch_grid,
    patch_conv_weight,
    patch_bias,
    merging_conv_weight,
    merge_bias,
    down_weight,
    down_bias,
    norm_gain,
    spectral_filter,
):
    section_index = lax.axis_index("section")
    field_cols = aerial_patch_grid.shape[1]
    channels = down_weight.shape[3]
    full_rows = spectral_filter.shape[2]
    half_channels = channels // 2
    cell_half = field_cols // 2
    tile_index = lax.axis_index("tile")
    grid = jnp.pad(aerial_patch_grid, ((0, 0), (1, 0), (0, 0)))
    own_part = lax.dynamic_slice_in_dim(grid, section_index * cell_half, cell_half + 1, 1)
    image_part = jnp.concatenate([from_behind(own_part[-1:], "tile", 1), own_part], axis=0)
    layer_two = stem_layers(
        image_part, patch_conv_weight, patch_bias, merging_conv_weight, merge_bias
    )
    row_ok = (jnp.arange(layer_two.shape[0]) > 0) | (tile_index > 0)
    col_ok = (jnp.arange(layer_two.shape[1]) > 0) | (section_index > 0)
    stacked = jnp.where(row_ok[:, None, None] & col_ok[None, :, None], layer_two, 0)
    feature_half = down_conv(stacked, down_weight, down_bias)
    normed_half = layer_norm(feature_half, norm_gain)
    tiles = lax.axis_size("tile")
    group_width, tile_rows = channels // tiles, normed_half.shape[1]
    slabs, length = pad_chunks(normed_half.reshape(tiles, -1))
    filter_rows = spectral_filter.reshape(-1, field_cols)
    slabs, cos_h, sin_h, negated_h, kernel_part, cos_part, negated_part = exchange_with_tables(
        slabs, filter_rows, 0, full_rows
    )
    kernel_part = kernel_part.reshape(spectral_filter.shape[:3] + (cell_half,))
    arrived = unpad_chunks(slabs, length)
    fields = (
        arrived.reshape(tiles, group_width, tile_rows, cell_half)
        .transpose(1, 0, 2, 3)
        .reshape(group_width, tiles * tile_rows, cell_half)
    )
    swap = [(0, 1), (1, 0)]
    other_fields = lax.ppermute(fields, "section", swap)

    forward_table = jnp.stack([cos_part, negated_part], axis=1)
    inverse_table = jnp.stack([cos_part, negated_part], axis=0)
    forward_h = jnp.stack(
        [jnp.stack([cos_h, sin_h], axis=1), jnp.stack([negated_h, cos_h], axis=1)], axis=0
    )
    inverse_h = jnp.stack(
        [jnp.stack([cos_h, negated_h], axis=1), jnp.stack([sin_h, cos_h], axis=1)], axis=0
    )
    norm_scale = 1.0 / (full_rows * field_cols)
    own_start = section_index * cell_half
    other_start = (1 - section_index) * cell_half
    frequency_rows = jnp.einsum(
        "chx,xqw->chqw",
        fields,
        lax.dynamic_slice_in_dim(forward_table, own_start, cell_half, 0),
        preferred_element_type=jnp.float32,
    ) + jnp.einsum(
        "chx,xqw->chqw",
        other_fields,
        lax.dynamic_slice_in_dim(forward_table, other_start, cell_half, 0),
        preferred_element_type=jnp.float32,
    )
    back_rows = filter_columns(
        frequency_rows.astype(jnp.bfloat16), kernel_part, forward_h, inverse_h
    )
    other_rows = lax.ppermute(back_rows, "section", swap)
    result = jnp.einsum(
        "chqw,qwv->chv",
        back_rows,
        lax.dynamic_slice_in_dim(inverse_table, own_start, cell_half, 1),
        preferred_element_type=jnp.float32,
    ) + jnp.einsum(
        "chqw,qwv->chv",
        other_rows,
        lax.dynamic_slice_in_dim(inverse_table, other_start, cell_half, 1),
        preferred_element_type=jnp.float32,
    )
    filtered_fields = (result * norm_scale).astype(jnp.bfloat16)
    outgoing = (
        filtered_fields.reshape(group_width, tiles, tile_rows, cell_half)
        .transpose(1, 0, 2, 3)
        .reshape(tiles, -1)
    )
    rows_back = exchange_chunks(outgoing, 1).reshape(channels, tile_rows, cell_half)
    summed = (feature_half.astype(jnp.float32) + rows_back.astype(jnp.float32)).astype(
        jnp.bfloat16
    )
    kept = lax.dynamic_slice_in_dim(summed, section_index * half_channels, half_channels, 0)
    sent = lax.dynamic_slice_in_dim(
        summed, (1 - section_index) * half_channels, half_channels, 0
    )
    received = lax.ppermute(sent, "section", swap)
    return jnp.where(
        section_index == 0,
        jnp.concatenate([kept, received], axis=2),
        jnp.concatenate([received, kept], axis=2),
    )


def solution(mesh):
    return jax.shard_map(
        local,
        mesh=mesh,
        in_specs=(
            P("tile", None, None),
            P(),
            P(),
            P(),
            P(),
            P(),
            P(),
            P(),
            P("tile", None, None, None),
        ),
        out_specs=P("section", "tile", None),
        check_vma=False,
    )
```

```python
import math

import jax
import jax.numpy as jnp
from jax import lax
from jax.experimental import pallas as pl
from jax.experimental.pallas import tpu as pltpu
from jax.sharding import PartitionSpec as P

EPSILON = 1e-05
MESH_ID = pl.DeviceIdType.MESH


def start_exchange(x_ref, o_ref, send_sem, recv_sem, own_sem):
    count = x_ref.shape[0]
    me = lax.axis_index("tile")
    section = lax.axis_index("section")
    barrier = pltpu.get_barrier_semaphore()

    def greet(step, carry):
        peer = lax.rem(me + step, count)
        pl.semaphore_signal(barrier, 1, device_id=(section, peer), device_id_type=MESH_ID)
        return carry

    lax.fori_loop(1, count, greet, 0)
    pl.semaphore_wait(barrier, count - 1)
    own = pltpu.make_async_copy(x_ref.at[pl.ds(me, 1)], o_ref.at[pl.ds(me, 1)], own_sem)
    own.start()

    def send(step, carry):
        peer = lax.rem(me + step, count)
        pltpu.make_async_remote_copy(
            src_ref=x_ref.at[pl.ds(peer, 1)],
            dst_ref=o_ref.at[pl.ds(me, 1)],
            send_sem=send_sem,
            recv_sem=recv_sem,
            device_id=(section, peer),
            device_id_type=MESH_ID,
        ).start()
        return carry

    lax.fori_loop(1, count, send, 0)
    every = pltpu.make_async_remote_copy(
        src_ref=x_ref.at[pl.ds(0, count - 1)],
        dst_ref=o_ref.at[pl.ds(0, count - 1)],
        send_sem=send_sem,
        recv_sem=recv_sem,
        device_id=(section, lax.rem(me + 1, count)),
        device_id_type=MESH_ID,
    )
    return every, own


def finish_exchange(every, own):
    every.wait_send()
    every.wait_recv()
    own.wait()


def exchange_kernel(x_ref, o_ref, send_sem, recv_sem, own_sem):
    finish_exchange(*start_exchange(x_ref, o_ref, send_sem, recv_sem, own_sem))


def exchange_tables_kernel(
    x_ref,
    filter_ref,
    o_ref,
    cos_ref,
    sin_ref,
    negated_ref,
    part_ref,
    cos_part_ref,
    negated_part_ref,
    send_sem,
    recv_sem,
    own_sem,
):
    pending = start_exchange(x_ref, o_ref, send_sem, recv_sem, own_sem)
    section = lax.axis_index("section")
    width = filter_ref.shape[1] // 2

    span = part_ref.shape[1]
    for half in range(filter_ref.shape[1] // width):

        @pl.when(section == half)
        def _():
            def move(index, carry):
                first = pl.multiple_of(index * span, 8)
                flipped = filter_ref[pl.ds(first, span), :].astype(jnp.float32).T
                part_ref[pl.ds(pl.multiple_of(index * width, 8), width), :] = flipped[
                    half * width : (half + 1) * width
                ].astype(part_ref.dtype)
                return carry

            lax.fori_loop(0, filter_ref.shape[0] // span, move, 0)

    length = cos_ref.shape[0]
    block = 16

    def rows(index, carry):
        first = pl.multiple_of(index * block, block)
        row = lax.broadcasted_iota(jnp.int32, (block, length), 0) + first
        col = lax.broadcasted_iota(jnp.int32, (block, length), 1)
        angles = lax.rem(row * col, length).astype(jnp.float32) * (2.0 * math.pi / length)
        cos_ref[pl.ds(first, block), :] = jnp.cos(angles).astype(cos_ref.dtype)
        sines = jnp.sin(angles)
        sin_ref[pl.ds(first, block), :] = sines.astype(sin_ref.dtype)
        negated_ref[pl.ds(first, block), :] = (-sines).astype(negated_ref.dtype)
        return carry

    lax.fori_loop(0, length // block, rows, 0)
    cols, half = cos_part_ref.shape

    def part_rows(index, carry):
        first = pl.multiple_of(index * block, block)
        row = lax.broadcasted_iota(jnp.int32, (block, half), 0) + first
        col = lax.broadcasted_iota(jnp.int32, (block, half), 1) + section * half
        angles = lax.rem(row * col, cols).astype(jnp.float32) * (2.0 * math.pi / cols)
        cos_part_ref[pl.ds(first, block), :] = jnp.cos(angles).astype(cos_part_ref.dtype)
        negated_part_ref[pl.ds(first, block), :] = (-jnp.sin(angles)).astype(negated_part_ref.dtype)
        return carry

    lax.fori_loop(0, cols // block, part_rows, 0)
    finish_exchange(*pending)


def exchange(chunks, collective_id):
    return pl.pallas_call(
        exchange_kernel,
        out_shape=jax.ShapeDtypeStruct(chunks.shape, chunks.dtype),
        in_specs=[pl.BlockSpec(memory_space=pl.ANY)],
        out_specs=pl.BlockSpec(memory_space=pl.ANY),
        scratch_shapes=[pltpu.SemaphoreType.DMA(())] * 3,
        compiler_params=pltpu.CompilerParams(collective_id=collective_id, has_side_effects=True),
    )(chunks)


def exchange_with_tables(chunks, filter_rows, collective_id, length):
    table = jax.ShapeDtypeStruct((length, length), jnp.bfloat16)
    part = jax.ShapeDtypeStruct(
        (filter_rows.shape[0] // length * (filter_rows.shape[1] // 2), length), filter_rows.dtype
    )
    return pl.pallas_call(
        exchange_tables_kernel,
        out_shape=(jax.ShapeDtypeStruct(chunks.shape, chunks.dtype), table, table, table, part)
        + (jax.ShapeDtypeStruct((filter_rows.shape[1], filter_rows.shape[1] // 2), jnp.bfloat16),) * 2,
        in_specs=[pl.BlockSpec(memory_space=pl.ANY), pl.BlockSpec(memory_space=pltpu.VMEM)],
        out_specs=(
            pl.BlockSpec(memory_space=pl.ANY),
            pl.BlockSpec(memory_space=pltpu.VMEM),
            pl.BlockSpec(memory_space=pltpu.VMEM),
            pl.BlockSpec(memory_space=pltpu.VMEM),
            pl.BlockSpec(memory_space=pltpu.VMEM),
            pl.BlockSpec(memory_space=pltpu.VMEM),
            pl.BlockSpec(memory_space=pltpu.VMEM),
        ),
        scratch_shapes=[pltpu.SemaphoreType.DMA(())] * 3,
        compiler_params=pltpu.CompilerParams(collective_id=collective_id, has_side_effects=True),
    )(chunks, filter_rows)


def pad_chunks(chunks):
    count, length = chunks.shape
    padded = -(-length // 2048) * 2048
    slabs = jnp.pad(chunks, ((0, 0), (0, padded - length)))
    return slabs.reshape(count, padded // 128, 128), length


def unpad_chunks(slabs, length):
    return slabs.reshape(slabs.shape[0], -1)[:, :length]


def exchange_chunks(chunks, collective_id):
    count, length = chunks.shape
    padded = -(-length // 2048) * 2048
    slabs = jnp.pad(chunks, ((0, 0), (0, padded - length))).reshape(count, padded // 128, 128)
    return exchange(slabs, collective_id).reshape(count, padded)[:, :length]


def from_behind(block, axis, distance):
    devices = range(lax.axis_size(axis))
    route = [(i - distance, i) for i in devices if i - distance in devices]
    return lax.ppermute(block, axis, route)


def fourier_tables(length):
    indices = jnp.arange(length, dtype=jnp.int32)
    product = indices[:, None] * indices[None, :] % length
    angles = product.astype(jnp.float32) * (2.0 * math.pi / length)
    return (jnp.cos(angles).astype(jnp.bfloat16), jnp.sin(angles).astype(jnp.bfloat16))


def one_hot_rows(indices, width):
    return (indices[:, None] == jnp.arange(width, dtype=jnp.int32)[None, :]).astype(jnp.bfloat16)


def spread_kernel(weight_rows, row_pick, row_cell, col_cell, width, out_cols):
    picked = jnp.dot(
        one_hot_rows(row_pick, weight_rows.shape[0]), weight_rows,
        preferred_element_type=jnp.float32,
    ).astype(jnp.bfloat16)
    col = jnp.arange(out_cols, dtype=jnp.int32)
    repeat = one_hot_rows(col % width, width).T
    full = jnp.dot(picked, repeat, preferred_element_type=jnp.float32)
    mask = row_cell[:, None] == col_cell[None, :]
    return jnp.where(mask, full, 0.0).astype(jnp.bfloat16)


def patch_kernel_matrix(patch_conv_weight):
    band_count = patch_conv_weight.shape[0]
    width = patch_conv_weight.shape[3]
    row = jnp.arange(band_count * 128, dtype=jnp.int32)
    pixel_row = (row % 128) // 16
    pixel_col = row % 16
    pick = (row // 128) * 16 + (pixel_row % 4) * 4 + pixel_col % 4
    row_cell = (pixel_row // 4) * 4 + pixel_col // 4
    col_cell = jnp.arange(8 * width, dtype=jnp.int32) // width
    weight_rows = patch_conv_weight.reshape(band_count * 16, width)
    return spread_kernel(weight_rows, pick, row_cell, col_cell, width, 8 * width)


def merging_kernel_matrix(merging_conv_weight):
    in_width = merging_conv_weight.shape[2]
    out_width = merging_conv_weight.shape[3]
    row = jnp.arange(8 * in_width, dtype=jnp.int32)
    cell = row // in_width
    pick = ((cell // 4) * 2 + cell % 2) * in_width + row % in_width
    row_cell = (cell % 4) // 2
    col_cell = jnp.arange(2 * out_width, dtype=jnp.int32) // out_width
    weight_rows = merging_conv_weight.reshape(4 * in_width, out_width)
    return spread_kernel(weight_rows, pick, row_cell, col_cell, out_width, 2 * out_width)


def down_matrices(down_weight):
    nothing = jnp.zeros_like(down_weight[0, 0])
    in_width = down_weight.shape[2]
    out_width = down_weight.shape[3]

    def arrange(entries):
        return jnp.stack(
            [jnp.stack(entries[0], axis=0), jnp.stack(entries[1], axis=0)], axis=0
        ).reshape(4 * in_width, out_width)

    own_taps = arrange(
        [[down_weight[1, 1], down_weight[1, 2]], [down_weight[2, 1], down_weight[2, 2]]]
    )
    upper_taps = arrange([[nothing, nothing], [down_weight[0, 1], down_weight[0, 2]]])
    left_taps = arrange([[nothing, down_weight[1, 0]], [nothing, down_weight[2, 0]]])
    corner_taps = arrange([[nothing, nothing], [nothing, down_weight[0, 0]]])
    return (own_taps, upper_taps, left_taps, corner_taps)


def stem_layers(aerial_patch_grid, patch_conv_weight, patch_bias, merging_conv_weight, merge_bias):
    band_count = patch_conv_weight.shape[0]
    patch_matrix = patch_kernel_matrix(patch_conv_weight)
    merging_matrix = merging_kernel_matrix(merging_conv_weight)
    halves = []
    for half in range(2):
        pixels = jnp.concatenate(
            [
                aerial_patch_grid[..., band * 256 + half * 128 : band * 256 + half * 128 + 128]
                for band in range(band_count)
            ],
            axis=-1,
        )
        initial_layer = jnp.einsum(
            "zji,if->zjf", pixels, patch_matrix, preferred_element_type=jnp.float32
        )
        initial_layer = jax.nn.gelu(
            initial_layer + jnp.tile(patch_bias, 8), approximate=True
        ).astype(jnp.bfloat16)
        layer_two = jnp.einsum(
            "zji,if->zjf", initial_layer, merging_matrix, preferred_element_type=jnp.float32
        )
        halves.append(
            jax.nn.gelu(layer_two + jnp.tile(merge_bias, 2), approximate=True).astype(jnp.bfloat16)
        )
    return jnp.concatenate(halves, axis=-1)


def down_conv(stacked, down_weight, down_bias):
    own_taps, upper_taps, left_taps, corner_taps = down_matrices(down_weight)
    summed = jnp.einsum(
        "rwk,kc->crw", stacked[1:, 1:], own_taps, preferred_element_type=jnp.float32
    )
    summed = summed + jnp.einsum(
        "rwk,kc->crw", stacked[:-1, 1:], upper_taps, preferred_element_type=jnp.float32
    )
    summed = summed + jnp.einsum(
        "rwk,kc->crw", stacked[1:, :-1], left_taps, preferred_element_type=jnp.float32
    )
    summed = summed + jnp.einsum(
        "rwk,kc->crw", stacked[:-1, :-1], corner_taps, preferred_element_type=jnp.float32
    )
    return (summed + down_bias[:, None, None]).astype(jnp.bfloat16)


def layer_norm(features, norm_gain):
    values = features.astype(jnp.float32)
    mean_value = jnp.mean(values, axis=0, keepdims=True)
    centered = values - mean_value
    variance = jnp.mean(centered * centered, axis=0, keepdims=True)
    return (norm_gain[:, None, None] * centered * lax.rsqrt(variance + EPSILON)).astype(
        jnp.bfloat16
    )


def filter_columns(row_spectrum, kernel, forward_h, inverse_h):
    spectrum = jnp.einsum(
        "puqh,chqw->cpuw", forward_h, row_spectrum, preferred_element_type=jnp.float32
    ).astype(jnp.bfloat16)
    spec_real = spectrum[:, 0].astype(jnp.float32)
    spec_imag = spectrum[:, 1].astype(jnp.float32)
    filter_real = kernel[:, 0].astype(jnp.float32)
    filter_imag = kernel[:, 1].astype(jnp.float32)
    weighted = jnp.stack(
        [
            filter_real * spec_real - filter_imag * spec_imag,
            filter_real * spec_imag + filter_imag * spec_real,
        ],
        axis=1,
    ).astype(jnp.bfloat16)
    return jnp.einsum(
        "qhpu,cpuw->chqw", inverse_h, weighted, preferred_element_type=jnp.float32
    ).astype(jnp.bfloat16)


def local(
    aerial_patch_grid,
    patch_conv_weight,
    patch_bias,
    merging_conv_weight,
    merge_bias,
    down_weight,
    down_bias,
    norm_gain,
    spectral_filter,
):
    section_index = lax.axis_index("section")
    field_cols = aerial_patch_grid.shape[1]
    channels = down_weight.shape[3]
    full_rows = spectral_filter.shape[2]
    half_channels = channels // 2
    cell_half = field_cols // 2
    tile_index = lax.axis_index("tile")
    grid = jnp.pad(aerial_patch_grid, ((0, 0), (1, 0), (0, 0)))
    own_part = lax.dynamic_slice_in_dim(grid, section_index * cell_half, cell_half + 1, 1)
    image_part = jnp.concatenate([from_behind(own_part[-1:], "tile", 1), own_part], axis=0)
    layer_two = stem_layers(
        image_part, patch_conv_weight, patch_bias, merging_conv_weight, merge_bias
    )
    row_ok = (jnp.arange(layer_two.shape[0]) > 0) | (tile_index > 0)
    col_ok = (jnp.arange(layer_two.shape[1]) > 0) | (section_index > 0)
    stacked = jnp.where(row_ok[:, None, None] & col_ok[None, :, None], layer_two, 0)
    feature_half = down_conv(stacked, down_weight, down_bias)
    normed_half = layer_norm(feature_half, norm_gain)
    tiles = lax.axis_size("tile")
    group_width, tile_rows = channels // tiles, normed_half.shape[1]
    slabs, length = pad_chunks(normed_half.reshape(tiles, -1))
    filter_rows = spectral_filter.reshape(-1, field_cols)
    slabs, cos_h, sin_h, negated_h, kernel_part, cos_part, negated_part = exchange_with_tables(
        slabs, filter_rows, 0, full_rows
    )
    kernel_part = jnp.swapaxes(
        kernel_part.reshape(spectral_filter.shape[:2] + (cell_half, full_rows)), 2, 3
    )
    arrived = unpad_chunks(slabs, length)
    fields = (
        arrived.reshape(tiles, group_width, tile_rows, cell_half)
        .transpose(1, 0, 2, 3)
        .reshape(group_width, tiles * tile_rows, cell_half)
    )
    swap = [(0, 1), (1, 0)]
    other_fields = lax.ppermute(fields, "section", swap)

    forward_table = jnp.stack([cos_part, negated_part], axis=1)
    inverse_table = jnp.stack([cos_part, negated_part], axis=0)
    forward_h = jnp.stack(
        [jnp.stack([cos_h, sin_h], axis=1), jnp.stack([negated_h, cos_h], axis=1)], axis=0
    )
    inverse_h = jnp.stack(
        [jnp.stack([cos_h, negated_h], axis=1), jnp.stack([sin_h, cos_h], axis=1)], axis=0
    )
    norm_scale = 1.0 / (full_rows * field_cols)
    own_start = section_index * cell_half
    other_start = (1 - section_index) * cell_half
    frequency_rows = jnp.einsum(
        "chx,xqw->chqw",
        fields,
        lax.dynamic_slice_in_dim(forward_table, own_start, cell_half, 0),
        preferred_element_type=jnp.float32,
    ) + jnp.einsum(
        "chx,xqw->chqw",
        other_fields,
        lax.dynamic_slice_in_dim(forward_table, other_start, cell_half, 0),
        preferred_element_type=jnp.float32,
    )
    back_rows = filter_columns(
        frequency_rows.astype(jnp.bfloat16), kernel_part, forward_h, inverse_h
    )
    other_rows = lax.ppermute(back_rows, "section", swap)
    result = jnp.einsum(
        "chqw,qwv->chv",
        back_rows,
        lax.dynamic_slice_in_dim(inverse_table, own_start, cell_half, 1),
        preferred_element_type=jnp.float32,
    ) + jnp.einsum(
        "chqw,qwv->chv",
        other_rows,
        lax.dynamic_slice_in_dim(inverse_table, other_start, cell_half, 1),
        preferred_element_type=jnp.float32,
    )
    filtered_fields = (result * norm_scale).astype(jnp.bfloat16)
    outgoing = (
        filtered_fields.reshape(group_width, tiles, tile_rows, cell_half)
        .transpose(1, 0, 2, 3)
        .reshape(tiles, -1)
    )
    rows_back = exchange_chunks(outgoing, 1).reshape(channels, tile_rows, cell_half)
    summed = (feature_half.astype(jnp.float32) + rows_back.astype(jnp.float32)).astype(
        jnp.bfloat16
    )
    kept = lax.dynamic_slice_in_dim(summed, section_index * half_channels, half_channels, 0)
    sent = lax.dynamic_slice_in_dim(
        summed, (1 - section_index) * half_channels, half_channels, 0
    )
    received = lax.ppermute(sent, "section", swap)
    return jnp.where(
        section_index == 0,
        jnp.concatenate([kept, received], axis=2),
        jnp.concatenate([received, kept], axis=2),
    )


def solution(mesh):
    return jax.shard_map(
        local,
        mesh=mesh,
        in_specs=(
            P("tile", None, None),
            P(),
            P(),
            P(),
            P(),
            P(),
            P(),
            P(),
            P("tile", None, None, None),
        ),
        out_specs=P("section", "tile", None),
        check_vma=False,
    )
```

```python
import math

import jax
import jax.numpy as jnp
from jax import lax
from jax.experimental import pallas as pl
from jax.experimental.pallas import tpu as pltpu
from jax.sharding import PartitionSpec as P

EPSILON = 1e-05
MESH_ID = pl.DeviceIdType.MESH


def start_exchange(x_ref, o_ref, send_sem, recv_sem, own_sem):
    count = x_ref.shape[0]
    me = lax.axis_index("tile")
    section = lax.axis_index("section")
    barrier = pltpu.get_barrier_semaphore()

    def greet(step, carry):
        peer = lax.rem(me + step, count)
        pl.semaphore_signal(barrier, 1, device_id=(section, peer), device_id_type=MESH_ID)
        return carry

    lax.fori_loop(1, count, greet, 0)
    pl.semaphore_wait(barrier, count - 1)
    own = pltpu.make_async_copy(x_ref.at[pl.ds(me, 1)], o_ref.at[pl.ds(me, 1)], own_sem)
    own.start()

    def send(step, carry):
        peer = lax.rem(me + step, count)
        pltpu.make_async_remote_copy(
            src_ref=x_ref.at[pl.ds(peer, 1)],
            dst_ref=o_ref.at[pl.ds(me, 1)],
            send_sem=send_sem,
            recv_sem=recv_sem,
            device_id=(section, peer),
            device_id_type=MESH_ID,
        ).start()
        return carry

    lax.fori_loop(1, count, send, 0)
    every = pltpu.make_async_remote_copy(
        src_ref=x_ref.at[pl.ds(0, count - 1)],
        dst_ref=o_ref.at[pl.ds(0, count - 1)],
        send_sem=send_sem,
        recv_sem=recv_sem,
        device_id=(section, lax.rem(me + 1, count)),
        device_id_type=MESH_ID,
    )
    return every, own


def finish_exchange(every, own):
    every.wait_send()
    every.wait_recv()
    own.wait()


def exchange_kernel(x_ref, o_ref, send_sem, recv_sem, own_sem):
    finish_exchange(*start_exchange(x_ref, o_ref, send_sem, recv_sem, own_sem))


def exchange_tables_kernel(
    x_ref,
    filter_ref,
    o_ref,
    cos_ref,
    sin_ref,
    negated_ref,
    part_ref,
    cos_part_ref,
    negated_part_ref,
    send_sem,
    recv_sem,
    own_sem,
):
    pending = start_exchange(x_ref, o_ref, send_sem, recv_sem, own_sem)
    section = lax.axis_index("section")
    width = filter_ref.shape[1] // 2

    span = part_ref.shape[1]
    for half in range(filter_ref.shape[1] // width):

        @pl.when(section == half)
        def _():
            def move(index, carry):
                first = pl.multiple_of(index * span, 8)
                flipped = filter_ref[pl.ds(first, span), :].astype(jnp.float32).T
                part_ref[pl.ds(pl.multiple_of(index * width, 8), width), :] = flipped[
                    half * width : (half + 1) * width
                ].astype(part_ref.dtype)
                return carry

            lax.fori_loop(0, filter_ref.shape[0] // span, move, 0)

    length = cos_ref.shape[0]
    block = 16

    def rows(index, carry):
        first = pl.multiple_of(index * block, block)
        row = lax.broadcasted_iota(jnp.int32, (block, length), 0) + first
        col = lax.broadcasted_iota(jnp.int32, (block, length), 1)
        angles = lax.rem(row * col, length).astype(jnp.float32) * (2.0 * math.pi / length)
        cos_ref[pl.ds(first, block), :] = jnp.cos(angles).astype(cos_ref.dtype)
        sines = jnp.sin(angles)
        sin_ref[pl.ds(first, block), :] = sines.astype(sin_ref.dtype)
        negated_ref[pl.ds(first, block), :] = (-sines).astype(negated_ref.dtype)
        return carry

    lax.fori_loop(0, length // block, rows, 0)
    cols, half = cos_part_ref.shape

    def part_rows(index, carry):
        first = pl.multiple_of(index * block, block)
        row = lax.broadcasted_iota(jnp.int32, (block, half), 0) + first
        col = lax.broadcasted_iota(jnp.int32, (block, half), 1) + section * half
        angles = lax.rem(row * col, cols).astype(jnp.float32) * (2.0 * math.pi / cols)
        cos_part_ref[pl.ds(first, block), :] = jnp.cos(angles).astype(cos_part_ref.dtype)
        negated_part_ref[pl.ds(first, block), :] = (-jnp.sin(angles)).astype(negated_part_ref.dtype)
        return carry

    lax.fori_loop(0, cols // block, part_rows, 0)
    finish_exchange(*pending)


def exchange(chunks, collective_id):
    return pl.pallas_call(
        exchange_kernel,
        out_shape=jax.ShapeDtypeStruct(chunks.shape, chunks.dtype),
        in_specs=[pl.BlockSpec(memory_space=pl.ANY)],
        out_specs=pl.BlockSpec(memory_space=pl.ANY),
        scratch_shapes=[pltpu.SemaphoreType.DMA(())] * 3,
        compiler_params=pltpu.CompilerParams(collective_id=collective_id, has_side_effects=True),
    )(chunks)


def exchange_with_tables(chunks, filter_rows, collective_id, length):
    table = jax.ShapeDtypeStruct((length, length), jnp.bfloat16)
    part = jax.ShapeDtypeStruct(
        (filter_rows.shape[0] // length * (filter_rows.shape[1] // 2), length), filter_rows.dtype
    )
    return pl.pallas_call(
        exchange_tables_kernel,
        out_shape=(jax.ShapeDtypeStruct(chunks.shape, chunks.dtype), table, table, table, part)
        + (jax.ShapeDtypeStruct((filter_rows.shape[1], filter_rows.shape[1] // 2), jnp.bfloat16),) * 2,
        in_specs=[pl.BlockSpec(memory_space=pl.ANY), pl.BlockSpec(memory_space=pltpu.VMEM)],
        out_specs=(
            pl.BlockSpec(memory_space=pl.ANY),
            pl.BlockSpec(memory_space=pltpu.VMEM),
            pl.BlockSpec(memory_space=pltpu.VMEM),
            pl.BlockSpec(memory_space=pltpu.VMEM),
            pl.BlockSpec(memory_space=pltpu.VMEM),
            pl.BlockSpec(memory_space=pltpu.VMEM),
            pl.BlockSpec(memory_space=pltpu.VMEM),
        ),
        scratch_shapes=[pltpu.SemaphoreType.DMA(())] * 3,
        compiler_params=pltpu.CompilerParams(collective_id=collective_id, has_side_effects=True),
    )(chunks, filter_rows)


def pad_chunks(chunks):
    count, length = chunks.shape
    padded = -(-length // 2048) * 2048
    slabs = jnp.pad(chunks, ((0, 0), (0, padded - length)))
    return slabs.reshape(count, padded // 128, 128), length


def unpad_chunks(slabs, length):
    return slabs.reshape(slabs.shape[0], -1)[:, :length]


def exchange_chunks(chunks, collective_id):
    count, length = chunks.shape
    padded = -(-length // 2048) * 2048
    slabs = jnp.pad(chunks, ((0, 0), (0, padded - length))).reshape(count, padded // 128, 128)
    return exchange(slabs, collective_id).reshape(count, padded)[:, :length]


def from_behind(block, axis, distance):
    devices = range(lax.axis_size(axis))
    route = [(i - distance, i) for i in devices if i - distance in devices]
    return lax.ppermute(block, axis, route)


def fourier_tables(length):
    indices = jnp.arange(length, dtype=jnp.int32)
    product = indices[:, None] * indices[None, :] % length
    angles = product.astype(jnp.float32) * (2.0 * math.pi / length)
    return (jnp.cos(angles).astype(jnp.bfloat16), jnp.sin(angles).astype(jnp.bfloat16))


def one_hot_rows(indices, width):
    return (indices[:, None] == jnp.arange(width, dtype=jnp.int32)[None, :]).astype(jnp.bfloat16)


def spread_kernel(weight_rows, row_pick, row_cell, col_cell, width, out_cols):
    picked = jnp.dot(
        one_hot_rows(row_pick, weight_rows.shape[0]), weight_rows,
        preferred_element_type=jnp.float32,
    ).astype(jnp.bfloat16)
    col = jnp.arange(out_cols, dtype=jnp.int32)
    repeat = one_hot_rows(col % width, width).T
    full = jnp.dot(picked, repeat, preferred_element_type=jnp.float32)
    mask = row_cell[:, None] == col_cell[None, :]
    return jnp.where(mask, full, 0.0).astype(jnp.bfloat16)


def patch_kernel_matrix(patch_conv_weight):
    band_count = patch_conv_weight.shape[0]
    width = patch_conv_weight.shape[3]
    row = jnp.arange(band_count * 128, dtype=jnp.int32)
    pixel_row = (row % 128) // 16
    pixel_col = row % 16
    pick = (row // 128) * 16 + (pixel_row % 4) * 4 + pixel_col % 4
    row_cell = (pixel_row // 4) * 4 + pixel_col // 4
    col_cell = jnp.arange(8 * width, dtype=jnp.int32) // width
    weight_rows = patch_conv_weight.reshape(band_count * 16, width)
    return spread_kernel(weight_rows, pick, row_cell, col_cell, width, 8 * width)


def merging_kernel_matrix(merging_conv_weight):
    in_width = merging_conv_weight.shape[2]
    out_width = merging_conv_weight.shape[3]
    row = jnp.arange(8 * in_width, dtype=jnp.int32)
    cell = row // in_width
    pick = ((cell // 4) * 2 + cell % 2) * in_width + row % in_width
    row_cell = (cell % 4) // 2
    col_cell = jnp.arange(2 * out_width, dtype=jnp.int32) // out_width
    weight_rows = merging_conv_weight.reshape(4 * in_width, out_width)
    return spread_kernel(weight_rows, pick, row_cell, col_cell, out_width, 2 * out_width)


def down_matrices(down_weight):
    nothing = jnp.zeros_like(down_weight[0, 0])
    in_width = down_weight.shape[2]
    out_width = down_weight.shape[3]

    def arrange(entries):
        return jnp.stack(
            [jnp.stack(entries[0], axis=0), jnp.stack(entries[1], axis=0)], axis=0
        ).reshape(4 * in_width, out_width)

    own_taps = arrange(
        [[down_weight[1, 1], down_weight[1, 2]], [down_weight[2, 1], down_weight[2, 2]]]
    )
    upper_taps = arrange([[nothing, nothing], [down_weight[0, 1], down_weight[0, 2]]])
    left_taps = arrange([[nothing, down_weight[1, 0]], [nothing, down_weight[2, 0]]])
    corner_taps = arrange([[nothing, nothing], [nothing, down_weight[0, 0]]])
    return (own_taps, upper_taps, left_taps, corner_taps)


def stem_layers(aerial_patch_grid, patch_conv_weight, patch_bias, merging_conv_weight, merge_bias):
    band_count = patch_conv_weight.shape[0]
    patch_matrix = patch_kernel_matrix(patch_conv_weight)
    merging_matrix = merging_kernel_matrix(merging_conv_weight)
    halves = []
    for half in range(2):
        pixels = jnp.concatenate(
            [
                aerial_patch_grid[..., band * 256 + half * 128 : band * 256 + half * 128 + 128]
                for band in range(band_count)
            ],
            axis=-1,
        )
        initial_layer = jnp.einsum(
            "zji,if->zjf", pixels, patch_matrix, preferred_element_type=jnp.float32
        )
        initial_layer = jax.nn.gelu(
            initial_layer + jnp.tile(patch_bias, 8), approximate=True
        ).astype(jnp.bfloat16)
        layer_two = jnp.einsum(
            "zji,if->zjf", initial_layer, merging_matrix, preferred_element_type=jnp.float32
        )
        halves.append(
            jax.nn.gelu(layer_two + jnp.tile(merge_bias, 2), approximate=True).astype(jnp.bfloat16)
        )
    return jnp.concatenate(halves, axis=-1)


def down_conv(stacked, down_weight, down_bias):
    own_taps, upper_taps, left_taps, corner_taps = down_matrices(down_weight)
    summed = jnp.einsum(
        "rwk,kc->crw", stacked[1:, 1:], own_taps, preferred_element_type=jnp.float32
    )
    summed = summed + jnp.einsum(
        "rwk,kc->crw", stacked[:-1, 1:], upper_taps, preferred_element_type=jnp.float32
    )
    summed = summed + jnp.einsum(
        "rwk,kc->crw", stacked[1:, :-1], left_taps, preferred_element_type=jnp.float32
    )
    summed = summed + jnp.einsum(
        "rwk,kc->crw", stacked[:-1, :-1], corner_taps, preferred_element_type=jnp.float32
    )
    return (summed + down_bias[:, None, None]).astype(jnp.bfloat16)


def layer_norm(features, norm_gain):
    values = features.astype(jnp.float32)
    mean_value = jnp.mean(values, axis=0, keepdims=True)
    centered = values - mean_value
    variance = jnp.mean(centered * centered, axis=0, keepdims=True)
    return (norm_gain[:, None, None] * centered * lax.rsqrt(variance + EPSILON)).astype(
        jnp.bfloat16
    )


def filter_columns(row_spectrum, kernel, forward_h, inverse_h):
    spectrum = jnp.einsum(
        "puqh,chqw->cpuw", forward_h, row_spectrum, preferred_element_type=jnp.float32
    ).astype(jnp.bfloat16)
    spec_real = spectrum[:, 0].astype(jnp.float32)
    spec_imag = spectrum[:, 1].astype(jnp.float32)
    filter_real = kernel[:, 0].astype(jnp.float32)
    filter_imag = kernel[:, 1].astype(jnp.float32)
    weighted = jnp.stack(
        [
            filter_real * spec_real - filter_imag * spec_imag,
            filter_real * spec_imag + filter_imag * spec_real,
        ],
        axis=1,
    ).astype(jnp.bfloat16)
    return jnp.einsum(
        "qhpu,cpuw->chqw", inverse_h, weighted, preferred_element_type=jnp.float32
    ).astype(jnp.bfloat16)


def local(
    aerial_patch_grid,
    patch_conv_weight,
    patch_bias,
    merging_conv_weight,
    merge_bias,
    down_weight,
    down_bias,
    norm_gain,
    spectral_filter,
):
    section_index = lax.axis_index("section")
    field_cols = aerial_patch_grid.shape[1]
    channels = down_weight.shape[3]
    full_rows = spectral_filter.shape[2]
    half_channels = channels // 2
    cell_half = field_cols // 2
    tile_index = lax.axis_index("tile")
    grid = jnp.pad(aerial_patch_grid, ((0, 0), (1, 0), (0, 0)))
    own_part = lax.dynamic_slice_in_dim(grid, section_index * cell_half, cell_half + 1, 1)
    image_part = jnp.concatenate([from_behind(own_part[-1:], "tile", 1), own_part], axis=0)
    layer_two = stem_layers(
        image_part, patch_conv_weight, patch_bias, merging_conv_weight, merge_bias
    )
    row_ok = (jnp.arange(layer_two.shape[0]) > 0) | (tile_index > 0)
    col_ok = (jnp.arange(layer_two.shape[1]) > 0) | (section_index > 0)
    stacked = jnp.where(row_ok[:, None, None] & col_ok[None, :, None], layer_two, 0)
    feature_half = down_conv(stacked, down_weight, down_bias)
    normed_half = layer_norm(feature_half, norm_gain)
    tiles = lax.axis_size("tile")
    group_width, tile_rows = channels // tiles, normed_half.shape[1]
    slabs, length = pad_chunks(normed_half.reshape(tiles, -1))
    filter_rows = spectral_filter.reshape(-1, field_cols)
    slabs, cos_h, sin_h, negated_h, kernel_part, cos_part, negated_part = exchange_with_tables(
        slabs, filter_rows, 0, full_rows
    )
    kernel_part = jnp.swapaxes(
        kernel_part.reshape(spectral_filter.shape[:2] + (cell_half, full_rows)), 2, 3
    )
    arrived = unpad_chunks(slabs, length)
    fields = (
        arrived.reshape(tiles, group_width, tile_rows, cell_half)
        .transpose(1, 0, 2, 3)
        .reshape(group_width, tiles * tile_rows, cell_half)
    )
    swap = [(0, 1), (1, 0)]
    other_fields = lax.ppermute(fields, "section", swap)

    forward_table = jnp.stack([cos_part, negated_part], axis=1)
    inverse_table = jnp.stack([cos_part, negated_part], axis=0)
    forward_h = jnp.stack(
        [jnp.stack([cos_h, sin_h], axis=1), jnp.stack([negated_h, cos_h], axis=1)], axis=0
    )
    inverse_h = jnp.stack(
        [jnp.stack([cos_h, negated_h], axis=1), jnp.stack([sin_h, cos_h], axis=1)], axis=0
    )
    norm_scale = 1.0 / (full_rows * field_cols)
    own_start = section_index * cell_half
    other_start = (1 - section_index) * cell_half
    frequency_rows = jnp.einsum(
        "chx,xqw->chqw",
        fields,
        lax.dynamic_slice_in_dim(forward_table, own_start, cell_half, 0),
        preferred_element_type=jnp.float32,
    ) + jnp.einsum(
        "chx,xqw->chqw",
        other_fields,
        lax.dynamic_slice_in_dim(forward_table, other_start, cell_half, 0),
        preferred_element_type=jnp.float32,
    )
    back_rows = filter_columns(
        frequency_rows.astype(jnp.bfloat16), kernel_part, forward_h, inverse_h
    )
    other_rows = lax.ppermute(back_rows, "section", swap)
    result = jnp.einsum(
        "chqw,qwv->chv",
        back_rows,
        lax.dynamic_slice_in_dim(inverse_table, own_start, cell_half, 1),
        preferred_element_type=jnp.float32,
    ) + jnp.einsum(
        "chqw,qwv->chv",
        other_rows,
        lax.dynamic_slice_in_dim(inverse_table, other_start, cell_half, 1),
        preferred_element_type=jnp.float32,
    )
    filtered_fields = (result * norm_scale).astype(jnp.bfloat16)
    outgoing = (
        filtered_fields.reshape(group_width, tiles, tile_rows, cell_half)
        .transpose(1, 0, 2, 3)
        .reshape(tiles, -1)
    )
    rows_back = exchange_chunks(outgoing, 1).reshape(channels, tile_rows, cell_half)
    summed = (feature_half.astype(jnp.float32) + rows_back.astype(jnp.float32)).astype(
        jnp.bfloat16
    )
    kept = lax.dynamic_slice_in_dim(summed, section_index * half_channels, half_channels, 0)
    sent = lax.dynamic_slice_in_dim(
        summed, (1 - section_index) * half_channels, half_channels, 0
    )
    received = lax.ppermute(sent, "section", swap)
    first_section = section_index == 0
    return jnp.concatenate(
        [jnp.where(first_section, kept, received), jnp.where(first_section, received, kept)], axis=2
    )


def solution(mesh):
    return jax.shard_map(
        local,
        mesh=mesh,
        in_specs=(
            P("tile", None, None),
            P(),
            P(),
            P(),
            P(),
            P(),
            P(),
            P(),
            P("tile", None, None, None),
        ),
        out_specs=P("section", "tile", None),
        check_vma=False,
    )
```

```python
import math

import jax
import jax.numpy as jnp
from jax import lax
from jax.experimental import pallas as pl
from jax.experimental.pallas import tpu as pltpu
from jax.sharding import PartitionSpec as P

EPSILON = 1e-05
MESH_ID = pl.DeviceIdType.MESH


def start_exchange(x_ref, o_ref, send_sem, recv_sem, own_sem):
    count = x_ref.shape[0]
    me = lax.axis_index("tile")
    section = lax.axis_index("section")
    barrier = pltpu.get_barrier_semaphore()

    def greet(step, carry):
        peer = lax.rem(me + step, count)
        pl.semaphore_signal(barrier, 1, device_id=(section, peer), device_id_type=MESH_ID)
        return carry

    lax.fori_loop(1, count, greet, 0)
    pl.semaphore_wait(barrier, count - 1)
    own = pltpu.make_async_copy(x_ref.at[pl.ds(me, 1)], o_ref.at[pl.ds(me, 1)], own_sem)
    own.start()

    def send(step, carry):
        offset = jnp.where(step % 2 == 1, (step + 1) // 2, count - step // 2)
        peer = lax.rem(me + offset, count)
        pltpu.make_async_remote_copy(
            src_ref=x_ref.at[pl.ds(peer, 1)],
            dst_ref=o_ref.at[pl.ds(me, 1)],
            send_sem=send_sem,
            recv_sem=recv_sem,
            device_id=(section, peer),
            device_id_type=MESH_ID,
        ).start()
        return carry

    lax.fori_loop(1, count, send, 0)
    every = pltpu.make_async_remote_copy(
        src_ref=x_ref.at[pl.ds(0, count - 1)],
        dst_ref=o_ref.at[pl.ds(0, count - 1)],
        send_sem=send_sem,
        recv_sem=recv_sem,
        device_id=(section, lax.rem(me + 1, count)),
        device_id_type=MESH_ID,
    )
    return every, own


def finish_exchange(every, own):
    every.wait_send()
    every.wait_recv()
    own.wait()


def exchange_kernel(x_ref, o_ref, send_sem, recv_sem, own_sem):
    finish_exchange(*start_exchange(x_ref, o_ref, send_sem, recv_sem, own_sem))


def exchange_tables_kernel(
    x_ref,
    filter_ref,
    o_ref,
    cos_ref,
    sin_ref,
    negated_ref,
    part_ref,
    cos_part_ref,
    negated_part_ref,
    send_sem,
    recv_sem,
    own_sem,
):
    pending = start_exchange(x_ref, o_ref, send_sem, recv_sem, own_sem)
    section = lax.axis_index("section")
    width = filter_ref.shape[1] // 2

    span = part_ref.shape[1]
    for half in range(filter_ref.shape[1] // width):

        @pl.when(section == half)
        def _():
            def move(index, carry):
                first = pl.multiple_of(index * span, 8)
                flipped = filter_ref[pl.ds(first, span), :].astype(jnp.float32).T
                part_ref[pl.ds(pl.multiple_of(index * width, 8), width), :] = flipped[
                    half * width : (half + 1) * width
                ].astype(part_ref.dtype)
                return carry

            lax.fori_loop(0, filter_ref.shape[0] // span, move, 0)

    length = cos_ref.shape[0]
    block = 16

    def rows(index, carry):
        first = pl.multiple_of(index * block, block)
        row = lax.broadcasted_iota(jnp.int32, (block, length), 0) + first
        col = lax.broadcasted_iota(jnp.int32, (block, length), 1)
        angles = lax.rem(row * col, length).astype(jnp.float32) * (2.0 * math.pi / length)
        cos_ref[pl.ds(first, block), :] = jnp.cos(angles).astype(cos_ref.dtype)
        sines = jnp.sin(angles)
        sin_ref[pl.ds(first, block), :] = sines.astype(sin_ref.dtype)
        negated_ref[pl.ds(first, block), :] = (-sines).astype(negated_ref.dtype)
        return carry

    lax.fori_loop(0, length // block, rows, 0)
    cols, half = cos_part_ref.shape

    def part_rows(index, carry):
        first = pl.multiple_of(index * block, block)
        row = lax.broadcasted_iota(jnp.int32, (block, half), 0) + first
        col = lax.broadcasted_iota(jnp.int32, (block, half), 1) + section * half
        angles = lax.rem(row * col, cols).astype(jnp.float32) * (2.0 * math.pi / cols)
        cos_part_ref[pl.ds(first, block), :] = jnp.cos(angles).astype(cos_part_ref.dtype)
        negated_part_ref[pl.ds(first, block), :] = (-jnp.sin(angles)).astype(negated_part_ref.dtype)
        return carry

    lax.fori_loop(0, cols // block, part_rows, 0)
    finish_exchange(*pending)


def exchange(chunks, collective_id):
    return pl.pallas_call(
        exchange_kernel,
        out_shape=jax.ShapeDtypeStruct(chunks.shape, chunks.dtype),
        in_specs=[pl.BlockSpec(memory_space=pl.ANY)],
        out_specs=pl.BlockSpec(memory_space=pl.ANY),
        scratch_shapes=[pltpu.SemaphoreType.DMA(())] * 3,
        compiler_params=pltpu.CompilerParams(collective_id=collective_id, has_side_effects=True),
    )(chunks)


def exchange_with_tables(chunks, filter_rows, collective_id, length):
    table = jax.ShapeDtypeStruct((length, length), jnp.bfloat16)
    part = jax.ShapeDtypeStruct(
        (filter_rows.shape[0] // length * (filter_rows.shape[1] // 2), length), filter_rows.dtype
    )
    return pl.pallas_call(
        exchange_tables_kernel,
        out_shape=(jax.ShapeDtypeStruct(chunks.shape, chunks.dtype), table, table, table, part)
        + (jax.ShapeDtypeStruct((filter_rows.shape[1], filter_rows.shape[1] // 2), jnp.bfloat16),) * 2,
        in_specs=[pl.BlockSpec(memory_space=pl.ANY), pl.BlockSpec(memory_space=pltpu.VMEM)],
        out_specs=(
            pl.BlockSpec(memory_space=pl.ANY),
            pl.BlockSpec(memory_space=pltpu.VMEM),
            pl.BlockSpec(memory_space=pltpu.VMEM),
            pl.BlockSpec(memory_space=pltpu.VMEM),
            pl.BlockSpec(memory_space=pltpu.VMEM),
            pl.BlockSpec(memory_space=pltpu.VMEM),
            pl.BlockSpec(memory_space=pltpu.VMEM),
        ),
        scratch_shapes=[pltpu.SemaphoreType.DMA(())] * 3,
        compiler_params=pltpu.CompilerParams(collective_id=collective_id, has_side_effects=True),
    )(chunks, filter_rows)


def pad_chunks(chunks):
    count, length = chunks.shape
    padded = -(-length // 2048) * 2048
    slabs = jnp.pad(chunks, ((0, 0), (0, padded - length)))
    return slabs.reshape(count, padded // 128, 128), length


def unpad_chunks(slabs, length):
    return slabs.reshape(slabs.shape[0], -1)[:, :length]


def exchange_chunks(chunks, collective_id):
    count, length = chunks.shape
    padded = -(-length // 2048) * 2048
    slabs = jnp.pad(chunks, ((0, 0), (0, padded - length))).reshape(count, padded // 128, 128)
    return exchange(slabs, collective_id).reshape(count, padded)[:, :length]


def from_behind(block, axis, distance):
    devices = range(lax.axis_size(axis))
    route = [(i - distance, i) for i in devices if i - distance in devices]
    return lax.ppermute(block, axis, route)


def fourier_tables(length):
    indices = jnp.arange(length, dtype=jnp.int32)
    product = indices[:, None] * indices[None, :] % length
    angles = product.astype(jnp.float32) * (2.0 * math.pi / length)
    return (jnp.cos(angles).astype(jnp.bfloat16), jnp.sin(angles).astype(jnp.bfloat16))


def one_hot_rows(indices, width):
    return (indices[:, None] == jnp.arange(width, dtype=jnp.int32)[None, :]).astype(jnp.bfloat16)


def spread_kernel(weight_rows, row_pick, row_cell, col_cell, width, out_cols):
    picked = jnp.dot(
        one_hot_rows(row_pick, weight_rows.shape[0]), weight_rows,
        preferred_element_type=jnp.float32,
    ).astype(jnp.bfloat16)
    col = jnp.arange(out_cols, dtype=jnp.int32)
    repeat = one_hot_rows(col % width, width).T
    full = jnp.dot(picked, repeat, preferred_element_type=jnp.float32)
    mask = row_cell[:, None] == col_cell[None, :]
    return jnp.where(mask, full, 0.0).astype(jnp.bfloat16)


def patch_kernel_matrix(patch_conv_weight):
    band_count = patch_conv_weight.shape[0]
    width = patch_conv_weight.shape[3]
    row = jnp.arange(band_count * 128, dtype=jnp.int32)
    pixel_row = (row % 128) // 16
    pixel_col = row % 16
    pick = (row // 128) * 16 + (pixel_row % 4) * 4 + pixel_col % 4
    row_cell = (pixel_row // 4) * 4 + pixel_col // 4
    col_cell = jnp.arange(8 * width, dtype=jnp.int32) // width
    weight_rows = patch_conv_weight.reshape(band_count * 16, width)
    return spread_kernel(weight_rows, pick, row_cell, col_cell, width, 8 * width)


def merging_kernel_matrix(merging_conv_weight):
    in_width = merging_conv_weight.shape[2]
    out_width = merging_conv_weight.shape[3]
    row = jnp.arange(8 * in_width, dtype=jnp.int32)
    cell = row // in_width
    pick = ((cell // 4) * 2 + cell % 2) * in_width + row % in_width
    row_cell = (cell % 4) // 2
    col_cell = jnp.arange(2 * out_width, dtype=jnp.int32) // out_width
    weight_rows = merging_conv_weight.reshape(4 * in_width, out_width)
    return spread_kernel(weight_rows, pick, row_cell, col_cell, out_width, 2 * out_width)


def down_matrices(down_weight):
    nothing = jnp.zeros_like(down_weight[0, 0])
    in_width = down_weight.shape[2]
    out_width = down_weight.shape[3]

    def arrange(entries):
        return jnp.stack(
            [jnp.stack(entries[0], axis=0), jnp.stack(entries[1], axis=0)], axis=0
        ).reshape(4 * in_width, out_width)

    own_taps = arrange(
        [[down_weight[1, 1], down_weight[1, 2]], [down_weight[2, 1], down_weight[2, 2]]]
    )
    upper_taps = arrange([[nothing, nothing], [down_weight[0, 1], down_weight[0, 2]]])
    left_taps = arrange([[nothing, down_weight[1, 0]], [nothing, down_weight[2, 0]]])
    corner_taps = arrange([[nothing, nothing], [nothing, down_weight[0, 0]]])
    return (own_taps, upper_taps, left_taps, corner_taps)


def stem_layers(aerial_patch_grid, patch_conv_weight, patch_bias, merging_conv_weight, merge_bias):
    band_count = patch_conv_weight.shape[0]
    patch_matrix = patch_kernel_matrix(patch_conv_weight)
    merging_matrix = merging_kernel_matrix(merging_conv_weight)
    halves = []
    for half in range(2):
        pixels = jnp.concatenate(
            [
                aerial_patch_grid[..., band * 256 + half * 128 : band * 256 + half * 128 + 128]
                for band in range(band_count)
            ],
            axis=-1,
        )
        initial_layer = jnp.einsum(
            "zji,if->zjf", pixels, patch_matrix, preferred_element_type=jnp.float32
        )
        initial_layer = jax.nn.gelu(
            initial_layer + jnp.tile(patch_bias, 8), approximate=True
        ).astype(jnp.bfloat16)
        layer_two = jnp.einsum(
            "zji,if->zjf", initial_layer, merging_matrix, preferred_element_type=jnp.float32
        )
        halves.append(
            jax.nn.gelu(layer_two + jnp.tile(merge_bias, 2), approximate=True).astype(jnp.bfloat16)
        )
    return jnp.concatenate(halves, axis=-1)


def down_conv(stacked, down_weight, down_bias):
    own_taps, upper_taps, left_taps, corner_taps = down_matrices(down_weight)
    summed = jnp.einsum(
        "rwk,kc->crw", stacked[1:, 1:], own_taps, preferred_element_type=jnp.float32
    )
    summed = summed + jnp.einsum(
        "rwk,kc->crw", stacked[:-1, 1:], upper_taps, preferred_element_type=jnp.float32
    )
    summed = summed + jnp.einsum(
        "rwk,kc->crw", stacked[1:, :-1], left_taps, preferred_element_type=jnp.float32
    )
    summed = summed + jnp.einsum(
        "rwk,kc->crw", stacked[:-1, :-1], corner_taps, preferred_element_type=jnp.float32
    )
    return (summed + down_bias[:, None, None]).astype(jnp.bfloat16)


def layer_norm(features, norm_gain):
    values = features.astype(jnp.float32)
    mean_value = jnp.mean(values, axis=0, keepdims=True)
    centered = values - mean_value
    variance = jnp.mean(centered * centered, axis=0, keepdims=True)
    return (norm_gain[:, None, None] * centered * lax.rsqrt(variance + EPSILON)).astype(
        jnp.bfloat16
    )


def filter_columns(row_spectrum, kernel, forward_h, inverse_h):
    spectrum = jnp.einsum(
        "puqh,chqw->cpuw", forward_h, row_spectrum, preferred_element_type=jnp.float32
    ).astype(jnp.bfloat16)
    spec_real = spectrum[:, 0].astype(jnp.float32)
    spec_imag = spectrum[:, 1].astype(jnp.float32)
    filter_real = kernel[:, 0].astype(jnp.float32)
    filter_imag = kernel[:, 1].astype(jnp.float32)
    weighted = jnp.stack(
        [
            filter_real * spec_real - filter_imag * spec_imag,
            filter_real * spec_imag + filter_imag * spec_real,
        ],
        axis=1,
    ).astype(jnp.bfloat16)
    return jnp.einsum(
        "qhpu,cpuw->chqw", inverse_h, weighted, preferred_element_type=jnp.float32
    ).astype(jnp.bfloat16)


def local(
    aerial_patch_grid,
    patch_conv_weight,
    patch_bias,
    merging_conv_weight,
    merge_bias,
    down_weight,
    down_bias,
    norm_gain,
    spectral_filter,
):
    section_index = lax.axis_index("section")
    field_cols = aerial_patch_grid.shape[1]
    channels = down_weight.shape[3]
    full_rows = spectral_filter.shape[2]
    half_channels = channels // 2
    cell_half = field_cols // 2
    tile_index = lax.axis_index("tile")
    grid = jnp.pad(aerial_patch_grid, ((0, 0), (1, 0), (0, 0)))
    own_part = lax.dynamic_slice_in_dim(grid, section_index * cell_half, cell_half + 1, 1)
    image_part = jnp.concatenate([from_behind(own_part[-1:], "tile", 1), own_part], axis=0)
    layer_two = stem_layers(
        image_part, patch_conv_weight, patch_bias, merging_conv_weight, merge_bias
    )
    row_ok = (jnp.arange(layer_two.shape[0]) > 0) | (tile_index > 0)
    col_ok = (jnp.arange(layer_two.shape[1]) > 0) | (section_index > 0)
    stacked = jnp.where(row_ok[:, None, None] & col_ok[None, :, None], layer_two, 0)
    feature_half = down_conv(stacked, down_weight, down_bias)
    normed_half = layer_norm(feature_half, norm_gain)
    tiles = lax.axis_size("tile")
    group_width, tile_rows = channels // tiles, normed_half.shape[1]
    slabs, length = pad_chunks(normed_half.reshape(tiles, -1))
    filter_rows = spectral_filter.reshape(-1, field_cols)
    slabs, cos_h, sin_h, negated_h, kernel_part, cos_part, negated_part = exchange_with_tables(
        slabs, filter_rows, 0, full_rows
    )
    kernel_part = jnp.swapaxes(
        kernel_part.reshape(spectral_filter.shape[:2] + (cell_half, full_rows)), 2, 3
    )
    arrived = unpad_chunks(slabs, length)
    fields = (
        arrived.reshape(tiles, group_width, tile_rows, cell_half)
        .transpose(1, 0, 2, 3)
        .reshape(group_width, tiles * tile_rows, cell_half)
    )
    swap = [(0, 1), (1, 0)]
    other_fields = lax.ppermute(fields, "section", swap)

    forward_table = jnp.stack([cos_part, negated_part], axis=1)
    inverse_table = jnp.stack([cos_part, negated_part], axis=0)
    forward_h = jnp.stack(
        [jnp.stack([cos_h, sin_h], axis=1), jnp.stack([negated_h, cos_h], axis=1)], axis=0
    )
    inverse_h = jnp.stack(
        [jnp.stack([cos_h, negated_h], axis=1), jnp.stack([sin_h, cos_h], axis=1)], axis=0
    )
    norm_scale = 1.0 / (full_rows * field_cols)
    own_start = section_index * cell_half
    other_start = (1 - section_index) * cell_half
    frequency_rows = jnp.einsum(
        "chx,xqw->chqw",
        fields,
        lax.dynamic_slice_in_dim(forward_table, own_start, cell_half, 0),
        preferred_element_type=jnp.float32,
    ) + jnp.einsum(
        "chx,xqw->chqw",
        other_fields,
        lax.dynamic_slice_in_dim(forward_table, other_start, cell_half, 0),
        preferred_element_type=jnp.float32,
    )
    back_rows = filter_columns(
        frequency_rows.astype(jnp.bfloat16), kernel_part, forward_h, inverse_h
    )
    other_rows = lax.ppermute(back_rows, "section", swap)
    result = jnp.einsum(
        "chqw,qwv->chv",
        back_rows,
        lax.dynamic_slice_in_dim(inverse_table, own_start, cell_half, 1),
        preferred_element_type=jnp.float32,
    ) + jnp.einsum(
        "chqw,qwv->chv",
        other_rows,
        lax.dynamic_slice_in_dim(inverse_table, other_start, cell_half, 1),
        preferred_element_type=jnp.float32,
    )
    filtered_fields = (result * norm_scale).astype(jnp.bfloat16)
    outgoing = (
        filtered_fields.reshape(group_width, tiles, tile_rows, cell_half)
        .transpose(1, 0, 2, 3)
        .reshape(tiles, -1)
    )
    rows_back = exchange_chunks(outgoing, 1).reshape(channels, tile_rows, cell_half)
    summed = (feature_half.astype(jnp.float32) + rows_back.astype(jnp.float32)).astype(
        jnp.bfloat16
    )
    kept = lax.dynamic_slice_in_dim(summed, section_index * half_channels, half_channels, 0)
    sent = lax.dynamic_slice_in_dim(
        summed, (1 - section_index) * half_channels, half_channels, 0
    )
    received = lax.ppermute(sent, "section", swap)
    return jnp.where(
        section_index == 0,
        jnp.concatenate([kept, received], axis=2),
        jnp.concatenate([received, kept], axis=2),
    )


def solution(mesh):
    return jax.shard_map(
        local,
        mesh=mesh,
        in_specs=(
            P("tile", None, None),
            P(),
            P(),
            P(),
            P(),
            P(),
            P(),
            P(),
            P("tile", None, None, None),
        ),
        out_specs=P("section", "tile", None),
        check_vma=False,
    )
```
